32 devices in a mesh: section: 2 (over x), dp: 16 (over z, y, core).
Axes of the slice: x: 2, y: 2, z: 4, core: 2. Of those that a mesh axis runs over, the one named last changes fastest.
Arguments:
- block_input: float32 [2048, 1024], P('dp'), may hold values from -6 to 6
- cotangent: float32 [2048, 1024], P('dp'), may hold values from -6 to 6
- marks: int32 [2048], P('dp'), may hold values 0 or 1
- w_in: bfloat16 [2, 1024, 4096], P('section', 'dp'), may hold values from -0.1875 to 0.1875
- w_out: bfloat16 [2, 1024, 1024], P('section', 'dp'), may hold values from -0.1875 to 0.1875
- w_up: bfloat16 [2, 1024, 5632], P('section', 'dp'), may hold values from -0.1875 to 0.1875
- w_down: bfloat16 [2, 1024, 2816], P('section', 'dp'), may hold values from -0.109375 to 0.109375
- gate_weights: bfloat16 [2, 1024, 16], P('section'), may hold values from -0.1875 to 0.1875
- norm_gains: float32 [2, 2, 1024], P('section'), may hold values from 0.5 to 1.5
- conv_weights: float32 [2, 4, 3072], P('section'), may hold values from -3 to 3
- decay_log: float32 [2, 8], P('section'), may hold values from -4 to 1
- decay_bias: float32 [2, 8], P('section'), may hold values from -4 to 0
- out_gain: float32 [2, 128], P('section'), may hold values from 0.5 to 1.5
Outputs:
- layer_outputs: float32 [2, 2048, 1024], P('section', 'dp')
- input_grads: float32 [2, 2048, 1024], P('section', 'dp')
- grad_w_in: float32 [2, 1024, 4096], P('section', 'dp')
- grad_w_out: float32 [2, 1024, 1024], P('section', 'dp')
- grad_w_up: float32 [2, 1024, 5632], P('section', 'dp')
- grad_w_down: float32 [2, 1024, 2816], P('section', 'dp')
- grad_gate_weights: float32 [2, 1024, 16], P('section')
- grad_norm_gains: float32 [2, 2, 1024], P('section')
- grad_conv_weights: float32 [2, 4, 3072], P('section')
- grad_decay_log: float32 [2, 8], P('section')
- grad_decay_bias: float32 [2, 8], P('section')
- grad_out_gain: float32 [2, 128], P('section')
The draws below stay inside these ranges and needn't reach their ends.
Inputs may be any that keep to these rules, and one draw needn't show every extreme that they name: A 1 marks the first token of a sequence; the first of every 128 rows begins a sequence whatever its mark.
All inputs are finite; a program needn't handle non-finite values. No bound on the sum of `marks` on one device may be relied on, other than what follows from the above.
Results may differ from the reference program's by a relative error of at most 0.01575.
Values may be sent and summed in bfloat16 or wider, within the bound.
A program may use at most 256 MiB of HBM per device.

```python
import jax
import jax.numpy as jnp
from jax import lax

D = 1024
FF = 2816
HEADS = 8
HEAD_DIM = 128
CONV = 4
GROUP = 64
TOK_DEV = 128
TOKENS = 2048


def touch_ends(values, own_key, smallest, high):
    place = [jax.random.randint(jax.random.fold_in(own_key, axis), (), 0, length) for axis, length in enumerate(values.shape)]
    longest = values.shape.index(max(values.shape))
    beside = place[:longest] + [(place[longest] + 1) % values.shape[longest]] + place[longest + 1:]
    return values.at[tuple(place)].set(smallest).at[tuple(beside)].set(high)


def spiked(values, key, source, target, blocks, factor):
    def block_of(axis_at):
        return (jnp.arange(values.shape[axis_at]) // (values.shape[axis_at] // blocks)).reshape((-1,) + (1,) * (values.ndim - 1 - axis_at))

    near = jax.random.permutation(key, blocks)[block_of(target)]
    second = (block_of(target) + blocks // 2) % blocks
    return jnp.where((block_of(source) == near) | (block_of(source) == second), factor * values, values)


def shard_levels(own_key, shape, split, least, largest):
    loudness, own = 1.0, jax.random.fold_in(own_key, 6)
    for dim, parts in split:
        heights = jnp.exp(jax.random.uniform(jax.random.fold_in(own, dim), (parts,), jnp.float32, least / len(split), largest / len(split)))
        loudness = loudness * jnp.repeat(heights, shape[dim] // parts).reshape([-1 if axis == dim else 1 for axis in range(len(shape))])
    return loudness


def bell_draw(own_key, extent, scale, limit, shards=(), kind=jnp.bfloat16):
    drawn = jax.random.normal(own_key, extent, jnp.float32) * scale
    if len(shards) > 0:
        drawn = shard_levels(own_key, extent, shards, -0.22, 0.18) * drawn
    return jnp.clip(drawn, min=-limit, max=limit).astype(kind)


def noise_with(rng, extent, scale, most, cuts, heavy, held_as=jnp.bfloat16):
    drawn = scale * jax.random.normal(rng, extent, jnp.float32)
    if cuts:
        drawn = drawn * shard_levels(rng, extent, cuts, -0.22, 0.18)
    return jnp.clip(spiked(drawn, jax.random.fold_in(rng, 3), *heavy), -most, most).astype(held_as)


def setup_inputs(seed: int = 0) -> dict:
    key_list = jax.random.split(jax.random.key(seed), 14)
    block_input = noise_with(key_list[0], (TOKENS, D), 1.0, 6.0, ((0, 16),), (0, 1, 16, 2.0), jnp.float32)
    cotangent = noise_with(key_list[1], (TOKENS, D), 1.0, 6.0, ((0, 16),), (0, 1, 16, 2.0), jnp.float32)
    marks = touch_ends((jax.random.randint(key_list[2], (TOKENS,), 0, 48) < 1).astype(jnp.int32), jax.random.fold_in(key_list[2], 1), 0, 1)
    w_in = bell_draw(key_list[3], (2, D, 4 * D), D ** -0.5, 0.1875, ((0, 2), (1, 16)))
    w_out = bell_draw(key_list[4], (2, D, D), D ** -0.5, 0.1875, ((0, 2), (1, 16)))
    w_up = bell_draw(key_list[5], (2, D, 2 * FF), D ** -0.5, 0.1875, ((0, 2), (1, 16)))
    w_down = bell_draw(key_list[6], (2, D, FF), FF ** -0.5, 0.109375, ((0, 2), (1, 16)))
    gate_weights = bell_draw(key_list[7], (2, D, 2 * HEADS), D ** -0.5, 0.1875, ((0, 2),))
    norm_gains = jnp.clip(1.0 + 0.1 * jax.random.normal(key_list[8], (2, 2, D), jnp.float32), 0.5, 1.5)
    conv_weights = bell_draw(key_list[9], (2, CONV, 3 * D), CONV ** -0.5, 3.0, ((0, 2),), jnp.float32)
    decay_log = jnp.clip(-4.0 + 5.0 * jax.random.uniform(key_list[10], (2, HEADS), jnp.float32) ** shard_levels(key_list[10], (2, HEADS), ((0, 2),), -0.2, 0.2), -4.0, 1.0)
    decay_bias = jnp.clip(-4.0 + 4.0 * jax.random.uniform(key_list[11], (2, HEADS), jnp.float32) ** shard_levels(key_list[11], (2, HEADS), ((0, 2),), -0.2, 0.2), -4.0, 0.0)
    out_gain = jnp.clip(1.0 + 0.1 * jax.random.normal(key_list[12], (2, HEAD_DIM), jnp.float32), 0.5, 1.5)
    return dict(block_input=block_input, cotangent=cotangent, marks=marks, w_in=w_in, w_out=w_out, w_up=w_up, w_down=w_down, gate_weights=gate_weights, norm_gains=norm_gains, conv_weights=conv_weights, decay_log=decay_log, decay_bias=decay_bias, out_gain=out_gain)


epsilon = 1e-06
highest = lax.Precision.HIGHEST

def dot_rows(left, right):
    return lax.dot_general(left.astype(jnp.float32), right.astype(jnp.float32), (((1,), (1,)), ((), ())), preferred_element_type=jnp.float32)

def dot_cols(left, right):
    return lax.dot_general(left.astype(jnp.float32), right.astype(jnp.float32), (((0,), (0,)), ((), ())), preferred_element_type=jnp.float32)

def rms_scale(values, gain):
    return values * lax.rsqrt(lax.optimization_barrier(jnp.mean(values * values, axis=-1, keepdims=True)) + epsilon) * gain

def segment_ids(marks_block):
    position = jnp.arange(marks_block.shape[0])
    starts = jnp.logical_or(marks_block > 0, position == 0).astype(jnp.int32)
    return jnp.cumsum(starts).astype(jnp.int32)

def short_conv(columns, kernel, segment):
    row_count, width = columns.shape
    total = columns * kernel[CONV - 1]
    for offset in range(1, CONV):
        shifted = jnp.concatenate([jnp.zeros((offset, width), columns.dtype), columns[:row_count - offset]], axis=0)
        same = jnp.concatenate([jnp.zeros((offset,), jnp.bool_), segment[offset:] == segment[:row_count - offset]])
        total = total + jnp.where(same[:, None], shifted, 0.0) * kernel[CONV - 1 - offset]
    return jax.nn.silu(total)

def delta_rule(queries, key_rows, value_rows, beta_rows, log_decay, segment):
    row_count = queries.shape[0]
    blocks = row_count // GROUP

    def to_blocks(array):
        shaped = array.reshape((blocks, GROUP, HEADS) + array.shape[2:])
        return jnp.moveaxis(shaped, 2, 1)
    seg_blocks = segment.reshape(blocks, GROUP)
    before = jnp.concatenate([jnp.full((1,), -1, jnp.int32), seg_blocks[:-1, GROUP - 1]]).astype(jnp.int32)
    index_a = jnp.arange(GROUP)[:, None]
    index_b = jnp.arange(GROUP)[None, :]
    lower = index_a >= index_b
    strict = index_a > index_b
    identity = jnp.eye(GROUP, dtype=jnp.float32)

    def step_block(state, inputs):
        query_b, key_b, value_b, beta_b, decay_b, seg_b, prior = inputs
        cumul = jnp.cumsum(decay_b, axis=1)
        within = jnp.logical_and(seg_b[:, None] == seg_b[None, :], lower)
        spread = cumul[:, :, None] - cumul[:, None, :]
        weights_in = jnp.where(within[None], jnp.exp(jnp.minimum(spread, 0.0)), 0.0)
        carried = jnp.where((seg_b == prior)[None, :], jnp.exp(cumul), 0.0)
        key_key = jnp.einsum('hid,hjd->hij', key_b, key_b, precision=highest)
        left_side = identity + jnp.where(strict[None], weights_in, 0.0) * key_key * beta_b[:, :, None]
        state_keys = jnp.einsum('hid,hed->hie', key_b, state, precision=highest)
        right_side = beta_b[:, :, None] * (value_b - carried[:, :, None] * state_keys)
        pseudo = lax.linalg.triangular_solve(left_side, right_side, left_side=True, lower=True, unit_diagonal=True)
        query_key = jnp.einsum('hid,hjd->hij', query_b, key_b, precision=highest)
        state_query = jnp.einsum('hid,hed->hie', query_b, state, precision=highest)
        output = carried[:, :, None] * state_query + jnp.einsum('hij,hje->hie', query_key * weights_in, pseudo, precision=highest)
        tail = weights_in[:, GROUP - 1, :]
        state = carried[:, GROUP - 1][:, None, None] * state + jnp.einsum('hje,hjd->hed', pseudo * tail[:, :, None], key_b, precision=highest)
        return (state, output)
    start_state = jnp.zeros((HEADS, HEAD_DIM, HEAD_DIM), jnp.float32)
    inputs = (to_blocks(queries), to_blocks(key_rows), to_blocks(value_rows), to_blocks(beta_rows), to_blocks(log_decay), seg_blocks, before)
    _, outputs = lax.scan(step_block, start_state, inputs)
    return jnp.moveaxis(outputs, 1, 2).reshape(row_count, HEADS, HEAD_DIM)

def mixer_core(proj, gate_pre, kernel, decay_log, decay_bias, out_gain, segment):
    row_count = proj.shape[0]
    mixed_in = short_conv(proj[:, :3 * D], kernel, segment)
    heads_shape = (row_count, HEADS, HEAD_DIM)
    query_raw = mixed_in[:, :D].reshape(heads_shape)
    key_raw = mixed_in[:, D:2 * D].reshape(heads_shape)
    value_rows = mixed_in[:, 2 * D:].reshape(heads_shape)
    queries = query_raw * lax.rsqrt(lax.optimization_barrier(jnp.sum(query_raw * query_raw, axis=-1, keepdims=True)) + epsilon) * HEAD_DIM ** (-0.5)
    key_rows = key_raw * lax.rsqrt(lax.optimization_barrier(jnp.sum(key_raw * key_raw, axis=-1, keepdims=True)) + epsilon)
    beta_rows = jax.nn.sigmoid(gate_pre[:, HEADS:])
    log_decay = -jnp.exp(decay_log) * jax.nn.softplus(gate_pre[:, :HEADS] + decay_bias)
    delta_out = delta_rule(queries, key_rows, value_rows, beta_rows, log_decay, segment)
    scaled = delta_out * lax.rsqrt(lax.optimization_barrier(jnp.mean(delta_out * delta_out, axis=-1, keepdims=True)) + epsilon) * out_gain
    gate_part = proj[:, 3 * D:].reshape(heads_shape)
    return (scaled * jax.nn.silu(gate_part)).reshape(row_count, D)

def swiglu(upgate):
    return jax.nn.silu(upgate[:, :FF]) * upgate[:, FF:]

def layer_forward(w_in, w_out, w_up, w_down, gate_weights, norm_gains, kernel, decay_log, decay_bias, out_gain, block, marks_block):
    segment = segment_ids(marks_block)
    normed_a = rms_scale(block, norm_gains[0]).astype(jnp.bfloat16)
    proj = jnp.dot(normed_a.astype(jnp.float32), w_in.astype(jnp.float32), preferred_element_type=jnp.float32)
    gate_pre = jnp.dot(normed_a.astype(jnp.float32), gate_weights.astype(jnp.float32), preferred_element_type=jnp.float32)
    mixer = mixer_core(proj, gate_pre, kernel, decay_log, decay_bias, out_gain, segment).astype(jnp.bfloat16)
    middle = block + jnp.dot(mixer.astype(jnp.float32), w_out.astype(jnp.float32), preferred_element_type=jnp.float32)
    normed_f = rms_scale(middle, norm_gains[1]).astype(jnp.bfloat16)
    upgate = jnp.dot(normed_f.astype(jnp.float32), w_up.astype(jnp.float32), preferred_element_type=jnp.float32)
    hidden = swiglu(upgate).astype(jnp.bfloat16)
    result = middle + dot_rows(hidden, w_down)
    return (result, (normed_a, proj, gate_pre, mixer, middle, normed_f, upgate, hidden))

def layer_backward(w_in, w_out, w_up, w_down, gate_weights, norm_gains, kernel, decay_log, decay_bias, out_gain, block, marks_block, saved, grad_out):
    segment = segment_ids(marks_block)
    normed_a, proj, gate_pre, mixer, middle, normed_f, upgate, hidden = saved
    g_bf = grad_out.astype(jnp.bfloat16)
    d_hidden = jnp.dot(g_bf.astype(jnp.float32), w_down.astype(jnp.float32), preferred_element_type=jnp.float32)
    _, swiglu_back = jax.vjp(swiglu, upgate)
    d_upgate = swiglu_back(d_hidden)[0].astype(jnp.bfloat16)
    d_normed_f = dot_rows(d_upgate, w_up)
    _, norm_back_f = jax.vjp(rms_scale, middle, norm_gains[1])
    d_middle, gain_f = norm_back_f(d_normed_f)
    d_middle = d_middle + grad_out
    dm_bf = d_middle.astype(jnp.bfloat16)
    d_mixer = dot_rows(dm_bf, w_out)

    def core_of(proj_in, gate_in, kernel_in, log_in, bias_in, gain_in):
        return mixer_core(proj_in, gate_in, kernel_in, log_in, bias_in, gain_in, segment)
    _, core_back = jax.vjp(core_of, proj, gate_pre, kernel, decay_log, decay_bias, out_gain)
    d_proj, d_gate_pre, d_kernel, d_log, d_bias, d_gain = core_back(d_mixer)
    d_proj = d_proj.astype(jnp.bfloat16)
    d_gate_pre = d_gate_pre.astype(jnp.bfloat16)
    d_normed_a = dot_rows(d_proj, w_in) + dot_rows(d_gate_pre, gate_weights)
    _, norm_back_a = jax.vjp(rms_scale, block, norm_gains[0])
    d_block, gain_a = norm_back_a(d_normed_a)
    d_block = d_block + d_middle
    small = (dot_cols(normed_a, d_gate_pre), jnp.stack([gain_a, gain_f]), d_kernel, d_log, d_bias, d_gain)
    factors = (normed_a, d_proj, mixer, dm_bf, normed_f, d_upgate, g_bf, hidden)
    return (d_block, small, factors)

def weight_terms(factors, start, count):
    normed_a, d_proj, mixer, dm_bf, normed_f, d_upgate, g_bf, hidden = factors

    def part(left, right):
        columns = lax.dynamic_slice_in_dim(left, start, count, 1)
        return dot_cols(columns, right)
    return jnp.concatenate([part(normed_a, d_proj), part(mixer, dm_bf), part(normed_f, d_upgate), part(g_bf, hidden)], axis=1)

def reference(block_input, cotangent, marks, w_in, w_out, w_up, w_down, gate_weights, norm_gains, conv_weights, decay_log, decay_bias, out_gain):
    blocks = TOKENS // TOK_DEV
    mark_blocks = marks.reshape(blocks, TOK_DEV)

    def params_of(layer):
        return (w_in[layer], w_out[layer], w_up[layer], w_down[layer], gate_weights[layer], norm_gains[layer], conv_weights[layer], decay_log[layer], decay_bias[layer], out_gain[layer])

    def forward_layer(layer, values):
        params = params_of(layer)
        pieces = values.reshape(blocks, TOK_DEV, D)
        outputs = lax.map(lambda item: layer_forward(*params, item[0], item[1])[0], (pieces, mark_blocks))
        return outputs.reshape(TOKENS, D)

    def backward_layer(layer, values, grads):
        params = params_of(layer)

        def step_block(carry, item):
            piece, mark_piece, grad_piece = item
            _, saved = layer_forward(*params, piece, mark_piece)
            d_block, small, factors = layer_backward(*params, piece, mark_piece, saved, grad_piece)
            big = carry[0] + weight_terms(factors, 0, D)
            rest = jax.tree.map(jnp.add, carry[1], small)
            return ((big, rest), d_block)
        start_small = (jnp.zeros((D, 2 * HEADS), jnp.float32), jnp.zeros((2, D), jnp.float32), jnp.zeros((CONV, 3 * D), jnp.float32), jnp.zeros((HEADS,), jnp.float32), jnp.zeros((HEADS,), jnp.float32), jnp.zeros((HEAD_DIM,), jnp.float32))
        start = (jnp.zeros((D, 5 * D + 3 * FF), jnp.float32), start_small)
        inputs = (values.reshape(blocks, TOK_DEV, D), mark_blocks, grads.reshape(blocks, TOK_DEV, D))
        (big, small), d_blocks = lax.scan(step_block, start, inputs)
        return (d_blocks.reshape(TOKENS, D), big, small)
    first_out = forward_layer(0, block_input)
    second_out = forward_layer(1, first_out)
    second_grad, second_big, second_small = backward_layer(1, first_out, cotangent)
    first_grad, first_big, first_small = backward_layer(0, block_input, second_grad)
    bigs = jnp.stack([first_big, second_big])
    smalls = jax.tree.map(lambda a, b: jnp.stack([a, b]), first_small, second_small)
    return (jnp.stack([first_out, second_out]), jnp.stack([first_grad, second_grad]), bigs[:, :, :4 * D], bigs[:, :, 4 * D:5 * D], bigs[:, :, 5 * D:5 * D + 2 * FF], bigs[:, :, 5 * D + 2 * FF:], smalls[0], smalls[1], smalls[2], smalls[3], smalls[4], smalls[5])
```

```python
import functools

import jax
import jax.numpy as jnp
from jax import lax
from jax.experimental import pallas as pl
from jax.experimental.pallas import tpu as pltpu
from jax.sharding import PartitionSpec as P

D = 1024
FF = 2816
HEADS = 8
HEAD_DIM = 128
CONV = 4
BLOCK = 128
GROUP_HEADS = 4
LANES = 128
WIDTHS = (4 * D, D, 2 * FF, FF)
W_IN, W_OUT, W_UP, W_DOWN = range(4)
GATE_ROW, GAIN_ROW, CONV_ROW, LOG_ROW, BIAS_ROW, OUT_ROW, SMALL_ROWS = 0, 128, 144, 240, 241, 242, 243

epsilon = 1e-06
highest = lax.Precision.HIGHEST
MESH = pl.DeviceIdType.MESH
f32, bf16 = jnp.float32, jnp.bfloat16

NN = ((1,), (0,))
NT = ((1,), (1,))
TN = ((0,), (0,))


def unit_table():
    units = []
    for matrix, parts in ((W_IN, 4), (W_OUT, 2), (W_UP, 4), (W_DOWN, 2)):
        width = WIDTHS[matrix] // parts
        for k in range(parts):
            units.append((matrix, k * width, width, k % 2))
    return units


UNITS = unit_table()


def mm(left, right, dims):
    return lax.dot_general(
        left, right, (dims, ((), ())), precision=highest, preferred_element_type=f32
    )


def dot(left, right, dims=NN):
    return lax.dot_general(left, right, (dims, ((), ())), preferred_element_type=f32)


def sigmoid(x):
    return lax.logistic(x)


def softplus(x):
    return jnp.maximum(x, 0.0) + jnp.log1p(jnp.exp(-jnp.abs(x)))


def cols_at(index, width):
    return pl.ds(pl.multiple_of(index * width, width), width)


def loop(lo, hi, body):
    def step(i, carry):
        body(i)
        return carry

    lax.fori_loop(lo, hi, step, 0)


def kernel(
    dp,
    rows,
    x_in, cot, marks, sh_in, sh_out, sh_up, sh_down, gate_w, gains, taps, smalls,
    layer_out, in_grad, g_in, g_out, g_up, g_down, small_out,
    w_in, w_out, w_up, w_down,
    l_in, l_out, l_up, l_down,
    r_in, r_out, r_up, r_down,
    proj, tot, qkv, upg, xs, mid, dmid, big_a, delta_o, t_inv, pseudo,
    normed, gp, cum, cum_t, beta, mask, same, dcol, drow, dbeta,
    pass_out, pass_in, small_sum, small_land,
    local_sem, ring_recv, ring_send, sib_recv, sib_send, pair_recv, pair_send,
    pass_sem, ready_sem, small_sem,
):
    chips = dp // 2
    half = chips // 2
    sec, me = lax.axis_index("section"), lax.axis_index("dp")
    chip, core = lax.div(me, 2), lax.rem(me, 2)
    shards = (sh_in, sh_out, sh_up, sh_down)
    held = (w_in, w_out, w_up, w_down)
    left = (l_in, l_out, l_up, l_down)
    right = (r_in, r_out, r_up, r_down)
    grads = (g_in, g_out, g_up, g_down)

    turn = lax.rem(chip, 2)
    spot = (1 - turn) * lax.div(chip, 2) + turn * (chips - 1 - lax.div(chip, 2))

    def device_at(position):
        back = lax.div(position, half)
        there = (1 - back) * 2 * position + back * (2 * (chips - 1 - position) + 1)
        return 2 * there + core

    towards = (
        device_at(lax.rem(spot + 1, chips)),
        device_at(lax.rem(spot + chips - 1, chips)),
    )
    sibling = 2 * chip + 1 - core

    def rows_of(device):
        return pl.ds(pl.multiple_of(device * rows, rows), rows)

    barrier = pltpu.get_barrier_semaphore()

    def greet(offset):
        pl.semaphore_signal(
            barrier, inc=1, device_id={"dp": lax.rem(me + offset, dp)}, device_id_type=MESH
        )

    loop(1, dp, greet)
    pl.semaphore_signal(barrier, inc=1, device_id={"section": 1 - sec}, device_id_type=MESH)
    pl.semaphore_wait(barrier, dp)

    def ring_copy(unit, source, target, arrival):
        matrix, _, _, way = UNITS[unit]
        return pltpu.make_async_remote_copy(
            src_ref=source,
            dst_ref=target,
            send_sem=ring_send.at[matrix],
            recv_sem=arrival,
            device_id={"dp": towards[way]},
            device_id_type=MESH,
        )

    def to_sibling(matrix, source, target):
        return pltpu.make_async_remote_copy(
            src_ref=source,
            dst_ref=target,
            send_sem=sib_send.at[matrix],
            recv_sem=sib_recv.at[matrix],
            device_id={"dp": sibling},
            device_id_type=MESH,
        )

    def own_local(matrix):
        return pltpu.make_async_copy(
            shards[matrix], held[matrix].at[rows_of(me), :], local_sem.at[matrix]
        )

    def send_own(matrix):
        for unit, (which, start, width, way) in enumerate(UNITS):
            if which == matrix:
                part = pl.ds(start, width)
                ring_copy(
                    unit,
                    shards[matrix].at[:, part],
                    held[matrix].at[rows_of(me), part],
                    ring_recv.at[unit, 0],
                ).start()
        to_sibling(matrix, shards[matrix], held[matrix].at[rows_of(me), :]).start()
        own_local(matrix).start()

    def gather_step(matrices, step, last=False):
        for unit, (matrix, start, width, way) in enumerate(UNITS):
            if matrix not in matrices:
                continue
            if way == 0:
                origin = lax.rem(spot + 2 * chips - 1 - step, chips)
            else:
                origin = lax.rem(spot + 1 + step, chips)
            block = held[matrix].at[rows_of(device_at(origin)), pl.ds(start, width)]
            ring_copy(unit, block, block, ring_recv.at[unit, step]).wait_recv()
            if not last:
                ring_copy(unit, block, block, ring_recv.at[unit, step + 1]).start()
            to_sibling(matrix, block, block).start()

    def gather_rest(matrices, lo, hi):
        loop(lo, hi, lambda step: gather_step(matrices, step))

    def gather_end(matrices):
        for matrix in matrices:
            every = held[matrix].at[pl.ds(0, chips * rows), :]
            to_sibling(matrix, every, every).wait_recv()
            own_local(matrix).wait()

    def gather_sent(matrix):
        every = held[matrix].at[pl.ds(0, chips * rows), :]
        most = held[matrix].at[pl.ds(0, (chips - 1) * rows), :]
        to_sibling(matrix, every, every).wait_send()
        pltpu.make_async_remote_copy(
            src_ref=most,
            dst_ref=most,
            send_sem=ring_send.at[matrix],
            recv_sem=ring_recv.at[0, 0],
            device_id={"dp": towards[0]},
            device_id_type=MESH,
        ).wait_send()

    def passing():
        return pltpu.make_async_remote_copy(
            src_ref=pass_out,
            dst_ref=pass_in,
            send_sem=pass_sem.at[0],
            recv_sem=pass_sem.at[1],
            device_id={"section": 1 - sec},
            device_id_type=MESH,
        )

    final = chips - 2
    send_own(W_IN)
    gather_rest((W_IN,), 0, final - 1)
    send_own(W_OUT)
    send_own(W_UP)
    gather_rest((W_IN,), final - 1, final)
    gather_step((W_IN,), final, True)

    row = lax.broadcasted_iota(jnp.int32, (BLOCK, BLOCK), 0)
    col = lax.broadcasted_iota(jnp.int32, (BLOCK, BLOCK), 1)
    starts = jnp.logical_or(marks[...] > 0, col[:1] == 0)
    starts = jnp.where(starts, 1.0, 0.0)
    seg_col = jnp.sum(jnp.where(row >= col, starts, 0.0), axis=1, keepdims=True)
    seg_row = jnp.sum(jnp.where(row == col, seg_col, 0.0), axis=0, keepdims=True)
    within = jnp.where(jnp.logical_and(seg_col == seg_row, row >= col), 1.0, 0.0)
    mask[...] = within
    for m in range(1, CONV):
        near = jnp.sum(jnp.where(row - col == m, within, 0.0), axis=1, keepdims=True)
        same[m - 1] = jnp.broadcast_to(near, (BLOCK, LANES))
    small_sum[...] = jnp.zeros(small_sum.shape, f32)

    first_group = (W_OUT, W_UP)
    hooks = min(5, final - 1)

    @pl.when(sec == 0)
    def _():
        xs[...] = x_in[...]

    @pl.when(sec != 0)
    def _():
        gather_rest(first_group, 0, final - 1)
        send_own(W_DOWN)
        gather_rest(first_group, final - 1, final)
        gather_step(first_group, final, True)
        gather_rest((W_DOWN,), 0, final)
        gather_step((W_DOWN,), final, True)

    gather_end((W_IN,))

    @pl.when(sec != 0)
    def _():
        passing().wait_recv()
        xs[...] = pass_in[...].astype(f32)

    def hook(matrices, step):
        if step < hooks:

            @pl.when(sec == 0)
            def _():
                gather_step(matrices, step)

    def rms(source, gain_row, target, turned):
        def part(i):
            at = cols_at(i, 32)
            x = source[at, :]
            scale = lax.rsqrt(jnp.mean(x * x, axis=1, keepdims=True) + epsilon)
            target[at, :] = (x * scale * gains[gain_row : gain_row + 1, :]).astype(bf16)

        loop(0, BLOCK // 32, part)
        turn_over(target, turned)

    def turn_over(source, turned):
        def part(i):
            at = cols_at(i, 128)
            turned[at, pl.ds(0, BLOCK)] = source[:, at].astype(f32).T.astype(bf16)

        loop(0, D // 128, part)

    rms(xs, 0, normed, l_in)

    def project(j):
        at = cols_at(j, 512)
        proj[:, at] = dot(normed[...], w_in[:, at])

    loop(0, 4 * D // 512, project)
    pre = dot(normed[...], gate_w[...])
    gp[...] = pre
    beta[...] = sigmoid(pre)
    decay = -jnp.exp(smalls[0:1, :]) * softplus(pre + smalls[1:2, :])
    running = mm(jnp.where(row >= col, 1.0, 0.0), decay, NN)
    cum[...] = running
    cum_t[...] = running.T
    hook(first_group, 0)

    def conv_total(at):
        x = proj[:, at]
        total = x * taps[CONV - 1 : CONV, at]
        for m in range(1, CONV):
            total += pltpu.roll(x, m, 0) * same[m - 1] * taps[CONV - 1 - m : CONV - m, at]
        return total

    def head_parts(h):
        for part in range(3):
            at = cols_at(part * HEADS + h, HEAD_DIM)
            total = conv_total(at)
            tot[:, at] = total
            value = total * sigmoid(total)
            if part < 2:
                value = value * lax.rsqrt(jnp.sum(value * value, axis=1, keepdims=True) + epsilon)
            if part == 0:
                value = value * HEAD_DIM ** (-0.5)
            qkv[:, at] = value

    loop(0, HEADS, head_parts)
    hook(first_group, 1)

    def lane_of(array, lane):
        lanes = lax.broadcasted_iota(jnp.int32, (BLOCK, LANES), 1)
        return jnp.sum(jnp.where(lanes == lane, array, 0.0), axis=1, keepdims=True)

    def row_of(array, which):
        lines = lax.broadcasted_iota(jnp.int32, (LANES, BLOCK), 0)
        return jnp.sum(jnp.where(lines == which, array, 0.0), axis=0, keepdims=True)

    def spread(h):
        gap = lane_of(cum[...], h) - row_of(cum_t[...], h)
        return jnp.where(mask[...] > 0.0, jnp.exp(jnp.minimum(gap, 0.0)), 0.0)

    def part_at(part, h):
        return cols_at(part * HEADS + h, HEAD_DIM)

    apart = jnp.bitwise_xor(row, col)

    def delta_forward(first):
        heads = [first + i for i in range(GROUP_HEADS)]
        span = range(GROUP_HEADS)
        weights = [spread(h) for h in heads]
        betas = [lane_of(beta[...], HEADS + h) for h in heads]
        keys = [qkv[:, part_at(1, h)] for h in heads]
        below = [
            jnp.where(row > col, weights[i], 0.0) * mm(keys[i], keys[i], NT) * betas[i]
            for i in span
        ]
        inverse = [jnp.where(row == col, 1.0, 0.0) - jnp.where(apart == 1, below[i], 0.0) for i in span]
        size = 2
        while size < BLOCK:
            level = jnp.logical_and(apart >= size, apart < 2 * size)
            inner = [mm(jnp.where(level, below[i], 0.0), inverse[i], NN) for i in span]
            inverse = [inverse[i] - mm(inverse[i], inner[i], NN) for i in span]
            size *= 2
        solved = [mm(inverse[i], betas[i] * qkv[:, part_at(2, heads[i])], NN) for i in span]
        for i in span:
            at = part_at(0, heads[i])
            score = mm(qkv[:, at], keys[i], NT) * weights[i]
            delta_o[:, at] = mm(score, solved[i], NN)
            t_inv[:, at] = inverse[i]
            pseudo[:, at] = solved[i]

    for group in range(HEADS // GROUP_HEADS):
        delta_forward(group * GROUP_HEADS)
        hook(first_group, 2 + group)

    def gate_norm(h):
        at = part_at(0, h)
        out = delta_o[:, at]
        scaled = out * lax.rsqrt(jnp.mean(out * out, axis=1, keepdims=True) + epsilon) * smalls[2:3, :]
        gate = proj[:, part_at(3, h)]
        mixed = scaled * (gate * sigmoid(gate))
        normed[:, at] = mixed.astype(bf16)
        l_out[at, pl.ds(0, BLOCK)] = mixed.T.astype(bf16)

    loop(0, HEADS, gate_norm)
    hook(first_group, 4)

    @pl.when(sec == 0)
    def _():
        gather_rest(first_group, hooks, final - 1)
        send_own(W_DOWN)
        gather_rest(first_group, final - 1, final)
        gather_step(first_group, final, True)

    gather_end(first_group)

    def output_part(j):
        at = cols_at(j, 512)
        mid[:, at] = xs[:, at] + dot(normed[...], w_out[:, at])

    loop(0, D // 512, output_part)
    hook((W_DOWN,), 0)
    rms(mid, 1, normed, l_up)
    hook((W_DOWN,), 1)

    def up_part(j):
        at = cols_at(j, 512)
        upg[:, at] = dot(normed[...], w_up[:, at])

    loop(0, 2 * FF // 512, up_part)
    hook((W_DOWN,), 2)

    def hidden_part(j):
        at = cols_at(j, 256)
        first, second = upg[:, at], upg[:, cols_at(j + FF // 256, 256)]
        r_down[pl.ds(0, BLOCK), at] = (first * sigmoid(first) * second).astype(bf16)

    loop(0, FF // 256, hidden_part)

    @pl.when(sec == 0)
    def _():
        gather_rest((W_DOWN,), min(3, hooks), final)
        gather_step((W_DOWN,), final, True)

    gather_end((W_DOWN,))

    def down_part(j):
        at = cols_at(j, 256)
        total = mid[:, at] + dot(r_down[pl.ds(0, BLOCK), :], w_down[at, :], NT)
        layer_out[:, at] = total
        pass_out[:, at] = total.astype(bf16)

    loop(0, D // 256, down_part)

    @pl.when(sec == 0)
    def _():
        passing().start()

    def pair_copy(index, array, lanes):
        if lanes:
            source, target = array.at[:, pl.ds(0, BLOCK)], array.at[:, pl.ds(BLOCK, BLOCK)]
        else:
            source, target = array.at[pl.ds(0, BLOCK), :], array.at[pl.ds(BLOCK, BLOCK), :]
        return pltpu.make_async_remote_copy(
            src_ref=source,
            dst_ref=target,
            send_sem=pair_send.at[index],
            recv_sem=pair_recv.at[index],
            device_id={"dp": sibling},
            device_id_type=MESH,
        )

    def left_copy(matrix):
        return pair_copy(matrix, left[matrix], True)

    def right_copy(matrix):
        return pair_copy(4 + matrix, right[matrix], False)

    left_copy(W_IN).start()
    left_copy(W_OUT).start()
    left_copy(W_UP).start()
    right_copy(W_DOWN).start()
    for matrix in range(4):
        gather_sent(matrix)

    @pl.when(sec == 0)
    def _():
        passing().wait_send()
        passing().wait_recv()
        xs_grad = pass_in[...].astype(f32)
        dmid[...] = xs_grad

    @pl.when(sec != 0)
    def _():
        dmid[...] = cot[...]

    normed[...] = dmid[...].astype(bf16)
    turn_over(normed, l_down)
    left_copy(W_DOWN).start()

    def hidden_back(j):
        at = cols_at(j, 256)
        other = cols_at(j + FF // 256, 256)
        d_hidden = dot(normed[...], w_down[:, at])
        first, second = upg[:, at], upg[:, other]
        gate = sigmoid(first)
        r_up[pl.ds(0, BLOCK), at] = (
            d_hidden * second * gate * (1.0 + first * (1.0 - gate))
        ).astype(bf16)
        r_up[pl.ds(0, BLOCK), other] = (d_hidden * (first * gate)).astype(bf16)

    loop(0, FF // 256, hidden_back)
    right_copy(W_UP).start()

    def up_back(j):
        at = cols_at(j, 256)
        big_a[:, at] = dot(r_up[pl.ds(0, BLOCK), :], w_up[at, :], NT)

    loop(0, D // 256, up_back)

    def ready(group):
        for way in range(2):
            pl.semaphore_signal(
                ready_sem.at[group], inc=1, device_id={"dp": towards[way]}, device_id_type=MESH
            )

    ready(0)

    def rms_back(source, grad, gain_row, rest, target):
        gain = gains[gain_row : gain_row + 1, :]

        def part(i, total):
            at = cols_at(i, 32)
            x, dy = source[at, :], grad[at, :]
            scale = lax.rsqrt(jnp.mean(x * x, axis=1, keepdims=True) + epsilon)
            unit = x * scale
            dyg = dy * gain
            dx = scale * (dyg - unit * jnp.mean(dyg * unit, axis=1, keepdims=True))
            target[at, :] = dx + rest[at, :]
            return total + jnp.sum(dy * unit, axis=0, keepdims=True)

        total = lax.fori_loop(0, BLOCK // 32, part, jnp.zeros((1, D), f32))
        for j in range(D // LANES):
            line = GAIN_ROW + gain_row * (D // LANES) + j
            small_sum[line : line + 1, :] = total[:, j * LANES : (j + 1) * LANES]

    rms_back(mid, big_a, 1, dmid, dmid)
    r_out[pl.ds(0, BLOCK), :] = dmid[...].astype(bf16)
    right_copy(W_OUT).start()

    def sum_step(matrices, step, place):
        for unit, (matrix, start, width, way) in enumerate(UNITS):
            if matrix not in matrices:
                continue
            part = pl.ds(start, width)
            if way == 0:
                owner = lax.rem(spot + 2 * chips - 1 - step, chips)
            else:
                owner = lax.rem(spot + 1 + step, chips)
            own = dot(left[matrix][rows_of(device_at(owner)), :], right[matrix][:, part])
            before = pl.ds(pl.multiple_of((step + chips - 1 if place == 0 else step - 1) * rows, rows), rows)
            here = held[matrix].at[before, part]
            if place > 0:
                ring_copy(unit, here, here, ring_recv.at[unit, step - 1]).wait_recv()
                own = own + held[matrix][before, part].astype(f32)
            if place < 2:
                held[matrix][before, part] = own.astype(bf16)
                after = pl.ds(pl.multiple_of(step * rows, rows), rows)
                ring_copy(
                    unit, here, held[matrix].at[after, part], ring_recv.at[unit, step]
                ).start()
            else:
                grads[matrix][:, part] = own

    def sums_begin(matrices, group):
        for matrix in matrices:
            left_copy(matrix).wait_recv()
            right_copy(matrix).wait_recv()
        pl.semaphore_wait(ready_sem.at[group], 2)

    def sums_sent(matrices):
        for matrix in matrices:
            most = held[matrix].at[pl.ds(0, (chips - 1) * rows), :]
            pltpu.make_async_remote_copy(
                src_ref=most,
                dst_ref=most,
                send_sem=ring_send.at[matrix],
                recv_sem=ring_recv.at[0, 0],
                device_id={"dp": towards[0]},
                device_id_type=MESH,
            ).wait_send()

    group_a, group_b = (W_UP, W_DOWN), (W_IN, W_OUT)
    back_hooks = min(5, final)

    def back_hook(step):
        if step < back_hooks:

            @pl.when(sec == 0)
            def _():
                if step == 0:
                    sums_begin(group_a, 0)
                sum_step(group_a, step, min(step, 1))

    def mixer_back(j):
        at = cols_at(j, 256)
        big_a[:, at] = dot(r_out[pl.ds(0, BLOCK), :], w_out[at, :], NT)

    loop(0, D // 256, mixer_back)
    back_hook(0)

    def gate_norm_back(h):
        at = part_at(0, h)
        out = delta_o[:, at]
        scale = lax.rsqrt(jnp.mean(out * out, axis=1, keepdims=True) + epsilon)
        unit = out * scale
        gate = proj[:, part_at(3, h)]
        passed = sigmoid(gate)
        d_mixed = big_a[:, at]
        gain = smalls[2:3, :]
        d_gate = d_mixed * unit * gain * (passed * (1.0 + gate * (1.0 - passed)))
        r_in[pl.ds(0, BLOCK), part_at(3, h)] = d_gate.astype(bf16)
        d_scaled = d_mixed * (gate * passed)
        small_sum[OUT_ROW : OUT_ROW + 1, :] += jnp.sum(d_scaled * unit, axis=0, keepdims=True)
        d_unit = d_scaled * gain
        delta_o[:, at] = scale * (d_unit - unit * jnp.mean(d_unit * unit, axis=1, keepdims=True))

    loop(0, HEADS, gate_norm_back)
    back_hook(1)

    dcol[...] = jnp.zeros(dcol.shape, f32)
    drow[...] = jnp.zeros(drow.shape, f32)
    dbeta[...] = jnp.zeros(dbeta.shape, f32)
    strict = row > col

    def norm_silu_back(part, h, d_value):
        at = part_at(part, h)
        total = tot[:, at]
        passed = sigmoid(total)
        if part < 2:
            raw = total * passed
            scale = lax.rsqrt(jnp.sum(raw * raw, axis=1, keepdims=True) + epsilon)
            unit = raw * scale
            if part == 0:
                d_value = d_value * HEAD_DIM ** (-0.5)
            d_value = scale * (d_value - unit * jnp.sum(d_value * unit, axis=1, keepdims=True))
        tot[:, at] = d_value * (passed * (1.0 + total * (1.0 - passed)))

    def delta_backward(h):
        at = part_at(0, h)
        weights = spread(h)
        query, key, value = [qkv[:, part_at(part, h)] for part in range(3)]
        write = lane_of(beta[...], HEADS + h)
        solved, d_out = pseudo[:, at], delta_o[:, at]
        key_key = mm(key, key, NT)
        query_key = mm(query, key, NT)
        d_score = mm(d_out, solved, NT)
        d_pseudo = mm(query_key * weights, d_out, TN)
        d_right = mm(t_inv[:, at], d_pseudo, TN)
        d_left = jnp.where(strict, -mm(d_right, solved, NT), 0.0)
        left_key = d_left * weights
        d_write = jnp.sum(d_right * value, axis=1, keepdims=True) + jnp.sum(
            left_key * key_key, axis=1, keepdims=True
        )
        d_query_key = d_score * weights
        d_key_key = left_key * write
        norm_silu_back(0, h, mm(d_query_key, key, NN))
        norm_silu_back(
            1, h, mm(d_query_key, query, TN) + mm(d_key_key, key, NN) + mm(d_key_key, key, TN)
        )
        norm_silu_back(2, h, write * d_right)
        d_gap = d_query_key * query_key + d_key_key * key_key
        dcol[...] += jnp.where(col == h, jnp.sum(d_gap, axis=1, keepdims=True), 0.0)
        drow[...] += jnp.where(row == h, jnp.sum(d_gap, axis=0, keepdims=True), 0.0)
        dbeta[...] += jnp.where(col == HEADS + h, d_write, 0.0)

    for group in range(HEADS // GROUP_HEADS):
        for i in range(GROUP_HEADS):
            delta_backward(group * GROUP_HEADS + i)
        back_hook(2 + group)

    def conv_back(j):
        at = cols_at(j, LANES)
        d_total, x = tot[:, at], proj[:, at]
        d_proj = d_total * taps[CONV - 1 : CONV, at]
        line = CONV_ROW + (CONV - 1) * (3 * D // LANES) + j
        small_sum[pl.ds(line, 1), :] = jnp.sum(d_total * x, axis=0, keepdims=True)
        for m in range(1, CONV):
            met = d_total * same[m - 1]
            d_proj += pltpu.roll(met * taps[CONV - 1 - m : CONV - m, at], BLOCK - m, 0)
            line = CONV_ROW + (CONV - 1 - m) * (3 * D // LANES) + j
            small_sum[pl.ds(line, 1), :] = jnp.sum(met * pltpu.roll(x, m, 0), axis=0, keepdims=True)
        r_in[pl.ds(0, BLOCK), at] = d_proj.astype(bf16)

    loop(0, 3 * D // LANES, conv_back)
    right_copy(W_IN).start()

    d_running = dcol[...] - drow[...].T
    d_decay = mm(jnp.where(row <= col, 1.0, 0.0), d_running, NN)
    pre = gp[...] + smalls[1:2, :]
    rate = -jnp.exp(smalls[0:1, :])
    is_decay = col < HEADS
    d_pre = jnp.where(is_decay, d_decay * rate * sigmoid(pre), 0.0)
    small_sum[LOG_ROW : LOG_ROW + 1, :] = jnp.sum(
        jnp.where(is_decay, d_decay * rate * softplus(pre), 0.0), axis=0, keepdims=True
    )
    small_sum[BIAS_ROW : BIAS_ROW + 1, :] = jnp.sum(d_pre, axis=0, keepdims=True)
    d_gate_pre = (d_pre + dbeta[...] * beta[...] * (1.0 - beta[...])).astype(bf16)
    gate_grad = dot(l_in[:, pl.ds(0, BLOCK)], d_gate_pre).T
    for j in range(D // LANES):
        line = GATE_ROW + j * 2 * HEADS
        small_sum[line : line + 2 * HEADS, :] = gate_grad[: 2 * HEADS, j * LANES : (j + 1) * LANES]
    back_hook(4)

    def in_back(j):
        at = cols_at(j, 256)
        big_a[:, at] = dot(r_in[pl.ds(0, BLOCK), :], w_in[at, :], NT) + dot(
            d_gate_pre, gate_w[at, :], NT
        )

    loop(0, D // 256, in_back)
    ready(1)
    rms_back(xs, big_a, 0, dmid, in_grad)

    @pl.when(sec != 0)
    def _():
        pass_out[...] = in_grad[...].astype(bf16)
        passing().start()
        sums_begin(group_a, 0)
        sum_step(group_a, 0, 0)
        loop(1, chips - 1, lambda step: sum_step(group_a, step, 1))

    @pl.when(sec == 0)
    def _():
        loop(back_hooks, chips - 1, lambda step: sum_step(group_a, step, 1))

    sums_begin(group_b, 1)
    sum_step(group_b, 0, 0)
    sum_step(group_a, chips - 1, 2)

    piece = small_land.shape[1]

    def piece_rows(device):
        return pl.ds(pl.multiple_of(device * piece, piece), piece)

    def small_copy(stage, device, source, target):
        return pltpu.make_async_remote_copy(
            src_ref=source,
            dst_ref=target,
            send_sem=small_sem.at[stage, 0],
            recv_sem=small_sem.at[stage, 1],
            device_id={"dp": device},
            device_id_type=MESH,
        )

    def scatter_small(offset):
        device = lax.rem(me + offset, dp)
        small_copy(0, device, small_sum.at[piece_rows(device), :], small_land.at[me]).start()

    def spread_small(offset):
        device = lax.rem(me + offset, dp)
        small_copy(
            1, device, small_out.at[piece_rows(me), :], small_out.at[piece_rows(me), :]
        ).start()

    loop(1, dp, scatter_small)
    sum_step(group_b, 1, 1)
    small_land[me] = small_sum[piece_rows(me), :]
    others = small_land.at[pl.ds(0, dp - 1)]
    small_copy(0, sibling, others, others).wait_recv()
    small_out[piece_rows(me), :] = jnp.sum(small_land[...], axis=0)
    loop(1, dp, spread_small)
    loop(2, chips - 1, lambda step: sum_step(group_b, step, 1))
    sum_step(group_b, chips - 1, 2)

    small_copy(0, sibling, others, others).wait_send()
    spans = small_out.at[pl.ds(0, (dp - 1) * piece), :]
    small_copy(1, sibling, spans, spans).wait()
    sums_sent(group_a)
    sums_sent(group_b)
    for matrix in range(4):
        left_copy(matrix).wait_send()
        right_copy(matrix).wait_send()

    @pl.when(sec != 0)
    def _():
        passing().wait_send()


def padded(row):
    return jnp.pad(row, ((0, 0), (0, LANES - row.shape[1])))


def local(
    dp,
    block_input,
    cotangent,
    marks,
    w_in,
    w_out,
    w_up,
    w_down,
    gate_weights,
    norm_gains,
    conv_weights,
    decay_log,
    decay_bias,
    out_gain,
):
    rows = w_in.shape[1]
    chips = dp // 2
    smalls = jnp.concatenate(
        [padded(decay_log), padded(decay_bias), out_gain, jnp.zeros((5, LANES), f32)], axis=0
    )
    gate_w = jnp.pad(gate_weights[0], ((0, 0), (0, LANES - 2 * HEADS)))
    piece = 8 * -(-SMALL_ROWS // (8 * dp))
    vmem = pl.BlockSpec(memory_space=pltpu.VMEM)
    anywhere = pl.BlockSpec(memory_space=pl.ANY)

    def wide(width, kind=f32, lines=BLOCK):
        return pltpu.VMEM((lines, width), kind)

    scratch = (
        [wide(width, bf16, D) for width in WIDTHS]
        + [wide(2 * BLOCK, bf16, D) for _ in WIDTHS]
        + [wide(width, bf16, 2 * BLOCK) for width in WIDTHS]
        + [wide(4 * D), wide(3 * D), wide(3 * D), wide(2 * FF)]
        + [wide(D) for _ in range(7)]
        + [wide(D, bf16)]
        + [wide(LANES) for _ in range(5)]
        + [pltpu.VMEM((CONV - 1, BLOCK, LANES), f32)]
        + [wide(LANES) for _ in range(3)]
        + [wide(D, bf16), wide(D, bf16)]
        + [wide(LANES, f32, dp * piece), pltpu.VMEM((dp, piece, LANES), f32)]
        + [
            pltpu.SemaphoreType.DMA((4,)),
            pltpu.SemaphoreType.DMA((len(UNITS), chips - 1)),
            pltpu.SemaphoreType.DMA((4,)),
            pltpu.SemaphoreType.DMA((4,)),
            pltpu.SemaphoreType.DMA((4,)),
            pltpu.SemaphoreType.DMA((8,)),
            pltpu.SemaphoreType.DMA((8,)),
            pltpu.SemaphoreType.DMA((2,)),
            pltpu.SemaphoreType.REGULAR((2,)),
            pltpu.SemaphoreType.DMA((2, 2)),
        ]
    )
    layer_out, in_grad, g_in, g_out, g_up, g_down, small = pl.pallas_call(
        functools.partial(kernel, dp, rows),
        out_shape=[jax.ShapeDtypeStruct((BLOCK, D), f32)] * 2
        + [jax.ShapeDtypeStruct((rows, width), f32) for width in WIDTHS]
        + [jax.ShapeDtypeStruct((dp * piece, LANES), f32)],
        in_specs=[vmem] * 3 + [anywhere] * 4 + [vmem] * 4,
        out_specs=[vmem] * 7,
        scratch_shapes=scratch,
        compiler_params=pltpu.CompilerParams(
            collective_id=0, has_side_effects=True, vmem_limit_bytes=63 * 2**20
        ),
        cost_estimate=pl.CostEstimate(
            flops=6 * BLOCK * D * sum(WIDTHS), bytes_accessed=8 * rows * sum(WIDTHS), transcendentals=0
        ),
    )(
        block_input, cotangent, marks[None, :], w_in[0], w_out[0], w_up[0], w_down[0],
        gate_w, norm_gains[0], conv_weights[0], smalls,
    )
    gate_grad = small[GATE_ROW : GATE_ROW + 128].reshape(D // LANES, 2 * HEADS, LANES)
    rest = (
        gate_grad.transpose(0, 2, 1).reshape(D, 2 * HEADS),
        small[GAIN_ROW:CONV_ROW].reshape(2, D),
        small[CONV_ROW:LOG_ROW].reshape(CONV, 3 * D),
        small[LOG_ROW, :HEADS],
        small[BIAS_ROW, :HEADS],
        small[OUT_ROW],
    )
    return tuple(part[None] for part in (layer_out, in_grad, g_in, g_out, g_up, g_down, *rest))


def solution(mesh):
    sharded, whole, flat = P("section", "dp", None), P("section", None, None), P("section", None)
    return jax.shard_map(
        functools.partial(local, mesh.shape["dp"]),
        mesh=mesh,
        in_specs=(P("dp", None), P("dp", None), P("dp")) + (sharded,) * 4 + (whole,) * 3 + (flat,) * 3,
        out_specs=(sharded,) * 6 + (whole,) * 3 + (flat,) * 3,
        check_vma=False,
    )
```

```python
import functools

import jax
import jax.numpy as jnp
from jax import lax
from jax.experimental import pallas as pl
from jax.experimental.pallas import tpu as pltpu
from jax.sharding import PartitionSpec as P

D = 1024
FF = 2816
HEADS = 8
HEAD_DIM = 128
CONV = 4
BLOCK = 128
LANES = 128
WIDTHS = (4 * D, D, 2 * FF, FF)
HALVES = tuple(width // 2 for width in WIDTHS)
OWN_HEADS = HEADS // 2
HALF = D // 2
W_IN, W_OUT, W_UP, W_DOWN = range(4)
GATE_ROW, GAIN_ROW, CONV_ROW, LOG_ROW, BIAS_ROW, OUT_ROW, SMALL_ROWS = 0, 128, 144, 240, 241, 242, 243

epsilon = 1e-06
highest = lax.Precision.HIGHEST
MESH = pl.DeviceIdType.MESH
f32, bf16 = jnp.float32, jnp.bfloat16

NN = ((1,), (0,))
NT = ((1,), (1,))
TN = ((0,), (0,))


def unit_table():
    units = []
    for part in range(4):
        units.append((W_IN, part * HALVES[W_OUT], HALVES[W_OUT], part % 2, part * D, D // 2))
    for part in range(2):
        width = HALVES[W_OUT] // 2
        units.append((W_OUT, part * width, width, part, part * width, D // 2))
    low = LANES * -(-FF // (4 * LANES))
    for part in range(2):
        for k, (start, width) in enumerate(((0, low), (low, FF // 2 - low))):
            units.append(
                (W_UP, part * (FF // 2) + start, width, (part + k) % 2, part * FF + start, FF // 2)
            )
    for k, (start, width) in enumerate(((0, low), (low, FF // 2 - low))):
        units.append((W_DOWN, start, width, k, start, FF // 2))
    return units


UNITS = unit_table()


def mm(left, right, dims):
    return lax.dot_general(
        left, right, (dims, ((), ())), precision=highest, preferred_element_type=f32
    )


def dot(left, right, dims=NN):
    return lax.dot_general(left, right, (dims, ((), ())), preferred_element_type=f32)


def sigmoid(x):
    return lax.logistic(x)


def softplus(x):
    return jnp.maximum(x, 0.0) + jnp.log1p(jnp.exp(-jnp.abs(x)))


def cols_at(index, width):
    return pl.ds(pl.multiple_of(index * width, width), width)


def loop(lo, hi, body):
    def step(i, carry):
        body(i)
        return carry

    lax.fori_loop(lo, hi, step, 0)


def kernel(
    dp,
    rows,
    x_in, cot, marks, sh_in, sh_out, sh_up, sh_down, gate_in, gains_in, taps_in, smalls_in,
    layer_out, in_grad, g_in, g_out, g_up, g_down, small_out,
    w_in, w_out, w_up, w_down,
    l_in, l_out, l_up, l_down,
    r_in, r_out, r_up, r_down,
    proj, tot, qkv, upg, delta_o, t_inv, pseudo,
    mids, xs, big_x, dmid, big_a, normed,
    gp, cum, cum_t, beta, mask, same, dcol, drow, dbeta,
    gate_w, gains, taps, smalls,
    swap_out, swap_in, small_sum, small_mate, small_land,
    own_sem, own_send, ring_recv, ring_send, sib_recv, sib_send, pair_recv, pair_send,
    swap_recv, swap_send, ready_sem, small_sem, param_recv, param_send, last_recv, last_send, mate_sem,
):
    chips = dp // 2
    half = chips // 2
    sec, me = lax.axis_index("section"), lax.axis_index("dp")
    chip, core = lax.div(me, 2), lax.rem(me, 2)
    shards = (sh_in, sh_out, sh_up, sh_down)
    held = (w_in, w_out, w_up, w_down)
    left = (l_in, l_out, l_up, l_down)
    right = (r_in, r_out, r_up, r_down)
    grads = (g_in, g_out, g_up, g_down)
    mate = {"section": 1 - sec}

    turn = lax.rem(chip, 2)
    spot = (1 - turn) * lax.div(chip, 2) + turn * (chips - 1 - lax.div(chip, 2))

    def device_at(position):
        back = lax.div(position, half)
        there = (1 - back) * 2 * position + back * (2 * (chips - 1 - position) + 1)
        return 2 * there + core

    towards = (
        device_at(lax.rem(spot + 1, chips)),
        device_at(lax.rem(spot + chips - 1, chips)),
    )
    sibling = 2 * chip + 1 - core

    def rows_of(device):
        return pl.ds(pl.multiple_of(device * rows, rows), rows)

    def remote(source, target, sent, arrival, device):
        return pltpu.make_async_remote_copy(
            src_ref=source,
            dst_ref=target,
            send_sem=sent,
            recv_sem=arrival,
            device_id=device,
            device_id_type=MESH,
        )

    def whole_cols(unit, section):
        _, _, width, _, base, span = UNITS[unit]
        return pl.ds(pl.multiple_of(base + section * span, LANES), width)

    barrier = pltpu.get_barrier_semaphore()

    def greet(offset):
        pl.semaphore_signal(
            barrier, inc=1, device_id={"dp": lax.rem(me + offset, dp)}, device_id_type=MESH
        )

    loop(1, dp, greet)
    pl.semaphore_signal(barrier, inc=1, device_id=mate, device_id_type=MESH)
    pl.semaphore_wait(barrier, dp)

    def own_part(layer, unit):
        matrix, start, width = UNITS[unit][:3]
        return held[matrix].at[layer, rows_of(me), pl.ds(start, width)]

    for layer in range(2):

        @pl.when(sec == layer)
        def _(layer=layer):
            for unit in range(len(UNITS)):
                matrix = UNITS[unit][0]
                remote(
                    shards[matrix].at[:, whole_cols(unit, 1 - layer)],
                    own_part(layer, unit),
                    own_send.at[matrix],
                    own_sem.at[layer, unit],
                    mate,
                ).start()
                pltpu.make_async_copy(
                    shards[matrix].at[:, whole_cols(unit, layer)],
                    own_part(layer, unit),
                    own_sem.at[layer, unit],
                ).start()

    small_inputs = ((gate_in, gate_w), (gains_in, gains), (taps_in, taps), (smalls_in, smalls))

    def param_copy(index):
        source, target = small_inputs[index]
        lines = pl.ds(0, source.shape[0])
        return remote(
            source, target.at[sec, lines], param_send.at[index], param_recv.at[index], mate
        )

    for index, (source, target) in enumerate(small_inputs):
        param_copy(index).start()
        target[sec, 0 : source.shape[0], :] = source[...]
    for layer in range(2):
        gate_w[layer, 2 * HEADS :, :] = jnp.zeros((LANES - 2 * HEADS, D), bf16)

    def ring_copy(layer, unit, source, target, step):
        matrix, way = UNITS[unit][0], UNITS[unit][3]
        return remote(
            source, target, ring_send.at[layer, matrix], ring_recv.at[layer, unit, step], {"dp": towards[way]}
        )

    def to_sibling(layer, matrix, source, target):
        return remote(
            source, target, sib_send.at[layer, matrix], sib_recv.at[layer, matrix], {"dp": sibling}
        )

    def origin(way, step):
        if way == 0:
            return lax.rem(spot + 2 * chips - 1 - step, chips)
        return lax.rem(spot + 1 + step, chips)

    def units_of(matrices):
        return [(unit, *entry[:4]) for unit, entry in enumerate(UNITS) if entry[0] in matrices]

    def send_own(layer, matrices):
        for unit, matrix, start, width, way in units_of(matrices):
            block = own_part(layer, unit)
            pltpu.make_async_copy(block, block, own_sem.at[layer, unit]).wait()
            ring_copy(layer, unit, block, block, 0).start()
            to_sibling(layer, matrix, block, block).start()

    def gather_step(layer, matrices, step, last=False):
        for unit, matrix, start, width, way in units_of(matrices):
            device = device_at(origin(way, step))
            block = held[matrix].at[layer, rows_of(device), pl.ds(start, width)]
            ring_copy(layer, unit, block, block, step).wait_recv()
            if not last:
                ring_copy(layer, unit, block, block, step + 1).start()
            to_sibling(layer, matrix, block, block).start()

    def gather_rest(layer, matrices, lo, hi):
        if lo < hi:
            loop(lo, hi, lambda step: gather_step(layer, matrices, step))

    def gather_end(layer, matrices):
        for matrix in matrices:
            every = held[matrix].at[layer, pl.ds(0, chips * rows), :]
            to_sibling(layer, matrix, every, every).wait_recv()

    def gather_sent(layer, matrix):
        every = held[matrix].at[layer, pl.ds(0, chips * rows), :]
        to_sibling(layer, matrix, every, every).wait_send()
        ring_sent(layer, matrix)

    def ring_sent(layer, matrix):
        most = held[matrix].at[layer, pl.ds(0, (chips - 1) * rows), :]
        remote(
            most, most, ring_send.at[layer, matrix], ring_recv.at[layer, 0, 0], {"dp": towards[0]}
        ).wait_send()

    final = chips - 2
    MIX, FFN = (W_IN, W_OUT), (W_UP, W_DOWN)
    stages = ((0, MIX), (0, FFN), (1, MIX), (1, FFN))

    def advance(stage, lo, hi):
        if stage >= len(stages):
            return
        layer, matrices = stages[stage]
        hi = min(hi, final + 1)
        gather_rest(layer, matrices, lo, min(hi, final - 1))
        if lo <= final - 1 < hi:
            if stage + 1 < len(stages):
                send_own(*stages[stage + 1])
            gather_step(layer, matrices, final - 1)
        if lo <= final < hi:
            gather_step(layer, matrices, final, True)

    row = lax.broadcasted_iota(jnp.int32, (BLOCK, BLOCK), 0)
    col = lax.broadcasted_iota(jnp.int32, (BLOCK, BLOCK), 1)
    starts = jnp.logical_or(marks[...] > 0, col[:1] == 0)
    starts = jnp.where(starts, 1.0, 0.0)
    seg_col = jnp.sum(jnp.where(row >= col, starts, 0.0), axis=1, keepdims=True)
    seg_row = jnp.sum(jnp.where(row == col, seg_col, 0.0), axis=0, keepdims=True)
    within = jnp.where(jnp.logical_and(seg_col == seg_row, row >= col), 1.0, 0.0)
    mask[...] = within
    for m in range(1, CONV):
        near = jnp.sum(jnp.where(row - col == m, within, 0.0), axis=1, keepdims=True)
        same[m - 1] = jnp.broadcast_to(near, (BLOCK, LANES))
    small_sum[...] = jnp.zeros(small_sum.shape, f32)

    send_own(0, MIX)
    advance(0, 0, final + 1)
    for index in range(len(small_inputs)):
        param_copy(index).wait()

    swaps = [0]

    def swap_begin(width):
        slot = swaps[0] % 2
        swaps[0] += 1
        part = pl.ds(0, width)
        remote(
            swap_out.at[slot, :, part], swap_in.at[slot, :, part],
            swap_send.at[slot], swap_recv.at[slot], mate,
        ).start()

    def swap_slot():
        return swaps[0] % 2

    def swap_end(width):
        slot = (swaps[0] - 1) % 2
        part = pl.ds(0, width)
        remote(
            swap_out.at[slot, :, part], swap_in.at[slot, :, part],
            swap_send.at[slot], swap_recv.at[slot], mate,
        ).wait()
        return slot

    def left_copy(layer, matrix):
        array = left[matrix]
        return remote(
            array.at[layer, :, pl.ds(0, BLOCK)], array.at[layer, :, pl.ds(BLOCK, BLOCK)],
            pair_send.at[layer, matrix], pair_recv.at[layer, matrix], {"dp": sibling},
        )

    def right_copy(layer, matrix):
        array = right[matrix]
        return remote(
            array.at[layer, pl.ds(0, BLOCK), :], array.at[layer, pl.ds(BLOCK, BLOCK), :],
            pair_send.at[layer, 4 + matrix], pair_recv.at[layer, 4 + matrix], {"dp": sibling},
        )

    own_half = pl.ds(pl.multiple_of(sec * HALF, HALF), HALF)
    other_half = pl.ds(pl.multiple_of((1 - sec) * HALF, HALF), HALF)
    mine = pl.ds(0, BLOCK)

    def lane_of(array, lane):
        return jnp.sum(jnp.where(col == lane, array, 0.0), axis=1, keepdims=True)

    def row_of(array, which):
        return jnp.sum(jnp.where(row == which, array, 0.0), axis=0, keepdims=True)

    def part_at(part, i):
        return cols_at(part * OWN_HEADS + i, HEAD_DIM)

    def tap_cols(part, i):
        return cols_at(part * HEADS + sec * OWN_HEADS + i, HEAD_DIM)

    def turn_over(source, layer, turned):
        def part(i):
            at = cols_at(i, 128)
            turned[layer, at, mine] = source[:, at].astype(f32).T.astype(bf16)

        loop(0, D // 128, part)

    def rms(source, layer, gain_row, turned):
        def part(i):
            at = cols_at(i, 32)
            x = source[at, :]
            scale = lax.rsqrt(jnp.mean(x * x, axis=1, keepdims=True) + epsilon)
            normed[at, :] = (x * scale * gains[layer, gain_row : gain_row + 1, :]).astype(bf16)

        loop(0, BLOCK // 32, part)
        turn_over(normed, layer, turned)

    def spread(layer, i):
        h = sec * OWN_HEADS + i
        gap = lane_of(cum[layer], h) - row_of(cum_t[layer], h)
        return jnp.where(mask[...] > 0.0, jnp.exp(jnp.minimum(gap, 0.0)), 0.0)

    apart = jnp.bitwise_xor(row, col)

    def delta_forward(layer):
        span = range(OWN_HEADS)
        weights = [spread(layer, i) for i in span]
        betas = [lane_of(beta[layer], HEADS + sec * OWN_HEADS + i) for i in span]
        keys = [qkv[layer, :, part_at(1, i)] for i in span]
        below = [
            jnp.where(row > col, weights[i], 0.0) * mm(keys[i], keys[i], NT) * betas[i]
            for i in span
        ]
        inverse = [jnp.where(row == col, 1.0, 0.0) - jnp.where(apart == 1, below[i], 0.0) for i in span]
        size = 2
        while size < BLOCK:
            level = jnp.logical_and(apart >= size, apart < 2 * size)
            inner = [mm(jnp.where(level, below[i], 0.0), inverse[i], NN) for i in span]
            inverse = [inverse[i] - mm(inverse[i], inner[i], NN) for i in span]
            size *= 2
        solved = [mm(inverse[i], betas[i] * qkv[layer, :, part_at(2, i)], NN) for i in span]
        for i in span:
            at = part_at(0, i)
            score = mm(qkv[layer, :, at], keys[i], NT) * weights[i]
            delta_o[layer, :, at] = mm(score, solved[i], NN)
            t_inv[layer, :, at] = inverse[i]
            pseudo[layer, :, at] = solved[i]

    def forward(layer, source):
        stage = 2 * layer + 1
        rms(source, layer, 0, l_in)
        gather_end(layer, MIX)

        def project(j):
            at = cols_at(j, 512)
            proj[layer, :, at] = dot(normed[...], w_in[layer, :, at])

        loop(0, HALVES[W_IN] // 512, project)
        pre = dot(normed[...], gate_w[layer], NT)
        gp[layer] = pre
        beta[layer] = sigmoid(pre)
        decay = -jnp.exp(smalls[layer, 0:1, :]) * softplus(pre + smalls[layer, 1:2, :])
        running = mm(jnp.where(row >= col, 1.0, 0.0), decay, NN)
        cum[layer] = running
        cum_t[layer] = running.T
        left_copy(layer, W_IN).start()
        advance(stage, 0, 1)

        def head_parts(i):
            for part in range(3):
                at, tap = part_at(part, i), tap_cols(part, i)
                x = proj[layer, :, at]
                total = x * taps[layer, CONV - 1 : CONV, tap]
                for m in range(1, CONV):
                    total += pltpu.roll(x, m, 0) * same[m - 1] * taps[layer, CONV - 1 - m : CONV - m, tap]
                tot[layer, :, at] = total
                value = total * sigmoid(total)
                if part < 2:
                    value = value * lax.rsqrt(jnp.sum(value * value, axis=1, keepdims=True) + epsilon)
                if part == 0:
                    value = value * HEAD_DIM ** (-0.5)
                qkv[layer, :, at] = value

        loop(0, OWN_HEADS, head_parts)
        advance(stage, 1, 2)
        delta_forward(layer)
        slot = swap_slot()

        def gate_norm(i):
            at = part_at(0, i)
            out = delta_o[layer, :, at]
            scale = lax.rsqrt(jnp.mean(out * out, axis=1, keepdims=True) + epsilon)
            gate = proj[layer, :, part_at(3, i)]
            mixed = out * scale * smalls[layer, 2:3, :] * (gate * sigmoid(gate))
            swap_out[slot, :, at] = mixed.astype(bf16)

        loop(0, OWN_HEADS, gate_norm)
        swap_begin(HALF)
        normed[:, own_half] = swap_out[slot, :, pl.ds(0, HALF)]
        advance(stage, 2, 4)
        swap_end(HALF)
        normed[:, other_half] = swap_in[slot, :, pl.ds(0, HALF)]
        total = dot(normed[...], w_out[layer])
        slot = swap_slot()
        swap_out[slot, :, pl.ds(0, HALF)] = total.astype(bf16)
        swap_begin(HALF)
        mids[layer, :, own_half] = source[:, own_half] + total
        turn_over(normed, layer, l_out)
        left_copy(layer, W_OUT).start()
        advance(stage, 4, 6)
        swap_end(HALF)
        mids[layer, :, other_half] = source[:, other_half] + swap_in[slot, :, pl.ds(0, HALF)].astype(f32)
        rms(mids.at[layer], layer, 1, l_up)
        left_copy(layer, W_UP).start()
        advance(stage, 6, final + 1)
        gather_end(layer, FFN)

        def up_part(j):
            at = cols_at(j, 256)
            upg[layer, :, at] = dot(normed[...], w_up[layer, :, at])

        loop(0, FF // 256, up_part)
        advance(stage + 1, 0, 1)

        def hidden_part(j):
            at = cols_at(j, LANES)
            first, second = upg[layer, :, at], upg[layer, :, cols_at(j + FF // 2 // LANES, LANES)]
            r_down[layer, mine, at] = (first * sigmoid(first) * second).astype(bf16)

        loop(0, FF // 2 // LANES, hidden_part)
        right_copy(layer, W_DOWN).start()
        slot = swap_slot()

        def down_part(j):
            at = cols_at(j, 256)
            part = dot(r_down[layer, mine, :], w_down[layer, at, :], NT)
            big_a[:, at] = part
            swap_out[slot, :, at] = part.astype(bf16)

        loop(0, D // 256, down_part)
        swap_begin(D)
        advance(stage + 1, 1, 3)
        swap_end(D)
        xs[...] = mids[layer] + (big_a[...] + swap_in[slot].astype(f32))

        @pl.when(sec == layer)
        def _():
            layer_out[...] = xs[...]

        advance(stage + 1, 3, final + 1)

    def ready(group):
        for device in ({"dp": towards[0]}, {"dp": towards[1]}, mate):
            pl.semaphore_signal(ready_sem.at[group], inc=1, device_id=device, device_id_type=MESH)

    def slot_rows(index):
        return pl.ds(pl.multiple_of(index * rows, rows), rows)

    def sum_step(layer, matrices, step, place):
        for unit, matrix, start, width, way in units_of(matrices):
            part = pl.ds(start, width)
            owner = device_at(origin(way, step))
            own = dot(left[matrix][layer, rows_of(owner), :], right[matrix][layer, :, part])
            before = slot_rows(chips - 1 if place == 0 else step - 1)
            here = held[matrix].at[layer, before, part]
            if place > 0:
                ring_copy(layer, unit, here, here, step - 1).wait_recv()
                own = own + held[matrix][layer, before, part].astype(f32)
            if place < 2:
                held[matrix][layer, before, part] = own.astype(bf16)
                ring_copy(
                    layer, unit, here, held[matrix].at[layer, slot_rows(step), part], step
                ).start()
            else:

                @pl.when(sec == layer)
                def _():
                    grads[matrix][:, whole_cols(unit, layer)] = own

                @pl.when(sec != layer)
                def _():
                    held[matrix][layer, slot_rows(chips), part] = own.astype(bf16)
                    last = held[matrix].at[layer, slot_rows(chips), part]
                    remote(last, last, last_send.at[matrix], last_recv.at[unit], mate).start()

    sums = ((1, FFN), (1, MIX), (0, FFN), (0, MIX))

    def add_up(group, lo, hi):
        if group < 0:
            return
        layer, matrices = sums[group]
        hi = min(hi, chips)
        if lo == 0:
            for matrix in matrices:
                left_copy(layer, matrix).wait_recv()
                right_copy(layer, matrix).wait_recv()
            pl.semaphore_wait(ready_sem.at[group], 3)
            sum_step(layer, matrices, 0, 0)
        first, stop = max(lo, 1), min(hi, chips - 1)
        if stop - first == 1:
            sum_step(layer, matrices, first, 1)
        elif first < stop:
            loop(first, stop, lambda step: sum_step(layer, matrices, step, 1))
        if hi == chips:
            sum_step(layer, matrices, chips - 1, 2)

    def rms_back(source, layer, gain_row, rest, target, slot):
        gain = gains[layer, gain_row : gain_row + 1, :]

        def part(i, total):
            at = cols_at(i, 32)
            x, dy = source[at, :], big_a[at, :] + swap_in[slot, at, :].astype(f32)
            scale = lax.rsqrt(jnp.mean(x * x, axis=1, keepdims=True) + epsilon)
            unit = x * scale
            dyg = dy * gain
            dx = scale * (dyg - unit * jnp.mean(dyg * unit, axis=1, keepdims=True))
            target[at, :] = dx + rest[at, :]
            return total + jnp.sum(dy * unit, axis=0, keepdims=True)

        total = lax.fori_loop(0, BLOCK // 32, part, jnp.zeros((1, D), f32))

        @pl.when(sec == layer)
        def _():
            for j in range(D // LANES):
                line = GAIN_ROW + gain_row * (D // LANES) + j
                small_sum[layer, line : line + 1, :] = total[:, j * LANES : (j + 1) * LANES]

    strict = row > col

    def backward(layer, source, before):
        group = before + 1
        normed[...] = dmid[...].astype(bf16)
        turn_over(normed, layer, l_down)
        left_copy(layer, W_DOWN).start()

        def hidden_back(j):
            at = cols_at(j, LANES)
            other = cols_at(j + FF // 2 // LANES, LANES)
            d_hidden = dot(normed[...], w_down[layer, :, at])
            first, second = upg[layer, :, at], upg[layer, :, other]
            gate = sigmoid(first)
            r_up[layer, mine, at] = (
                d_hidden * second * gate * (1.0 + first * (1.0 - gate))
            ).astype(bf16)
            r_up[layer, mine, other] = (d_hidden * (first * gate)).astype(bf16)

        loop(0, FF // 2 // LANES, hidden_back)
        right_copy(layer, W_UP).start()
        slot = swap_slot()

        def up_back(j):
            at = cols_at(j, 256)
            part = dot(r_up[layer, mine, :], w_up[layer, at, :], NT)
            big_a[:, at] = part
            swap_out[slot, :, at] = part.astype(bf16)

        loop(0, D // 256, up_back)
        swap_begin(D)
        ready(group)
        add_up(before, 3, chips)
        add_up(group, 0, 1)
        swap_end(D)
        rms_back(mids.at[layer], layer, 1, dmid, dmid, slot)
        r_out[layer, mine, :] = dmid[:, own_half].astype(bf16)
        right_copy(layer, W_OUT).start()
        slot = swap_slot()

        def mixer_back(j):
            at = cols_at(j, 256)
            theirs = pl.ds(pl.multiple_of((1 - sec) * HALF + j * 256, 256), 256)
            swap_out[slot, :, at] = dot(r_out[layer, mine, :], w_out[layer, theirs, :], NT).astype(bf16)

        loop(0, HALF // 256, mixer_back)
        swap_begin(HALF)

        def mixer_own(j):
            at = cols_at(j, 256)
            ours = pl.ds(pl.multiple_of(sec * HALF + j * 256, 256), 256)
            big_a[:, at] = dot(r_out[layer, mine, :], w_out[layer, ours, :], NT)

        loop(0, HALF // 256, mixer_own)
        add_up(group, 1, 2)
        swap_end(HALF)

        def gate_norm_back(i):
            at = part_at(0, i)
            out = delta_o[layer, :, at]
            scale = lax.rsqrt(jnp.mean(out * out, axis=1, keepdims=True) + epsilon)
            unit = out * scale
            gate = proj[layer, :, part_at(3, i)]
            passed = sigmoid(gate)
            d_mixed = big_a[:, at] + swap_in[slot, :, at].astype(f32)
            gain = smalls[layer, 2:3, :]
            d_gate = d_mixed * unit * gain * (passed * (1.0 + gate * (1.0 - passed)))
            r_in[layer, mine, part_at(3, i)] = d_gate.astype(bf16)
            d_scaled = d_mixed * (gate * passed)
            small_sum[layer, OUT_ROW : OUT_ROW + 1, :] += jnp.sum(d_scaled * unit, axis=0, keepdims=True)
            d_unit = d_scaled * gain
            delta_o[layer, :, at] = scale * (d_unit - unit * jnp.mean(d_unit * unit, axis=1, keepdims=True))

        loop(0, OWN_HEADS, gate_norm_back)
        add_up(group, 2, 3)

        dcol[...] = jnp.zeros(dcol.shape, f32)
        drow[...] = jnp.zeros(drow.shape, f32)
        dbeta[...] = jnp.zeros(dbeta.shape, f32)

        def norm_silu_back(part, i, d_value):
            at = part_at(part, i)
            total = tot[layer, :, at]
            passed = sigmoid(total)
            if part < 2:
                raw = total * passed
                scale = lax.rsqrt(jnp.sum(raw * raw, axis=1, keepdims=True) + epsilon)
                unit = raw * scale
                if part == 0:
                    d_value = d_value * HEAD_DIM ** (-0.5)
                d_value = scale * (d_value - unit * jnp.sum(d_value * unit, axis=1, keepdims=True))
            tot[layer, :, at] = d_value * (passed * (1.0 + total * (1.0 - passed)))

        def delta_backward(i):
            h = sec * OWN_HEADS + i
            at = part_at(0, i)
            weights = spread(layer, i)
            query, key, value = [qkv[layer, :, part_at(part, i)] for part in range(3)]
            write = lane_of(beta[layer], HEADS + h)
            solved, d_out = pseudo[layer, :, at], delta_o[layer, :, at]
            key_key = mm(key, key, NT)
            query_key = mm(query, key, NT)
            d_score = mm(d_out, solved, NT)
            d_pseudo = mm(query_key * weights, d_out, TN)
            d_right = mm(t_inv[layer, :, at], d_pseudo, TN)
            d_left = jnp.where(strict, -mm(d_right, solved, NT), 0.0)
            left_key = d_left * weights
            d_write = jnp.sum(d_right * value, axis=1, keepdims=True) + jnp.sum(
                left_key * key_key, axis=1, keepdims=True
            )
            d_query_key = d_score * weights
            d_key_key = left_key * write
            norm_silu_back(0, i, mm(d_query_key, key, NN))
            norm_silu_back(
                1, i, mm(d_query_key, query, TN) + mm(d_key_key, key, NN) + mm(d_key_key, key, TN)
            )
            norm_silu_back(2, i, write * d_right)
            d_gap = d_query_key * query_key + d_key_key * key_key
            dcol[...] += jnp.where(col == h, jnp.sum(d_gap, axis=1, keepdims=True), 0.0)
            drow[...] += jnp.where(row == h, jnp.sum(d_gap, axis=0, keepdims=True), 0.0)
            dbeta[...] += jnp.where(col == HEADS + h, d_write, 0.0)

        for i in range(OWN_HEADS):
            delta_backward(i)
        add_up(group, 3, 4)

        def conv_back(i):
            for part in range(3):
                at, tap = part_at(part, i), tap_cols(part, i)
                d_total, x = tot[layer, :, at], proj[layer, :, at]
                d_proj = d_total * taps[layer, CONV - 1 : CONV, tap]
                line = CONV_ROW + part * HEADS + sec * OWN_HEADS + i
                tiles = 3 * D // LANES
                small_sum[layer, pl.ds(line + (CONV - 1) * tiles, 1), :] = jnp.sum(
                    d_total * x, axis=0, keepdims=True
                )
                for m in range(1, CONV):
                    met = d_total * same[m - 1]
                    weight = taps[layer, CONV - 1 - m : CONV - m, tap]
                    d_proj += pltpu.roll(met * weight, BLOCK - m, 0)
                    small_sum[layer, pl.ds(line + (CONV - 1 - m) * tiles, 1), :] = jnp.sum(
                        met * pltpu.roll(x, m, 0), axis=0, keepdims=True
                    )
                r_in[layer, mine, at] = d_proj.astype(bf16)

        loop(0, OWN_HEADS, conv_back)
        right_copy(layer, W_IN).start()

        d_running = dcol[...] - drow[...].T
        d_decay = mm(jnp.where(row <= col, 1.0, 0.0), d_running, NN)
        pre = gp[layer] + smalls[layer, 1:2, :]
        rate = -jnp.exp(smalls[layer, 0:1, :])
        is_decay = col < HEADS
        d_pre = jnp.where(is_decay, d_decay * rate * sigmoid(pre), 0.0)
        small_sum[layer, LOG_ROW : LOG_ROW + 1, :] = jnp.sum(
            jnp.where(is_decay, d_decay * rate * softplus(pre), 0.0), axis=0, keepdims=True
        )
        small_sum[layer, BIAS_ROW : BIAS_ROW + 1, :] = jnp.sum(d_pre, axis=0, keepdims=True)
        d_gate_pre = (d_pre + dbeta[...] * beta[layer] * (1.0 - beta[layer])).astype(bf16)
        gate_grad = dot(l_in[layer, :, mine], d_gate_pre).T
        for j in range(D // LANES):
            line = GATE_ROW + j * 2 * HEADS
            small_sum[layer, line : line + 2 * HEADS, :] = gate_grad[
                : 2 * HEADS, j * LANES : (j + 1) * LANES
            ]
        slot = swap_slot()

        def in_back(j):
            at = cols_at(j, 256)
            part = dot(r_in[layer, mine, :], w_in[layer, at, :], NT) + dot(
                d_gate_pre, gate_w[layer, :, at]
            )
            big_a[:, at] = part
            swap_out[slot, :, at] = part.astype(bf16)

        loop(0, D // 256, in_back)
        swap_begin(D)
        ready(group + 1)
        add_up(group, 4, chips)
        add_up(group + 1, 0, 1)
        swap_end(D)
        rms_back(source, layer, 0, dmid, dmid, slot)

        @pl.when(sec == layer)
        def _():
            in_grad[...] = dmid[...]

        add_up(group + 1, 1, 3)
        return group + 1

    forward(0, x_in)
    big_x[...] = xs[...]
    forward(1, big_x)
    for layer in range(2):
        for matrix in range(4):
            gather_sent(layer, matrix)
    dmid[...] = cot[...]
    done = backward(1, big_x, -1)
    done = backward(0, x_in, done)

    piece = small_land.shape[1]

    def piece_rows(device):
        return pl.ds(pl.multiple_of(device * piece, piece), piece)

    def small_copy(stage, device, source, target):
        return remote(
            source, target, small_sem.at[stage, 0], small_sem.at[stage, 1], {"dp": device}
        )

    def scatter_small(offset):
        device = lax.rem(me + offset, dp)
        small_copy(0, device, small_mate.at[piece_rows(device), :], small_land.at[me]).start()

    def spread_small(offset):
        device = lax.rem(me + offset, dp)
        small_copy(
            1, device, small_out.at[piece_rows(me), :], small_out.at[piece_rows(me), :]
        ).start()

    to_mate = remote(small_sum.at[1 - sec], small_mate, mate_sem.at[0], mate_sem.at[1], mate)
    to_mate.start()
    add_up(done, 3, 4)
    to_mate.wait()
    small_mate[...] += small_sum[sec]
    loop(1, dp, scatter_small)
    add_up(done, 4, 5)
    small_land[me] = small_mate[piece_rows(me), :]
    others = small_land.at[pl.ds(0, dp - 1)]
    small_copy(0, sibling, others, others).wait_recv()
    small_out[piece_rows(me), :] = jnp.sum(small_land[...], axis=0)
    loop(1, dp, spread_small)
    add_up(done, 5, chips)

    for unit, (matrix, start, width, _, _, _) in enumerate(UNITS):
        part = pl.ds(start, width)

        @pl.when(sec == 0)
        def _(unit=unit, matrix=matrix, part=part):
            last = held[matrix].at[0, slot_rows(chips), part]
            remote(last, last, last_send.at[matrix], last_recv.at[unit], mate).wait_recv()
            grads[matrix][:, whole_cols(unit, 1)] = held[matrix][0, slot_rows(chips), part].astype(f32)

        @pl.when(sec != 0)
        def _(unit=unit, matrix=matrix, part=part):
            last = held[matrix].at[1, slot_rows(chips), part]
            remote(last, last, last_send.at[matrix], last_recv.at[unit], mate).wait_recv()
            grads[matrix][:, whole_cols(unit, 0)] = held[matrix][1, slot_rows(chips), part].astype(f32)

    small_copy(0, sibling, others, others).wait_send()
    spans = small_out.at[pl.ds(0, (dp - 1) * piece), :]
    small_copy(1, sibling, spans, spans).wait()
    for matrix in range(4):
        own = held[matrix].at[0, pl.ds(0, rows), :]
        remote(own, own, own_send.at[matrix], last_recv.at[0], mate).wait_send()
        remote(own, own, last_send.at[matrix], last_recv.at[0], mate).wait_send()
        for layer in range(2):
            ring_sent(layer, matrix)
            left_copy(layer, matrix).wait_send()
            right_copy(layer, matrix).wait_send()


def padded(row):
    return jnp.pad(row, ((0, 0), (0, LANES - row.shape[1])))


def local(
    dp,
    block_input,
    cotangent,
    marks,
    w_in,
    w_out,
    w_up,
    w_down,
    gate_weights,
    norm_gains,
    conv_weights,
    decay_log,
    decay_bias,
    out_gain,
):
    rows = w_in.shape[1]
    chips = dp // 2
    smalls = jnp.concatenate(
        [padded(decay_log), padded(decay_bias), out_gain, jnp.zeros((5, LANES), f32)], axis=0
    )
    gate_w = gate_weights[0].T
    piece = 8 * -(-SMALL_ROWS // (8 * dp))
    vmem = pl.BlockSpec(memory_space=pltpu.VMEM)
    anywhere = pl.BlockSpec(memory_space=pl.ANY)

    def both(width, kind=f32, lines=BLOCK):
        return pltpu.VMEM((2, lines, width), kind)

    def wide(width, kind=f32, lines=BLOCK):
        return pltpu.VMEM((lines, width), kind)

    dma = pltpu.SemaphoreType.DMA
    scratch = (
        [both(width, bf16, D) for width in HALVES]
        + [both(2 * BLOCK, bf16, D) for _ in HALVES]
        + [both(width, bf16, 2 * BLOCK) for width in HALVES]
        + [both(2 * D), both(3 * HALF), both(3 * HALF), both(FF), both(HALF), both(HALF), both(HALF)]
        + [both(D), wide(D), wide(D), wide(D), wide(D), wide(D, bf16)]
        + [both(LANES)] * 4
        + [wide(LANES), pltpu.VMEM((CONV - 1, BLOCK, LANES), f32)]
        + [wide(LANES)] * 3
        + [both(D, bf16, LANES), both(D, f32, 2), both(3 * D, f32, CONV), both(LANES, f32, 8)]
        + [both(D, bf16), both(D, bf16)]
        + [both(LANES, f32, dp * piece), wide(LANES, f32, dp * piece)]
        + [pltpu.VMEM((dp, piece, LANES), f32)]
        + [dma((2, len(UNITS))), dma((4,)), dma((2, len(UNITS), chips - 1))]
        + [dma((2, 4))] * 3
        + [dma((2, 8))] * 2
        + [dma((2,))] * 2
        + [pltpu.SemaphoreType.REGULAR((4,)), dma((2, 2)), dma((4,)), dma((4,))]
        + [dma((len(UNITS),)), dma((4,)), dma((2,))]
    )
    layer_out, in_grad, g_in, g_out, g_up, g_down, small = pl.pallas_call(
        functools.partial(kernel, dp, rows),
        out_shape=[jax.ShapeDtypeStruct((BLOCK, D), f32)] * 2
        + [jax.ShapeDtypeStruct((rows, width), f32) for width in WIDTHS]
        + [jax.ShapeDtypeStruct((dp * piece, LANES), f32)],
        in_specs=[vmem] * 3 + [anywhere] * 4 + [vmem] * 4,
        out_specs=[vmem] * 7,
        scratch_shapes=scratch,
        compiler_params=pltpu.CompilerParams(
            collective_id=0, has_side_effects=True, vmem_limit_bytes=63 * 2**20
        ),
        cost_estimate=pl.CostEstimate(
            flops=6 * BLOCK * D * sum(WIDTHS), bytes_accessed=8 * rows * sum(WIDTHS), transcendentals=0
        ),
    )(
        block_input, cotangent, marks[None, :], w_in[0], w_out[0], w_up[0], w_down[0],
        gate_w, norm_gains[0], conv_weights[0], smalls,
    )
    gate_grad = small[GATE_ROW : GATE_ROW + 128].reshape(D // LANES, 2 * HEADS, LANES)
    rest = (
        gate_grad.transpose(0, 2, 1).reshape(D, 2 * HEADS),
        small[GAIN_ROW:CONV_ROW].reshape(2, D),
        small[CONV_ROW:LOG_ROW].reshape(CONV, 3 * D),
        small[LOG_ROW, :HEADS],
        small[BIAS_ROW, :HEADS],
        small[OUT_ROW],
    )
    return tuple(part[None] for part in (layer_out, in_grad, g_in, g_out, g_up, g_down, *rest))


def solution(mesh):
    sharded, whole, flat = P("section", "dp", None), P("section", None, None), P("section", None)
    return jax.shard_map(
        functools.partial(local, mesh.shape["dp"]),
        mesh=mesh,
        in_specs=(P("dp", None), P("dp", None), P("dp")) + (sharded,) * 4 + (whole,) * 3 + (flat,) * 3,
        out_specs=(sharded,) * 6 + (whole,) * 3 + (flat,) * 3,
        check_vma=False,
    )
```

```python
import functools

import jax
import jax.numpy as jnp
from jax import lax
from jax.experimental import pallas as pl
from jax.experimental.pallas import tpu as pltpu
from jax.sharding import PartitionSpec as P

D = 1024
FF = 2816
HEADS = 8
HEAD_DIM = 128
CONV = 4
BLOCK = 128
LANES = 128
WIDTHS = (4 * D, D, 2 * FF, FF)
HALVES = tuple(width // 2 for width in WIDTHS)
OWN_HEADS = HEADS // 2
HALF = D // 2
W_IN, W_OUT, W_UP, W_DOWN = range(4)
GATE_ROW, GAIN_ROW, CONV_ROW, LOG_ROW, BIAS_ROW, OUT_ROW, SMALL_ROWS = 0, 128, 144, 240, 241, 242, 243

epsilon = 1e-06
highest = lax.Precision.HIGHEST
MESH = pl.DeviceIdType.MESH
f32, bf16 = jnp.float32, jnp.bfloat16

NN = ((1,), (0,))
NT = ((1,), (1,))
TN = ((0,), (0,))


def unit_table():
    units = []
    for part in range(4):
        units.append((W_IN, part * HALVES[W_OUT], HALVES[W_OUT], part % 2, part * D, D // 2))
    for part in range(2):
        width = HALVES[W_OUT] // 2
        units.append((W_OUT, part * width, width, part, part * width, D // 2))
    low = LANES * -(-FF // (4 * LANES))
    for part in range(2):
        for k, (start, width) in enumerate(((0, low), (low, FF // 2 - low))):
            units.append(
                (W_UP, part * (FF // 2) + start, width, (part + k) % 2, part * FF + start, FF // 2)
            )
    for k, (start, width) in enumerate(((0, low), (low, FF // 2 - low))):
        units.append((W_DOWN, start, width, k, start, FF // 2))
    return units


UNITS = unit_table()


def mm(left, right, dims):
    return lax.dot_general(
        left, right, (dims, ((), ())), precision=highest, preferred_element_type=f32
    )


def dot(left, right, dims=NN):
    return lax.dot_general(left, right, (dims, ((), ())), preferred_element_type=f32)


def sigmoid(x):
    return lax.logistic(x)


def softplus(x):
    return jnp.maximum(x, 0.0) + jnp.log1p(jnp.exp(-jnp.abs(x)))


def cols_at(index, width):
    return pl.ds(pl.multiple_of(index * width, width), width)


def loop(lo, hi, body):
    def step(i, carry):
        body(i)
        return carry

    lax.fori_loop(lo, hi, step, 0)


def kernel(
    dp,
    rows,
    x_in, cot, marks, sh_in, sh_out, sh_up, sh_down, gate_in, gains_in, taps_in, smalls_in,
    layer_out, in_grad, g_in, g_out, g_up, g_down, small_out,
    w_in, w_out, w_up, w_down,
    l_in, l_out, l_up, l_down,
    r_in, r_out, r_up, r_down,
    proj, tot, qkv, upg, delta_o, t_inv, pseudo,
    mids, xs, big_x, dmid, big_a, normed,
    gp, cum, cum_t, beta, mask, same, dcol, drow, dbeta,
    gate_w, gains, taps, smalls,
    swap_out, swap_in, small_sum, small_mate, small_land,
    own_sem, own_send, ring_recv, ring_send, sib_recv, sib_send, pair_recv, pair_send,
    swap_recv, swap_send, ready_sem, small_sem, param_recv, param_send, last_recv, last_send, mate_sem,
):
    chips = dp // 2
    half = chips // 2
    sec, me = lax.axis_index("section"), lax.axis_index("dp")
    chip, core = lax.div(me, 2), lax.rem(me, 2)
    shards = (sh_in, sh_out, sh_up, sh_down)
    held = (w_in, w_out, w_up, w_down)
    left = (l_in, l_out, l_up, l_down)
    right = (r_in, r_out, r_up, r_down)
    grads = (g_in, g_out, g_up, g_down)
    mate = {"section": 1 - sec}

    turn = lax.rem(chip, 2)
    spot = (1 - turn) * lax.div(chip, 2) + turn * (chips - 1 - lax.div(chip, 2))

    def device_at(position):
        back = lax.div(position, half)
        there = (1 - back) * 2 * position + back * (2 * (chips - 1 - position) + 1)
        return 2 * there + core

    towards = (
        device_at(lax.rem(spot + 1, chips)),
        device_at(lax.rem(spot + chips - 1, chips)),
    )
    sibling = 2 * chip + 1 - core

    def rows_of(device):
        return pl.ds(pl.multiple_of(device * rows, rows), rows)

    def remote(source, target, sent, arrival, device):
        return pltpu.make_async_remote_copy(
            src_ref=source,
            dst_ref=target,
            send_sem=sent,
            recv_sem=arrival,
            device_id=device,
            device_id_type=MESH,
        )

    def whole_cols(unit, section):
        _, _, width, _, base, span = UNITS[unit]
        return pl.ds(pl.multiple_of(base + section * span, LANES), width)

    barrier = pltpu.get_barrier_semaphore()

    def greet(offset):
        pl.semaphore_signal(
            barrier, inc=1, device_id={"dp": lax.rem(me + offset, dp)}, device_id_type=MESH
        )

    loop(1, dp, greet)
    pl.semaphore_signal(barrier, inc=1, device_id=mate, device_id_type=MESH)
    pl.semaphore_wait(barrier, dp)

    def own_part(layer, unit):
        matrix, start, width = UNITS[unit][:3]
        return held[matrix].at[layer, rows_of(me), pl.ds(start, width)]

    def place(layer, matrices):
        @pl.when(sec == layer)
        def _():
            for unit, entry in enumerate(UNITS):
                matrix = entry[0]
                if matrix not in matrices:
                    continue
                remote(
                    shards[matrix].at[:, whole_cols(unit, 1 - layer)],
                    own_part(layer, unit),
                    own_send.at[matrix],
                    own_sem.at[layer, unit],
                    mate,
                ).start()
                pltpu.make_async_copy(
                    shards[matrix].at[:, whole_cols(unit, layer)],
                    own_part(layer, unit),
                    own_sem.at[layer, unit],
                ).start()

    MIX, FFN = (W_IN, W_OUT), (W_UP, W_DOWN)
    stages = ((0, MIX), (0, FFN), (1, MIX), (1, FFN))
    place(*stages[0])

    small_inputs = ((gate_in, gate_w), (gains_in, gains), (taps_in, taps), (smalls_in, smalls))

    def param_copy(index):
        source, target = small_inputs[index]
        lines = pl.ds(0, source.shape[0])
        return remote(
            source, target.at[sec, lines], param_send.at[index], param_recv.at[index], mate
        )

    for index, (source, target) in enumerate(small_inputs):
        param_copy(index).start()
        target[sec, 0 : source.shape[0], :] = source[...]
    for layer in range(2):
        gate_w[layer, 2 * HEADS :, :] = jnp.zeros((LANES - 2 * HEADS, D), bf16)

    def ring_copy(layer, unit, source, target, step):
        matrix, way = UNITS[unit][0], UNITS[unit][3]
        return remote(
            source, target, ring_send.at[layer, matrix], ring_recv.at[layer, unit, step], {"dp": towards[way]}
        )

    def to_sibling(layer, matrix, source, target):
        return remote(
            source, target, sib_send.at[layer, matrix], sib_recv.at[layer, matrix], {"dp": sibling}
        )

    def origin(way, step):
        if way == 0:
            return lax.rem(spot + 2 * chips - 1 - step, chips)
        return lax.rem(spot + 1 + step, chips)

    def units_of(matrices):
        return [(unit, *entry[:4]) for unit, entry in enumerate(UNITS) if entry[0] in matrices]

    def send_own(layer, matrices):
        for unit, matrix, start, width, way in units_of(matrices):
            block = own_part(layer, unit)
            pltpu.make_async_copy(block, block, own_sem.at[layer, unit]).wait()
            ring_copy(layer, unit, block, block, 0).start()
            to_sibling(layer, matrix, block, block).start()

    def gather_step(layer, matrices, step, last=False, only=None):
        for unit, matrix, start, width, way in units_of(matrices)[slice(only, None if only is None else only + 1)]:
            device = device_at(origin(way, step))
            block = held[matrix].at[layer, rows_of(device), pl.ds(start, width)]
            ring_copy(layer, unit, block, block, step).wait_recv()
            if not last:
                ring_copy(layer, unit, block, block, step + 1).start()
            to_sibling(layer, matrix, block, block).start()

    def gather_rest(layer, matrices, lo, hi):
        if lo < hi:
            loop(lo, hi, lambda step: gather_step(layer, matrices, step))

    def gather_end(layer, matrices):
        for matrix in matrices:
            every = held[matrix].at[layer, pl.ds(0, chips * rows), :]
            to_sibling(layer, matrix, every, every).wait_recv()

    def gather_sent(layer, matrix):
        every = held[matrix].at[layer, pl.ds(0, chips * rows), :]
        to_sibling(layer, matrix, every, every).wait_send()
        ring_sent(layer, matrix)

    def ring_sent(layer, matrix):
        most = held[matrix].at[layer, pl.ds(0, (chips - 1) * rows), :]
        remote(
            most, most, ring_send.at[layer, matrix], ring_recv.at[layer, 0, 0], {"dp": towards[0]}
        ).wait_send()

    final = chips - 2

    fed = [0, 0, 0]

    def next_stage(stage):
        if stage + 1 < len(stages):
            send_own(*stages[stage + 1])
        if stage + 2 < len(stages):
            place(*stages[stage + 2])

    def feed(count):
        for _ in range(count):
            stage, step, part = fed
            if stage == len(stages):
                return
            layer, matrices = stages[stage]
            if step == final - 1 and part == 0:
                next_stage(stage)
            gather_step(layer, matrices, step, step == final, part)
            part += 1
            if part == len(units_of(matrices)):
                step, part = step + 1, 0
            if step > final:
                stage, step = stage + 1, 0
            fed[:] = [stage, step, part]

    def feed_all(stage):
        while fed[0] <= stage and fed[0] < len(stages):
            if fed[2] == 0 and fed[1] < final - 1:
                gather_rest(*stages[fed[0]], fed[1], final - 1)
                fed[1] = final - 1
            else:
                feed(1)

    send_own(*stages[0])
    place(*stages[1])

    row = lax.broadcasted_iota(jnp.int32, (BLOCK, BLOCK), 0)
    col = lax.broadcasted_iota(jnp.int32, (BLOCK, BLOCK), 1)
    starts = jnp.logical_or(marks[...] > 0, col[:1] == 0)
    starts = jnp.where(starts, 1.0, 0.0)
    seg_col = jnp.sum(jnp.where(row >= col, starts, 0.0), axis=1, keepdims=True)
    seg_row = jnp.sum(jnp.where(row == col, seg_col, 0.0), axis=0, keepdims=True)
    within = jnp.where(jnp.logical_and(seg_col == seg_row, row >= col), 1.0, 0.0)
    mask[...] = within
    for m in range(1, CONV):
        near = jnp.sum(jnp.where(row - col == m, within, 0.0), axis=1, keepdims=True)
        same[m - 1] = jnp.broadcast_to(near, (BLOCK, LANES))
    small_sum[...] = jnp.zeros(small_sum.shape, f32)

    feed_all(0)
    for index in range(len(small_inputs)):
        param_copy(index).wait()

    swaps = [0]

    def swap_begin(width):
        slot = swaps[0] % 2
        swaps[0] += 1
        part = pl.ds(0, width)
        remote(
            swap_out.at[slot, :, part], swap_in.at[slot, :, part],
            swap_send.at[slot], swap_recv.at[slot], mate,
        ).start()

    def swap_slot():
        return swaps[0] % 2

    def swap_end(width):
        slot = (swaps[0] - 1) % 2
        part = pl.ds(0, width)
        remote(
            swap_out.at[slot, :, part], swap_in.at[slot, :, part],
            swap_send.at[slot], swap_recv.at[slot], mate,
        ).wait()
        return slot

    def left_copy(layer, matrix):
        array = left[matrix]
        return remote(
            array.at[layer, :, pl.ds(0, BLOCK)], array.at[layer, :, pl.ds(BLOCK, BLOCK)],
            pair_send.at[layer, matrix], pair_recv.at[layer, matrix], {"dp": sibling},
        )

    def right_copy(layer, matrix):
        array = right[matrix]
        return remote(
            array.at[layer, pl.ds(0, BLOCK), :], array.at[layer, pl.ds(BLOCK, BLOCK), :],
            pair_send.at[layer, 4 + matrix], pair_recv.at[layer, 4 + matrix], {"dp": sibling},
        )

    own_half = pl.ds(pl.multiple_of(sec * HALF, HALF), HALF)
    other_half = pl.ds(pl.multiple_of((1 - sec) * HALF, HALF), HALF)
    mine = pl.ds(0, BLOCK)

    def lane_of(array, lane):
        return jnp.sum(jnp.where(col == lane, array, 0.0), axis=1, keepdims=True)

    def row_of(array, which):
        return jnp.sum(jnp.where(row == which, array, 0.0), axis=0, keepdims=True)

    def part_at(part, i):
        return cols_at(part * OWN_HEADS + i, HEAD_DIM)

    def tap_cols(part, i):
        return cols_at(part * HEADS + sec * OWN_HEADS + i, HEAD_DIM)

    def turn_over(source, layer, turned):
        def part(i):
            at = cols_at(i, 128)
            turned[layer, at, mine] = source[:, at].astype(f32).T.astype(bf16)

        loop(0, D // 128, part)

    def rms(source, layer, gain_row, turned):
        def part(i):
            at = cols_at(i, 32)
            x = source[at, :]
            scale = lax.rsqrt(jnp.mean(x * x, axis=1, keepdims=True) + epsilon)
            normed[at, :] = (x * scale * gains[layer, gain_row : gain_row + 1, :]).astype(bf16)

        loop(0, BLOCK // 32, part)
        turn_over(normed, layer, turned)

    def spread(layer, i):
        h = sec * OWN_HEADS + i
        gap = lane_of(cum[layer], h) - row_of(cum_t[layer], h)
        return jnp.where(mask[...] > 0.0, jnp.exp(jnp.minimum(gap, 0.0)), 0.0)

    apart = jnp.bitwise_xor(row, col)

    def delta_forward(layer, pause):
        span = range(OWN_HEADS)
        weights = [spread(layer, i) for i in span]
        betas = [lane_of(beta[layer], HEADS + sec * OWN_HEADS + i) for i in span]
        keys = [qkv[layer, :, part_at(1, i)] for i in span]
        below = [
            jnp.where(row > col, weights[i], 0.0) * mm(keys[i], keys[i], NT) * betas[i]
            for i in span
        ]
        inverse = [jnp.where(row == col, 1.0, 0.0) - jnp.where(apart == 1, below[i], 0.0) for i in span]
        size = 2
        while size < BLOCK:
            level = jnp.logical_and(apart >= size, apart < 2 * size)
            inner = [mm(jnp.where(level, below[i], 0.0), inverse[i], NN) for i in span]
            inverse = [inverse[i] - mm(inverse[i], inner[i], NN) for i in span]
            if size in (4, 16, 64):
                pause()
            size *= 2
        solved = [mm(inverse[i], betas[i] * qkv[layer, :, part_at(2, i)], NN) for i in span]
        for i in span:
            at = part_at(0, i)
            score = mm(qkv[layer, :, at], keys[i], NT) * weights[i]
            delta_o[layer, :, at] = mm(score, solved[i], NN)
            t_inv[layer, :, at] = inverse[i]
            pseudo[layer, :, at] = solved[i]

    def forward(layer, source):
        stage = 2 * layer + 1
        rms(source, layer, 0, l_in)
        feed_all(stage - 1)
        gather_end(layer, MIX)

        def project(j):
            at = cols_at(j, 512)
            proj[layer, :, at] = dot(normed[...], w_in[layer, :, at])

        loop(0, HALVES[W_IN] // 512, project)
        feed(4)
        pre = dot(normed[...], gate_w[layer], NT)
        gp[layer] = pre
        beta[layer] = sigmoid(pre)
        decay = -jnp.exp(smalls[layer, 0:1, :]) * softplus(pre + smalls[layer, 1:2, :])
        running = mm(jnp.where(row >= col, 1.0, 0.0), decay, NN)
        cum[layer] = running
        cum_t[layer] = running.T
        left_copy(layer, W_IN).start()
        feed(4)

        def head_parts(i):
            for part in range(3):
                at, tap = part_at(part, i), tap_cols(part, i)
                x = proj[layer, :, at]
                total = x * taps[layer, CONV - 1 : CONV, tap]
                for m in range(1, CONV):
                    total += pltpu.roll(x, m, 0) * same[m - 1] * taps[layer, CONV - 1 - m : CONV - m, tap]
                tot[layer, :, at] = total
                value = total * sigmoid(total)
                if part < 2:
                    value = value * lax.rsqrt(jnp.sum(value * value, axis=1, keepdims=True) + epsilon)
                if part == 0:
                    value = value * HEAD_DIM ** (-0.5)
                qkv[layer, :, at] = value

        loop(0, OWN_HEADS // 2, head_parts)
        feed(4)
        loop(OWN_HEADS // 2, OWN_HEADS, head_parts)
        feed(4)
        delta_forward(layer, lambda: feed(4))
        feed(4)
        slot = swap_slot()

        def gate_norm(i):
            at = part_at(0, i)
            out = delta_o[layer, :, at]
            scale = lax.rsqrt(jnp.mean(out * out, axis=1, keepdims=True) + epsilon)
            gate = proj[layer, :, part_at(3, i)]
            mixed = out * scale * smalls[layer, 2:3, :] * (gate * sigmoid(gate))
            swap_out[slot, :, at] = mixed.astype(bf16)

        loop(0, OWN_HEADS, gate_norm)
        swap_begin(HALF)
        normed[:, own_half] = swap_out[slot, :, pl.ds(0, HALF)]
        feed(6)
        swap_end(HALF)
        normed[:, other_half] = swap_in[slot, :, pl.ds(0, HALF)]
        total = dot(normed[...], w_out[layer])
        slot = swap_slot()
        swap_out[slot, :, pl.ds(0, HALF)] = total.astype(bf16)
        swap_begin(HALF)
        mids[layer, :, own_half] = source[:, own_half] + total
        turn_over(normed, layer, l_out)
        left_copy(layer, W_OUT).start()
        feed(6)
        swap_end(HALF)
        mids[layer, :, other_half] = source[:, other_half] + swap_in[slot, :, pl.ds(0, HALF)].astype(f32)
        rms(mids.at[layer], layer, 1, l_up)
        left_copy(layer, W_UP).start()
        feed_all(stage)
        gather_end(layer, FFN)

        def up_part(j):
            at = cols_at(j, 256)
            upg[layer, :, at] = dot(normed[...], w_up[layer, :, at])

        middle = FF // 256 // 2
        loop(0, middle, up_part)
        feed(4)
        loop(middle, FF // 256, up_part)
        feed(4)

        def hidden_part(j):
            at = cols_at(j, LANES)
            first, second = upg[layer, :, at], upg[layer, :, cols_at(j + FF // 2 // LANES, LANES)]
            r_down[layer, mine, at] = (first * sigmoid(first) * second).astype(bf16)

        loop(0, FF // 2 // LANES, hidden_part)
        right_copy(layer, W_DOWN).start()
        feed(4)
        slot = swap_slot()

        def down_part(j):
            at = cols_at(j, 256)
            part = dot(r_down[layer, mine, :], w_down[layer, at, :], NT)
            big_a[:, at] = part
            swap_out[slot, :, at] = part.astype(bf16)

        loop(0, D // 256, down_part)
        swap_begin(D)
        feed(8)
        swap_end(D)
        xs[...] = mids[layer] + (big_a[...] + swap_in[slot].astype(f32))

        @pl.when(sec == layer)
        def _():
            layer_out[...] = xs[...]

        feed(6)

    def ready(group):
        for device in ({"dp": towards[0]}, {"dp": towards[1]}, mate):
            pl.semaphore_signal(ready_sem.at[group], inc=1, device_id=device, device_id_type=MESH)

    def slot_rows(index):
        return pl.ds(pl.multiple_of(index * rows, rows), rows)

    def sum_step(layer, matrices, step, place, only=None):
        for unit, matrix, start, width, way in units_of(matrices)[slice(only, None if only is None else only + 1)]:
            part = pl.ds(start, width)
            owner = device_at(origin(way, step))
            own = dot(left[matrix][layer, rows_of(owner), :], right[matrix][layer, :, part])
            before = slot_rows(chips - 1 if place == 0 else step - 1)
            here = held[matrix].at[layer, before, part]
            if place > 0:
                ring_copy(layer, unit, here, here, step - 1).wait_recv()
                own = own + held[matrix][layer, before, part].astype(f32)
            if place < 2:
                held[matrix][layer, before, part] = own.astype(bf16)
                ring_copy(
                    layer, unit, here, held[matrix].at[layer, slot_rows(step), part], step
                ).start()
            else:

                @pl.when(sec == layer)
                def _():
                    grads[matrix][:, whole_cols(unit, layer)] = own

                @pl.when(sec != layer)
                def _():
                    held[matrix][layer, slot_rows(chips), part] = own.astype(bf16)
                    last = held[matrix].at[layer, slot_rows(chips), part]
                    remote(last, last, last_send.at[matrix], last_recv.at[unit], mate).start()

    sums = ((1, FFN), (1, MIX), (0, FFN), (0, MIX))

    added = [0, 0, 0]

    def add_begin(group):
        layer, matrices = sums[group]
        for matrix in matrices:
            left_copy(layer, matrix).wait_recv()
            right_copy(layer, matrix).wait_recv()
        pl.semaphore_wait(ready_sem.at[group], 3)

    def add_up(count, upto):
        for _ in range(count):
            group, step, part = added
            if group >= upto:
                return
            layer, matrices = sums[group]
            if step == 0 and part == 0:
                add_begin(group)
            sum_step(layer, matrices, step, 0 if step == 0 else 1 if step < chips - 1 else 2, part)
            part += 1
            if part == len(units_of(matrices)):
                step, part = step + 1, 0
            if step == chips:
                group, step = group + 1, 0
            added[:] = [group, step, part]

    def add_all(upto):
        while added[0] < upto:
            if added[2] == 0 and 0 < added[1] < chips - 1:
                layer, matrices = sums[added[0]]
                loop(added[1], chips - 1, lambda step: sum_step(layer, matrices, step, 1))
                added[1] = chips - 1
            else:
                add_up(1, upto)

    def rms_back(source, layer, gain_row, rest, target, slot):
        gain = gains[layer, gain_row : gain_row + 1, :]

        def part(i, total):
            at = cols_at(i, 32)
            x, dy = source[at, :], big_a[at, :] + swap_in[slot, at, :].astype(f32)
            scale = lax.rsqrt(jnp.mean(x * x, axis=1, keepdims=True) + epsilon)
            unit = x * scale
            dyg = dy * gain
            dx = scale * (dyg - unit * jnp.mean(dyg * unit, axis=1, keepdims=True))
            target[at, :] = dx + rest[at, :]
            return total + jnp.sum(dy * unit, axis=0, keepdims=True)

        total = lax.fori_loop(0, BLOCK // 32, part, jnp.zeros((1, D), f32))

        @pl.when(sec == layer)
        def _():
            for j in range(D // LANES):
                line = GAIN_ROW + gain_row * (D // LANES) + j
                small_sum[layer, line : line + 1, :] = total[:, j * LANES : (j + 1) * LANES]

    strict = row > col

    def backward(layer, source, before):
        group = before + 1
        normed[...] = dmid[...].astype(bf16)
        turn_over(normed, layer, l_down)
        left_copy(layer, W_DOWN).start()
        add_up(4, group)

        def hidden_back(j):
            at = cols_at(j, LANES)
            other = cols_at(j + FF // 2 // LANES, LANES)
            d_hidden = dot(normed[...], w_down[layer, :, at])
            first, second = upg[layer, :, at], upg[layer, :, other]
            gate = sigmoid(first)
            r_up[layer, mine, at] = (
                d_hidden * second * gate * (1.0 + first * (1.0 - gate))
            ).astype(bf16)
            r_up[layer, mine, other] = (d_hidden * (first * gate)).astype(bf16)

        loop(0, FF // 2 // LANES, hidden_back)
        right_copy(layer, W_UP).start()
        add_up(4, group)
        slot = swap_slot()

        def up_back(j):
            at = cols_at(j, 256)
            part = dot(r_up[layer, mine, :], w_up[layer, at, :], NT)
            big_a[:, at] = part
            swap_out[slot, :, at] = part.astype(bf16)

        loop(0, D // 256, up_back)
        swap_begin(D)
        ready(group)
        add_all(group)
        add_up(8, group + 1)
        swap_end(D)
        rms_back(mids.at[layer], layer, 1, dmid, dmid, slot)
        r_out[layer, mine, :] = dmid[:, own_half].astype(bf16)
        right_copy(layer, W_OUT).start()
        slot = swap_slot()

        def mixer_back(j):
            at = cols_at(j, 256)
            theirs = pl.ds(pl.multiple_of((1 - sec) * HALF + j * 256, 256), 256)
            swap_out[slot, :, at] = dot(r_out[layer, mine, :], w_out[layer, theirs, :], NT).astype(bf16)

        loop(0, HALF // 256, mixer_back)
        swap_begin(HALF)

        def mixer_own(j):
            at = cols_at(j, 256)
            ours = pl.ds(pl.multiple_of(sec * HALF + j * 256, 256), 256)
            big_a[:, at] = dot(r_out[layer, mine, :], w_out[layer, ours, :], NT)

        loop(0, HALF // 256, mixer_own)
        add_up(6, group + 1)
        swap_end(HALF)

        def gate_norm_back(i):
            at = part_at(0, i)
            out = delta_o[layer, :, at]
            scale = lax.rsqrt(jnp.mean(out * out, axis=1, keepdims=True) + epsilon)
            unit = out * scale
            gate = proj[layer, :, part_at(3, i)]
            passed = sigmoid(gate)
            d_mixed = big_a[:, at] + swap_in[slot, :, at].astype(f32)
            gain = smalls[layer, 2:3, :]
            d_gate = d_mixed * unit * gain * (passed * (1.0 + gate * (1.0 - passed)))
            r_in[layer, mine, part_at(3, i)] = d_gate.astype(bf16)
            d_scaled = d_mixed * (gate * passed)
            small_sum[layer, OUT_ROW : OUT_ROW + 1, :] += jnp.sum(d_scaled * unit, axis=0, keepdims=True)
            d_unit = d_scaled * gain
            delta_o[layer, :, at] = scale * (d_unit - unit * jnp.mean(d_unit * unit, axis=1, keepdims=True))

        loop(0, OWN_HEADS, gate_norm_back)
        add_up(4, group + 1)

        dcol[...] = jnp.zeros(dcol.shape, f32)
        drow[...] = jnp.zeros(drow.shape, f32)
        dbeta[...] = jnp.zeros(dbeta.shape, f32)

        def norm_silu_back(part, i, d_value):
            at = part_at(part, i)
            total = tot[layer, :, at]
            passed = sigmoid(total)
            if part < 2:
                raw = total * passed
                scale = lax.rsqrt(jnp.sum(raw * raw, axis=1, keepdims=True) + epsilon)
                unit = raw * scale
                if part == 0:
                    d_value = d_value * HEAD_DIM ** (-0.5)
                d_value = scale * (d_value - unit * jnp.sum(d_value * unit, axis=1, keepdims=True))
            tot[layer, :, at] = d_value * (passed * (1.0 + total * (1.0 - passed)))

        def delta_backward(i):
            h = sec * OWN_HEADS + i
            at = part_at(0, i)
            weights = spread(layer, i)
            query, key, value = [qkv[layer, :, part_at(part, i)] for part in range(3)]
            write = lane_of(beta[layer], HEADS + h)
            solved, d_out = pseudo[layer, :, at], delta_o[layer, :, at]
            key_key = mm(key, key, NT)
            query_key = mm(query, key, NT)
            d_score = mm(d_out, solved, NT)
            d_pseudo = mm(query_key * weights, d_out, TN)
            d_right = mm(t_inv[layer, :, at], d_pseudo, TN)
            d_left = jnp.where(strict, -mm(d_right, solved, NT), 0.0)
            left_key = d_left * weights
            d_write = jnp.sum(d_right * value, axis=1, keepdims=True) + jnp.sum(
                left_key * key_key, axis=1, keepdims=True
            )
            d_query_key = d_score * weights
            d_key_key = left_key * write
            norm_silu_back(0, i, mm(d_query_key, key, NN))
            norm_silu_back(
                1, i, mm(d_query_key, query, TN) + mm(d_key_key, key, NN) + mm(d_key_key, key, TN)
            )
            norm_silu_back(2, i, write * d_right)
            d_gap = d_query_key * query_key + d_key_key * key_key
            dcol[...] += jnp.where(col == h, jnp.sum(d_gap, axis=1, keepdims=True), 0.0)
            drow[...] += jnp.where(row == h, jnp.sum(d_gap, axis=0, keepdims=True), 0.0)
            dbeta[...] += jnp.where(col == HEADS + h, d_write, 0.0)

        for i in range(OWN_HEADS):
            delta_backward(i)
            add_up(4, group + 1)

        def conv_back(i):
            for part in range(3):
                at, tap = part_at(part, i), tap_cols(part, i)
                d_total, x = tot[layer, :, at], proj[layer, :, at]
                d_proj = d_total * taps[layer, CONV - 1 : CONV, tap]
                line = CONV_ROW + part * HEADS + sec * OWN_HEADS + i
                tiles = 3 * D // LANES
                small_sum[layer, pl.ds(line + (CONV - 1) * tiles, 1), :] = jnp.sum(
                    d_total * x, axis=0, keepdims=True
                )
                for m in range(1, CONV):
                    met = d_total * same[m - 1]
                    weight = taps[layer, CONV - 1 - m : CONV - m, tap]
                    d_proj += pltpu.roll(met * weight, BLOCK - m, 0)
                    small_sum[layer, pl.ds(line + (CONV - 1 - m) * tiles, 1), :] = jnp.sum(
                        met * pltpu.roll(x, m, 0), axis=0, keepdims=True
                    )
                r_in[layer, mine, at] = d_proj.astype(bf16)

        loop(0, OWN_HEADS, conv_back)
        right_copy(layer, W_IN).start()
        add_up(4, group + 1)

        d_running = dcol[...] - drow[...].T
        d_decay = mm(jnp.where(row <= col, 1.0, 0.0), d_running, NN)
        pre = gp[layer] + smalls[layer, 1:2, :]
        rate = -jnp.exp(smalls[layer, 0:1, :])
        is_decay = col < HEADS
        d_pre = jnp.where(is_decay, d_decay * rate * sigmoid(pre), 0.0)
        small_sum[layer, LOG_ROW : LOG_ROW + 1, :] = jnp.sum(
            jnp.where(is_decay, d_decay * rate * softplus(pre), 0.0), axis=0, keepdims=True
        )
        small_sum[layer, BIAS_ROW : BIAS_ROW + 1, :] = jnp.sum(d_pre, axis=0, keepdims=True)
        d_gate_pre = (d_pre + dbeta[...] * beta[layer] * (1.0 - beta[layer])).astype(bf16)
        gate_grad = dot(l_in[layer, :, mine], d_gate_pre).T
        for j in range(D // LANES):
            line = GATE_ROW + j * 2 * HEADS
            small_sum[layer, line : line + 2 * HEADS, :] = gate_grad[
                : 2 * HEADS, j * LANES : (j + 1) * LANES
            ]
        slot = swap_slot()

        def in_back(j):
            at = cols_at(j, 256)
            part = dot(r_in[layer, mine, :], w_in[layer, at, :], NT) + dot(
                d_gate_pre, gate_w[layer, :, at]
            )
            big_a[:, at] = part
            swap_out[slot, :, at] = part.astype(bf16)

        loop(0, D // 256, in_back)
        swap_begin(D)
        ready(group + 1)
        add_all(group + 1)
        add_up(6, group + 2)
        swap_end(D)
        rms_back(source, layer, 0, dmid, dmid, slot)

        @pl.when(sec == layer)
        def _():
            in_grad[...] = dmid[...]

        add_up(4, group + 2)
        return group + 1

    forward(0, x_in)
    big_x[...] = xs[...]
    forward(1, big_x)
    for layer in range(2):
        for matrix in range(4):
            gather_sent(layer, matrix)
    dmid[...] = cot[...]
    done = backward(1, big_x, -1)
    done = backward(0, x_in, done)

    piece = small_land.shape[1]

    def piece_rows(device):
        return pl.ds(pl.multiple_of(device * piece, piece), piece)

    def small_copy(stage, device, source, target):
        return remote(
            source, target, small_sem.at[stage, 0], small_sem.at[stage, 1], {"dp": device}
        )

    def scatter_small(offset):
        device = lax.rem(me + offset, dp)
        small_copy(0, device, small_mate.at[piece_rows(device), :], small_land.at[me]).start()

    def spread_small(offset):
        device = lax.rem(me + offset, dp)
        small_copy(
            1, device, small_out.at[piece_rows(me), :], small_out.at[piece_rows(me), :]
        ).start()

    to_mate = remote(small_sum.at[1 - sec], small_mate, mate_sem.at[0], mate_sem.at[1], mate)
    to_mate.start()
    add_up(6, done + 1)
    to_mate.wait()
    small_mate[...] += small_sum[sec]
    loop(1, dp, scatter_small)
    add_up(12, done + 1)
    small_land[me] = small_mate[piece_rows(me), :]
    others = small_land.at[pl.ds(0, dp - 1)]
    small_copy(0, sibling, others, others).wait_recv()
    small_out[piece_rows(me), :] = jnp.sum(small_land[...], axis=0)
    loop(1, dp, spread_small)
    add_all(done + 1)

    for unit, (matrix, start, width, _, _, _) in enumerate(UNITS):
        part = pl.ds(start, width)

        @pl.when(sec == 0)
        def _(unit=unit, matrix=matrix, part=part):
            last = held[matrix].at[0, slot_rows(chips), part]
            remote(last, last, last_send.at[matrix], last_recv.at[unit], mate).wait_recv()
            grads[matrix][:, whole_cols(unit, 1)] = held[matrix][0, slot_rows(chips), part].astype(f32)

        @pl.when(sec != 0)
        def _(unit=unit, matrix=matrix, part=part):
            last = held[matrix].at[1, slot_rows(chips), part]
            remote(last, last, last_send.at[matrix], last_recv.at[unit], mate).wait_recv()
            grads[matrix][:, whole_cols(unit, 0)] = held[matrix][1, slot_rows(chips), part].astype(f32)

    small_copy(0, sibling, others, others).wait_send()
    spans = small_out.at[pl.ds(0, (dp - 1) * piece), :]
    small_copy(1, sibling, spans, spans).wait()
    for matrix in range(4):
        own = held[matrix].at[0, pl.ds(0, rows), :]
        remote(own, own, own_send.at[matrix], last_recv.at[0], mate).wait_send()
        remote(own, own, last_send.at[matrix], last_recv.at[0], mate).wait_send()
        for layer in range(2):
            ring_sent(layer, matrix)
            left_copy(layer, matrix).wait_send()
            right_copy(layer, matrix).wait_send()


def closing_kernel(*refs):
    bigs, small, outs, places, sem = refs[:6], refs[6], refs[7:13], refs[13:19], refs[19]
    copies = [
        pltpu.make_async_copy(big, out.at[0], sem.at[i]) for i, (big, out) in enumerate(zip(bigs, outs))
    ]
    for copy in copies:
        copy.start()
    gate, gains, taps, log, bias, out_gain = places
    turned = small[GATE_ROW : GATE_ROW + D // LANES * 2 * HEADS, :].T
    for j in range(D // LANES):
        at = slice(j * LANES, (j + 1) * LANES)
        gate[0, at, :] = turned[:, j * 2 * HEADS : (j + 1) * 2 * HEADS]
        for k in range(2):
            line = GAIN_ROW + k * (D // LANES) + j
            gains[0, k : k + 1, at] = small[line : line + 1, :]
    for j in range(3 * D // LANES):
        at = slice(j * LANES, (j + 1) * LANES)
        for k in range(CONV):
            line = CONV_ROW + k * (3 * D // LANES) + j
            taps[0, k : k + 1, at] = small[line : line + 1, :]
    log[...] = small[LOG_ROW : LOG_ROW + 1, :HEADS]
    bias[...] = small[BIAS_ROW : BIAS_ROW + 1, :HEADS]
    out_gain[...] = small[OUT_ROW : OUT_ROW + 1, :]
    for copy in copies:
        copy.wait()


def padded(row):
    return jnp.pad(row, ((0, 0), (0, LANES - row.shape[1])))


def local(
    dp,
    block_input,
    cotangent,
    marks,
    w_in,
    w_out,
    w_up,
    w_down,
    gate_weights,
    norm_gains,
    conv_weights,
    decay_log,
    decay_bias,
    out_gain,
):
    rows = w_in.shape[1]
    chips = dp // 2
    smalls = jnp.concatenate(
        [padded(decay_log), padded(decay_bias), out_gain, jnp.zeros((5, LANES), f32)], axis=0
    )
    gate_w = gate_weights[0].T
    piece = 8 * -(-SMALL_ROWS // (8 * dp))
    vmem = pl.BlockSpec(memory_space=pltpu.VMEM)
    anywhere = pl.BlockSpec(memory_space=pl.ANY)

    def both(width, kind=f32, lines=BLOCK):
        return pltpu.VMEM((2, lines, width), kind)

    def wide(width, kind=f32, lines=BLOCK):
        return pltpu.VMEM((lines, width), kind)

    dma = pltpu.SemaphoreType.DMA
    scratch = (
        [both(width, bf16, D) for width in HALVES]
        + [both(2 * BLOCK, bf16, D) for _ in HALVES]
        + [both(width, bf16, 2 * BLOCK) for width in HALVES]
        + [both(2 * D), both(3 * HALF), both(3 * HALF), both(FF), both(HALF), both(HALF), both(HALF)]
        + [both(D), wide(D), wide(D), wide(D), wide(D), wide(D, bf16)]
        + [both(LANES)] * 4
        + [wide(LANES), pltpu.VMEM((CONV - 1, BLOCK, LANES), f32)]
        + [wide(LANES)] * 3
        + [both(D, bf16, LANES), both(D, f32, 2), both(3 * D, f32, CONV), both(LANES, f32, 8)]
        + [both(D, bf16), both(D, bf16)]
        + [both(LANES, f32, dp * piece), wide(LANES, f32, dp * piece)]
        + [pltpu.VMEM((dp, piece, LANES), f32)]
        + [dma((2, len(UNITS))), dma((4,)), dma((2, len(UNITS), chips - 1))]
        + [dma((2, 4))] * 3
        + [dma((2, 8))] * 2
        + [dma((2,))] * 2
        + [pltpu.SemaphoreType.REGULAR((4,)), dma((2, 2)), dma((4,)), dma((4,))]
        + [dma((len(UNITS),)), dma((4,)), dma((2,))]
    )
    *bigs, small = pl.pallas_call(
        functools.partial(kernel, dp, rows),
        out_shape=[jax.ShapeDtypeStruct((BLOCK, D), f32)] * 2
        + [jax.ShapeDtypeStruct((rows, width), f32) for width in WIDTHS]
        + [jax.ShapeDtypeStruct((dp * piece, LANES), f32)],
        in_specs=[vmem] * 3 + [anywhere] * 4 + [vmem] * 4,
        out_specs=[vmem] * 7,
        scratch_shapes=scratch,
        compiler_params=pltpu.CompilerParams(
            collective_id=0, has_side_effects=True, vmem_limit_bytes=63 * 2**20
        ),
        cost_estimate=pl.CostEstimate(
            flops=6 * BLOCK * D * sum(WIDTHS), bytes_accessed=8 * rows * sum(WIDTHS), transcendentals=0
        ),
    )(
        block_input, cotangent, marks[None, :], w_in[0], w_out[0], w_up[0], w_down[0],
        gate_w, norm_gains[0], conv_weights[0], smalls,
    )
    shapes = [(1, *big.shape) for big in bigs]
    shapes += [(1, D, 2 * HEADS), (1, 2, D), (1, CONV, 3 * D), (1, HEADS), (1, HEADS), (1, LANES)]
    return tuple(
        pl.pallas_call(
            closing_kernel,
            out_shape=[jax.ShapeDtypeStruct(shape, f32) for shape in shapes],
            in_specs=[anywhere] * 6 + [vmem],
            out_specs=[vmem] * 12,
            scratch_shapes=[dma((6,))],
            compiler_params=pltpu.CompilerParams(vmem_limit_bytes=32 * 2**20),
        )(*bigs, small)
    )


def solution(mesh):
    sharded, whole, flat = P("section", "dp", None), P("section", None, None), P("section", None)
    return jax.shard_map(
        functools.partial(local, mesh.shape["dp"]),
        mesh=mesh,
        in_specs=(P("dp", None), P("dp", None), P("dp")) + (sharded,) * 4 + (whole,) * 3 + (flat,) * 3,
        out_specs=(sharded,) * 6 + (whole,) * 3 + (flat,) * 3,
        check_vma=False,
    )
```

```python
import functools

import jax
import jax.numpy as jnp
from jax import lax
from jax.experimental import pallas as pl
from jax.experimental.pallas import tpu as pltpu
from jax.sharding import PartitionSpec as P

D = 1024
FF = 2816
HEADS = 8
HEAD_DIM = 128
CONV = 4
BLOCK = 128
LANES = 128
WIDTHS = (4 * D, D, 2 * FF, FF)
HALVES = tuple(width // 2 for width in WIDTHS)
OWN_HEADS = HEADS // 2
HALF = D // 2
W_IN, W_OUT, W_UP, W_DOWN = range(4)
GATE_ROW, GAIN_ROW, CONV_ROW, LOG_ROW, BIAS_ROW, OUT_ROW, SMALL_ROWS = 0, 128, 144, 240, 241, 242, 243

epsilon = 1e-06
highest = lax.Precision.HIGHEST
MESH = pl.DeviceIdType.MESH
f32, bf16 = jnp.float32, jnp.bfloat16

NN = ((1,), (0,))
NT = ((1,), (1,))
TN = ((0,), (0,))


def unit_table():
    units = []
    for part in range(4):
        units.append((W_IN, part * HALVES[W_OUT], HALVES[W_OUT], part % 2, part * D, D // 2))
    for part in range(2):
        width = HALVES[W_OUT] // 2
        units.append((W_OUT, part * width, width, part, part * width, D // 2))
    low = LANES * -(-FF // (4 * LANES))
    for part in range(2):
        for k, (start, width) in enumerate(((0, low), (low, FF // 2 - low))):
            units.append(
                (W_UP, part * (FF // 2) + start, width, (part + k) % 2, part * FF + start, FF // 2)
            )
    for k, (start, width) in enumerate(((0, low), (low, FF // 2 - low))):
        units.append((W_DOWN, start, width, k, start, FF // 2))
    return units


UNITS = unit_table()


def mm(left, right, dims):
    return lax.dot_general(
        left, right, (dims, ((), ())), precision=highest, preferred_element_type=f32
    )


def dot(left, right, dims=NN):
    return lax.dot_general(left, right, (dims, ((), ())), preferred_element_type=f32)


def sigmoid(x):
    return lax.logistic(x)


def softplus(x):
    return jnp.maximum(x, 0.0) + jnp.log1p(jnp.exp(-jnp.abs(x)))


def cols_at(index, width):
    return pl.ds(pl.multiple_of(index * width, width), width)


def loop(lo, hi, body):
    def step(i, carry):
        body(i)
        return carry

    lax.fori_loop(lo, hi, step, 0)


def kernel(
    dp,
    rows,
    x_in, cot, marks, sh_in, sh_out, sh_up, sh_down, gate_in, gains_in, taps_in, smalls_in,
    layer_out, in_grad, g_in, g_out, g_up, g_down, small_out,
    w_in, w_out, w_up, w_down,
    l_in, l_out, l_up, l_down,
    r_in, r_out, r_up, r_down,
    proj, tot, qkv, upg, delta_o, t_inv, pseudo,
    mids, xs, big_x, dmid, big_a, normed,
    gp, cum, cum_t, beta, mask, same, dcol, drow, dbeta,
    gate_w, gains, taps, smalls,
    swap_out, swap_in, small_sum, small_mate, small_land,
    own_sem, own_send, ring_recv, ring_send, sib_recv, sib_send, pair_recv, pair_send,
    swap_recv, swap_send, ready_sem, small_sem, param_recv, param_send, last_recv, last_send, mate_sem,
):
    chips = dp // 2
    half = chips // 2
    sec, me = lax.axis_index("section"), lax.axis_index("dp")
    chip, core = lax.div(me, 2), lax.rem(me, 2)
    shards = (sh_in, sh_out, sh_up, sh_down)
    held = (w_in, w_out, w_up, w_down)
    left = (l_in, l_out, l_up, l_down)
    right = (r_in, r_out, r_up, r_down)
    grads = (g_in, g_out, g_up, g_down)
    mate = {"section": 1 - sec}

    turn = lax.rem(chip, 2)
    spot = (1 - turn) * lax.div(chip, 2) + turn * (chips - 1 - lax.div(chip, 2))

    def device_at(position):
        back = lax.div(position, half)
        there = (1 - back) * 2 * position + back * (2 * (chips - 1 - position) + 1)
        return 2 * there + core

    towards = (
        device_at(lax.rem(spot + 1, chips)),
        device_at(lax.rem(spot + chips - 1, chips)),
    )
    sibling = 2 * chip + 1 - core

    def rows_of(device):
        return pl.ds(pl.multiple_of(device * rows, rows), rows)

    def remote(source, target, sent, arrival, device):
        return pltpu.make_async_remote_copy(
            src_ref=source,
            dst_ref=target,
            send_sem=sent,
            recv_sem=arrival,
            device_id=device,
            device_id_type=MESH,
        )

    def whole_cols(unit, section):
        _, _, width, _, base, span = UNITS[unit]
        return pl.ds(pl.multiple_of(base + section * span, LANES), width)

    barrier = pltpu.get_barrier_semaphore()

    def greet(offset):
        pl.semaphore_signal(
            barrier, inc=1, device_id={"dp": lax.rem(me + offset, dp)}, device_id_type=MESH
        )

    loop(1, dp, greet)
    pl.semaphore_signal(barrier, inc=1, device_id=mate, device_id_type=MESH)
    pl.semaphore_wait(barrier, dp)

    def own_part(layer, unit):
        matrix, start, width = UNITS[unit][:3]
        return held[matrix].at[layer, rows_of(me), pl.ds(start, width)]

    def place(layer, matrices):
        @pl.when(sec == layer)
        def _():
            for unit, entry in enumerate(UNITS):
                matrix = entry[0]
                if matrix not in matrices:
                    continue
                remote(
                    shards[matrix].at[:, whole_cols(unit, 1 - layer)],
                    own_part(layer, unit),
                    own_send.at[matrix],
                    own_sem.at[layer, unit],
                    mate,
                ).start()
                pltpu.make_async_copy(
                    shards[matrix].at[:, whole_cols(unit, layer)],
                    own_part(layer, unit),
                    own_sem.at[layer, unit],
                ).start()

    MIX, FFN = (W_IN, W_OUT), (W_UP, W_DOWN)
    stages = ((0, MIX), (0, FFN), (1, MIX), (1, FFN))
    place(*stages[0])

    small_inputs = ((gate_in, gate_w), (gains_in, gains), (taps_in, taps), (smalls_in, smalls))

    def param_copy(index):
        source, target = small_inputs[index]
        lines = pl.ds(0, source.shape[0])
        return remote(
            source, target.at[sec, lines], param_send.at[index], param_recv.at[index], mate
        )

    for index, (source, target) in enumerate(small_inputs):
        param_copy(index).start()
        target[sec, 0 : source.shape[0], :] = source[...]
    for layer in range(2):
        gate_w[layer, 2 * HEADS :, :] = jnp.zeros((LANES - 2 * HEADS, D), bf16)

    def ring_copy(layer, unit, source, target, step):
        matrix, way = UNITS[unit][0], UNITS[unit][3]
        return remote(
            source, target, ring_send.at[layer, matrix], ring_recv.at[layer, unit, step], {"dp": towards[way]}
        )

    def to_sibling(layer, matrix, source, target):
        return remote(
            source, target, sib_send.at[layer, matrix], sib_recv.at[layer, matrix], {"dp": sibling}
        )

    def origin(way, step):
        if way == 0:
            return lax.rem(spot + 2 * chips - 1 - step, chips)
        return lax.rem(spot + 1 + step, chips)

    def units_of(matrices):
        return [(unit, *entry[:4]) for unit, entry in enumerate(UNITS) if entry[0] in matrices]

    def send_own(layer, matrices):
        for unit, matrix, start, width, way in units_of(matrices):
            block = own_part(layer, unit)
            pltpu.make_async_copy(block, block, own_sem.at[layer, unit]).wait()
            ring_copy(layer, unit, block, block, 0).start()
            to_sibling(layer, matrix, block, block).start()

    def gather_step(layer, matrices, step, last=False, only=None):
        for unit, matrix, start, width, way in units_of(matrices)[slice(only, None if only is None else only + 1)]:
            device = device_at(origin(way, step))
            block = held[matrix].at[layer, rows_of(device), pl.ds(start, width)]
            ring_copy(layer, unit, block, block, step).wait_recv()
            if not last:
                ring_copy(layer, unit, block, block, step + 1).start()
            to_sibling(layer, matrix, block, block).start()

    def gather_rest(layer, matrices, lo, hi):
        if lo < hi:
            loop(lo, hi, lambda step: gather_step(layer, matrices, step))

    def gather_end(layer, matrices):
        for matrix in matrices:
            every = held[matrix].at[layer, pl.ds(0, chips * rows), :]
            to_sibling(layer, matrix, every, every).wait_recv()

    def gather_sent(layer, matrix):
        every = held[matrix].at[layer, pl.ds(0, chips * rows), :]
        to_sibling(layer, matrix, every, every).wait_send()
        ring_sent(layer, matrix)

    def ring_sent(layer, matrix):
        most = held[matrix].at[layer, pl.ds(0, (chips - 1) * rows), :]
        remote(
            most, most, ring_send.at[layer, matrix], ring_recv.at[layer, 0, 0], {"dp": towards[0]}
        ).wait_send()

    final = chips - 2

    fed = [0, 0, 0]

    def next_stage(stage):
        if stage + 1 < len(stages):
            send_own(*stages[stage + 1])
        if stage + 2 < len(stages):
            place(*stages[stage + 2])

    def feed(count):
        for _ in range(count):
            stage, step, part = fed
            if stage == len(stages):
                return
            layer, matrices = stages[stage]
            if step == final - 1 and part == 0:
                next_stage(stage)
            gather_step(layer, matrices, step, step == final, part)
            part += 1
            if part == len(units_of(matrices)):
                step, part = step + 1, 0
            if step > final:
                stage, step = stage + 1, 0
            fed[:] = [stage, step, part]

    def feed_all(stage):
        while fed[0] <= stage and fed[0] < len(stages):
            if fed[2] == 0 and fed[1] < final - 1:
                gather_rest(*stages[fed[0]], fed[1], final - 1)
                fed[1] = final - 1
            else:
                feed(1)

    send_own(*stages[0])
    place(*stages[1])

    row = lax.broadcasted_iota(jnp.int32, (BLOCK, BLOCK), 0)
    col = lax.broadcasted_iota(jnp.int32, (BLOCK, BLOCK), 1)
    starts = jnp.logical_or(marks[...] > 0, col[:1] == 0)
    starts = jnp.where(starts, 1.0, 0.0)
    seg_col = jnp.sum(jnp.where(row >= col, starts, 0.0), axis=1, keepdims=True)
    seg_row = jnp.sum(jnp.where(row == col, seg_col, 0.0), axis=0, keepdims=True)
    within = jnp.where(jnp.logical_and(seg_col == seg_row, row >= col), 1.0, 0.0)
    mask[...] = within
    for m in range(1, CONV):
        near = jnp.sum(jnp.where(row - col == m, within, 0.0), axis=1, keepdims=True)
        same[m - 1] = jnp.broadcast_to(near, (BLOCK, LANES))
    small_sum[...] = jnp.zeros(small_sum.shape, f32)

    dmid[...] = cot[...]
    feed(len(units_of(MIX)))

    swaps = [0]
    OUTPUT_SLOT = 2

    def swap_slot():
        swaps[0] += 1
        return swaps[0] % 2

    def swapping(slot, width):
        part = pl.ds(0, width)
        return remote(
            swap_out.at[slot, :, part], swap_in.at[slot, :, part],
            swap_send.at[slot], swap_recv.at[slot], mate,
        )

    def swap_begin(slot, width):
        swapping(slot, width).start()

    def swap_end(slot, width):
        swapping(slot, width).wait()

    def left_copy(layer, matrix):
        array = left[matrix]
        return remote(
            array.at[layer, :, pl.ds(0, BLOCK)], array.at[layer, :, pl.ds(BLOCK, BLOCK)],
            pair_send.at[layer, matrix], pair_recv.at[layer, matrix], {"dp": sibling},
        )

    def right_copy(layer, matrix):
        array = right[matrix]
        return remote(
            array.at[layer, pl.ds(0, BLOCK), :], array.at[layer, pl.ds(BLOCK, BLOCK), :],
            pair_send.at[layer, 4 + matrix], pair_recv.at[layer, 4 + matrix], {"dp": sibling},
        )

    own_half = pl.ds(pl.multiple_of(sec * HALF, HALF), HALF)
    other_half = pl.ds(pl.multiple_of((1 - sec) * HALF, HALF), HALF)
    mine = pl.ds(0, BLOCK)

    def lane_of(array, lane):
        return jnp.sum(jnp.where(col == lane, array, 0.0), axis=1, keepdims=True)

    def row_of(array, which):
        return jnp.sum(jnp.where(row == which, array, 0.0), axis=0, keepdims=True)

    def part_at(part, i):
        return cols_at(part * OWN_HEADS + i, HEAD_DIM)

    def tap_cols(part, i):
        return cols_at(part * HEADS + sec * OWN_HEADS + i, HEAD_DIM)

    def turn_over(source, layer, turned):
        def part(i):
            at = cols_at(i, 128)
            turned[layer, at, mine] = source[:, at].astype(f32).T.astype(bf16)

        loop(0, D // 128, part)

    def rms(source, layer, gain_row, turned):
        def part(i):
            at = cols_at(i, 32)
            x = source[at, :]
            scale = lax.rsqrt(jnp.mean(x * x, axis=1, keepdims=True) + epsilon)
            normed[at, :] = (x * scale * gains[layer, gain_row : gain_row + 1, :]).astype(bf16)

        loop(0, BLOCK // 32, part)
        turn_over(normed, layer, turned)

    def spread(layer, i):
        h = sec * OWN_HEADS + i
        gap = lane_of(cum[layer], h) - row_of(cum_t[layer], h)
        return jnp.where(mask[...] > 0.0, jnp.exp(jnp.minimum(gap, 0.0)), 0.0)

    apart = jnp.bitwise_xor(row, col)

    def delta_forward(layer, pause):
        span = range(OWN_HEADS)
        weights = [spread(layer, i) for i in span]
        betas = [lane_of(beta[layer], HEADS + sec * OWN_HEADS + i) for i in span]
        keys = [qkv[layer, :, part_at(1, i)] for i in span]
        below = [
            jnp.where(row > col, weights[i], 0.0) * mm(keys[i], keys[i], NT) * betas[i]
            for i in span
        ]
        inverse = [jnp.where(row == col, 1.0, 0.0) - jnp.where(apart == 1, below[i], 0.0) for i in span]
        size = 2
        while size < BLOCK:
            level = jnp.logical_and(apart >= size, apart < 2 * size)
            inner = [mm(jnp.where(level, below[i], 0.0), inverse[i], NN) for i in span]
            inverse = [inverse[i] - mm(inverse[i], inner[i], NN) for i in span]
            if size in (4, 16, 64):
                pause()
            size *= 2
        solved = [mm(inverse[i], betas[i] * qkv[layer, :, part_at(2, i)], NN) for i in span]
        for i in span:
            at = part_at(0, i)
            score = mm(qkv[layer, :, at], keys[i], NT) * weights[i]
            delta_o[layer, :, at] = mm(score, solved[i], NN)
            t_inv[layer, :, at] = inverse[i]
            pseudo[layer, :, at] = solved[i]

    def forward(layer, source):
        stage = 2 * layer + 1
        rms(source, layer, 0, l_in)
        feed_all(stage - 1)
        gather_end(layer, MIX)

        def project(j):
            at = cols_at(j, 512)
            proj[layer, :, at] = dot(normed[...], w_in[layer, :, at])

        loop(0, HALVES[W_IN] // 512, project)
        feed(4)
        pre = dot(normed[...], gate_w[layer], NT)
        gp[layer] = pre
        beta[layer] = sigmoid(pre)
        decay = -jnp.exp(smalls[layer, 0:1, :]) * softplus(pre + smalls[layer, 1:2, :])
        running = mm(jnp.where(row >= col, 1.0, 0.0), decay, NN)
        cum[layer] = running
        cum_t[layer] = running.T
        left_copy(layer, W_IN).start()
        feed(4)

        def head_parts(i):
            for part in range(3):
                at, tap = part_at(part, i), tap_cols(part, i)
                x = proj[layer, :, at]
                total = x * taps[layer, CONV - 1 : CONV, tap]
                for m in range(1, CONV):
                    total += pltpu.roll(x, m, 0) * same[m - 1] * taps[layer, CONV - 1 - m : CONV - m, tap]
                tot[layer, :, at] = total
                value = total * sigmoid(total)
                if part < 2:
                    value = value * lax.rsqrt(jnp.sum(value * value, axis=1, keepdims=True) + epsilon)
                if part == 0:
                    value = value * HEAD_DIM ** (-0.5)
                qkv[layer, :, at] = value

        loop(0, OWN_HEADS // 2, head_parts)
        feed(4)
        loop(OWN_HEADS // 2, OWN_HEADS, head_parts)
        feed(4)
        delta_forward(layer, lambda: feed(4))
        feed(4)
        slot = swap_slot()

        def gate_norm(i):
            at = part_at(0, i)
            out = delta_o[layer, :, at]
            scale = lax.rsqrt(jnp.mean(out * out, axis=1, keepdims=True) + epsilon)
            gate = proj[layer, :, part_at(3, i)]
            mixed = out * scale * smalls[layer, 2:3, :] * (gate * sigmoid(gate))
            swap_out[slot, :, at] = mixed.astype(bf16)

        loop(0, OWN_HEADS, gate_norm)
        swap_begin(slot, HALF)
        normed[:, own_half] = swap_out[slot, :, pl.ds(0, HALF)]
        feed(6)
        swap_end(slot, HALF)
        normed[:, other_half] = swap_in[slot, :, pl.ds(0, HALF)]
        total = dot(normed[...], w_out[layer])
        slot = swap_slot()
        swap_out[slot, :, pl.ds(0, HALF)] = total.astype(bf16)
        swap_begin(slot, HALF)
        mids[layer, :, own_half] = source[:, own_half] + total
        turn_over(normed, layer, l_out)
        left_copy(layer, W_OUT).start()
        feed(6)
        swap_end(slot, HALF)
        mids[layer, :, other_half] = source[:, other_half] + swap_in[slot, :, pl.ds(0, HALF)].astype(f32)
        rms(mids.at[layer], layer, 1, l_up)
        left_copy(layer, W_UP).start()
        feed_all(stage)
        gather_end(layer, FFN)

        def up_part(j):
            at = cols_at(j, 256)
            upg[layer, :, at] = dot(normed[...], w_up[layer, :, at])

        middle = FF // 256 // 2
        loop(0, middle, up_part)
        feed(4)
        loop(middle, FF // 256, up_part)
        feed(4)

        def hidden_part(j):
            at = cols_at(j, LANES)
            first, second = upg[layer, :, at], upg[layer, :, cols_at(j + FF // 2 // LANES, LANES)]
            r_down[layer, mine, at] = (first * sigmoid(first) * second).astype(bf16)

        loop(0, FF // 2 // LANES, hidden_part)
        right_copy(layer, W_DOWN).start()
        feed(4)
        slot = OUTPUT_SLOT

        def down_part(j):
            at = cols_at(j, 256)
            part = dot(r_down[layer, mine, :], w_down[layer, at, :], NT)
            xs[:, at] = mids[layer, :, at] + part
            swap_out[slot, :, at] = part.astype(bf16)

        loop(0, D // 256, down_part)
        swap_begin(slot, D)
        feed(8)

        def finish():
            swap_end(slot, D)
            xs[...] += swap_in[slot].astype(f32)

            @pl.when(sec == layer)
            def _():
                layer_out[...] = xs[...]

        return finish

    def ready(group):
        for device in ({"dp": towards[0]}, {"dp": towards[1]}, mate):
            pl.semaphore_signal(ready_sem.at[group], inc=1, device_id=device, device_id_type=MESH)

    def slot_rows(index):
        return pl.ds(pl.multiple_of(index * rows, rows), rows)

    def sum_step(layer, matrices, step, place, only=None):
        for unit, matrix, start, width, way in units_of(matrices)[slice(only, None if only is None else only + 1)]:
            part = pl.ds(start, width)
            owner = device_at(origin(way, step))
            own = dot(left[matrix][layer, rows_of(owner), :], right[matrix][layer, :, part])
            before = slot_rows(chips - 1 if place == 0 else step - 1)
            here = held[matrix].at[layer, before, part]
            if place > 0:
                ring_copy(layer, unit, here, here, step - 1).wait_recv()
                own = own + held[matrix][layer, before, part].astype(f32)
            if place < 2:
                held[matrix][layer, before, part] = own.astype(bf16)
                ring_copy(
                    layer, unit, here, held[matrix].at[layer, slot_rows(step), part], step
                ).start()
            else:

                @pl.when(sec == layer)
                def _():
                    grads[matrix][:, whole_cols(unit, layer)] = own

                @pl.when(sec != layer)
                def _():
                    held[matrix][layer, slot_rows(chips), part] = own.astype(bf16)
                    last = held[matrix].at[layer, slot_rows(chips), part]
                    remote(last, last, last_send.at[matrix], last_recv.at[unit], mate).start()

    sums = ((1, FFN), (1, MIX), (0, FFN), (0, MIX))

    added = [0, 0, 0]

    def add_begin(group):
        layer, matrices = sums[group]
        for matrix in matrices:
            left_copy(layer, matrix).wait_recv()
            right_copy(layer, matrix).wait_recv()
        pl.semaphore_wait(ready_sem.at[group], 3)

    def add_up(count, upto):
        for _ in range(count):
            group, step, part = added
            if group >= upto:
                return
            layer, matrices = sums[group]
            if step == 0 and part == 0:
                add_begin(group)
            sum_step(layer, matrices, step, 0 if step == 0 else 1 if step < chips - 1 else 2, part)
            part += 1
            if part == len(units_of(matrices)):
                step, part = step + 1, 0
            if step == chips:
                group, step = group + 1, 0
            added[:] = [group, step, part]

    def add_all(upto):
        while added[0] < upto:
            if added[2] == 0 and 0 < added[1] < chips - 1:
                layer, matrices = sums[added[0]]
                loop(added[1], chips - 1, lambda step: sum_step(layer, matrices, step, 1))
                added[1] = chips - 1
            else:
                add_up(1, upto)

    def rms_back(source, layer, gain_row, rest, target, slot):
        gain = gains[layer, gain_row : gain_row + 1, :]

        def part(i, total):
            at = cols_at(i, 32)
            x, dy = source[at, :], big_a[at, :] + swap_in[slot, at, :].astype(f32)
            scale = lax.rsqrt(jnp.mean(x * x, axis=1, keepdims=True) + epsilon)
            unit = x * scale
            dyg = dy * gain
            dx = scale * (dyg - unit * jnp.mean(dyg * unit, axis=1, keepdims=True))
            target[at, :] = dx + rest[at, :]
            return total + jnp.sum(dy * unit, axis=0, keepdims=True)

        total = lax.fori_loop(0, BLOCK // 32, part, jnp.zeros((1, D), f32))

        @pl.when(sec == layer)
        def _():
            for j in range(D // LANES):
                line = GAIN_ROW + gain_row * (D // LANES) + j
                small_sum[layer, line : line + 1, :] = total[:, j * LANES : (j + 1) * LANES]

    strict = row > col

    def backward(layer, source, before, meanwhile):
        group = before + 1
        normed[...] = dmid[...].astype(bf16)
        add_up(4, group)

        def hidden_back(j):
            at = cols_at(j, LANES)
            other = cols_at(j + FF // 2 // LANES, LANES)
            d_hidden = dot(normed[...], w_down[layer, :, at])
            first, second = upg[layer, :, at], upg[layer, :, other]
            gate = sigmoid(first)
            r_up[layer, mine, at] = (
                d_hidden * second * gate * (1.0 + first * (1.0 - gate))
            ).astype(bf16)
            r_up[layer, mine, other] = (d_hidden * (first * gate)).astype(bf16)

        loop(0, FF // 2 // LANES, hidden_back)
        right_copy(layer, W_UP).start()
        add_up(4, group)
        slot = swap_slot()

        def up_back(j):
            at = cols_at(j, 256)
            part = dot(r_up[layer, mine, :], w_up[layer, at, :], NT)
            big_a[:, at] = part
            swap_out[slot, :, at] = part.astype(bf16)

        loop(0, D // 256, up_back)
        swap_begin(slot, D)
        ready(group)
        add_all(group)
        add_up(8, group + 1)
        meanwhile()
        swap_end(slot, D)
        rms_back(mids.at[layer], layer, 1, dmid, dmid, slot)
        r_out[layer, mine, :] = dmid[:, own_half].astype(bf16)
        right_copy(layer, W_OUT).start()
        slot = swap_slot()

        def mixer_back(j):
            at = cols_at(j, 256)
            theirs = pl.ds(pl.multiple_of((1 - sec) * HALF + j * 256, 256), 256)
            swap_out[slot, :, at] = dot(r_out[layer, mine, :], w_out[layer, theirs, :], NT).astype(bf16)

        loop(0, HALF // 256, mixer_back)
        swap_begin(slot, HALF)

        def mixer_own(j):
            at = cols_at(j, 256)
            ours = pl.ds(pl.multiple_of(sec * HALF + j * 256, 256), 256)
            big_a[:, at] = dot(r_out[layer, mine, :], w_out[layer, ours, :], NT)

        loop(0, HALF // 256, mixer_own)
        add_up(6, group + 1)
        swap_end(slot, HALF)

        def gate_norm_back(i):
            at = part_at(0, i)
            out = delta_o[layer, :, at]
            scale = lax.rsqrt(jnp.mean(out * out, axis=1, keepdims=True) + epsilon)
            unit = out * scale
            gate = proj[layer, :, part_at(3, i)]
            passed = sigmoid(gate)
            d_mixed = big_a[:, at] + swap_in[slot, :, at].astype(f32)
            gain = smalls[layer, 2:3, :]
            d_gate = d_mixed * unit * gain * (passed * (1.0 + gate * (1.0 - passed)))
            r_in[layer, mine, part_at(3, i)] = d_gate.astype(bf16)
            d_scaled = d_mixed * (gate * passed)
            small_sum[layer, OUT_ROW : OUT_ROW + 1, :] += jnp.sum(d_scaled * unit, axis=0, keepdims=True)
            d_unit = d_scaled * gain
            delta_o[layer, :, at] = scale * (d_unit - unit * jnp.mean(d_unit * unit, axis=1, keepdims=True))

        loop(0, OWN_HEADS, gate_norm_back)
        add_up(4, group + 1)

        dcol[...] = jnp.zeros(dcol.shape, f32)
        drow[...] = jnp.zeros(drow.shape, f32)
        dbeta[...] = jnp.zeros(dbeta.shape, f32)

        def norm_silu_back(part, i, d_value):
            at = part_at(part, i)
            total = tot[layer, :, at]
            passed = sigmoid(total)
            if part < 2:
                raw = total * passed
                scale = lax.rsqrt(jnp.sum(raw * raw, axis=1, keepdims=True) + epsilon)
                unit = raw * scale
                if part == 0:
                    d_value = d_value * HEAD_DIM ** (-0.5)
                d_value = scale * (d_value - unit * jnp.sum(d_value * unit, axis=1, keepdims=True))
            tot[layer, :, at] = d_value * (passed * (1.0 + total * (1.0 - passed)))

        def delta_backward(i):
            h = sec * OWN_HEADS + i
            at = part_at(0, i)
            weights = spread(layer, i)
            query, key, value = [qkv[layer, :, part_at(part, i)] for part in range(3)]
            write = lane_of(beta[layer], HEADS + h)
            solved, d_out = pseudo[layer, :, at], delta_o[layer, :, at]
            key_key = mm(key, key, NT)
            query_key = mm(query, key, NT)
            d_score = mm(d_out, solved, NT)
            d_pseudo = mm(query_key * weights, d_out, TN)
            d_right = mm(t_inv[layer, :, at], d_pseudo, TN)
            d_left = jnp.where(strict, -mm(d_right, solved, NT), 0.0)
            left_key = d_left * weights
            d_write = jnp.sum(d_right * value, axis=1, keepdims=True) + jnp.sum(
                left_key * key_key, axis=1, keepdims=True
            )
            d_query_key = d_score * weights
            d_key_key = left_key * write
            norm_silu_back(0, i, mm(d_query_key, key, NN))
            norm_silu_back(
                1, i, mm(d_query_key, query, TN) + mm(d_key_key, key, NN) + mm(d_key_key, key, TN)
            )
            norm_silu_back(2, i, write * d_right)
            d_gap = d_query_key * query_key + d_key_key * key_key
            dcol[...] += jnp.where(col == h, jnp.sum(d_gap, axis=1, keepdims=True), 0.0)
            drow[...] += jnp.where(row == h, jnp.sum(d_gap, axis=0, keepdims=True), 0.0)
            dbeta[...] += jnp.where(col == HEADS + h, d_write, 0.0)

        for i in range(OWN_HEADS):
            delta_backward(i)
            add_up(4, group + 1)

        def conv_back(i):
            for part in range(3):
                at, tap = part_at(part, i), tap_cols(part, i)
                d_total, x = tot[layer, :, at], proj[layer, :, at]
                d_proj = d_total * taps[layer, CONV - 1 : CONV, tap]
                line = CONV_ROW + part * HEADS + sec * OWN_HEADS + i
                tiles = 3 * D // LANES
                small_sum[layer, pl.ds(line + (CONV - 1) * tiles, 1), :] = jnp.sum(
                    d_total * x, axis=0, keepdims=True
                )
                for m in range(1, CONV):
                    met = d_total * same[m - 1]
                    weight = taps[layer, CONV - 1 - m : CONV - m, tap]
                    d_proj += pltpu.roll(met * weight, BLOCK - m, 0)
                    small_sum[layer, pl.ds(line + (CONV - 1 - m) * tiles, 1), :] = jnp.sum(
                        met * pltpu.roll(x, m, 0), axis=0, keepdims=True
                    )
                r_in[layer, mine, at] = d_proj.astype(bf16)

        loop(0, OWN_HEADS, conv_back)
        right_copy(layer, W_IN).start()
        add_up(4, group + 1)

        d_running = dcol[...] - drow[...].T
        d_decay = mm(jnp.where(row <= col, 1.0, 0.0), d_running, NN)
        pre = gp[layer] + smalls[layer, 1:2, :]
        rate = -jnp.exp(smalls[layer, 0:1, :])
        is_decay = col < HEADS
        d_pre = jnp.where(is_decay, d_decay * rate * sigmoid(pre), 0.0)
        small_sum[layer, LOG_ROW : LOG_ROW + 1, :] = jnp.sum(
            jnp.where(is_decay, d_decay * rate * softplus(pre), 0.0), axis=0, keepdims=True
        )
        small_sum[layer, BIAS_ROW : BIAS_ROW + 1, :] = jnp.sum(d_pre, axis=0, keepdims=True)
        d_gate_pre = (d_pre + dbeta[...] * beta[layer] * (1.0 - beta[layer])).astype(bf16)
        gate_grad = dot(l_in[layer, :, mine], d_gate_pre).T
        for j in range(D // LANES):
            line = GATE_ROW + j * 2 * HEADS
            small_sum[layer, line : line + 2 * HEADS, :] = gate_grad[
                : 2 * HEADS, j * LANES : (j + 1) * LANES
            ]
        slot = swap_slot()

        def in_back(j):
            at = cols_at(j, 256)
            part = dot(r_in[layer, mine, :], w_in[layer, at, :], NT) + dot(
                d_gate_pre, gate_w[layer, :, at]
            )
            big_a[:, at] = part
            swap_out[slot, :, at] = part.astype(bf16)

        loop(0, D // 256, in_back)
        swap_begin(slot, D)
        ready(group + 1)
        add_all(group + 1)
        add_up(6, group + 2)
        swap_end(slot, D)
        rms_back(source, layer, 0, dmid, dmid, slot)

        @pl.when(sec == layer)
        def _():
            in_grad[...] = dmid[...]

        add_up(4, group + 2)
        return group + 1

    turn_over(dmid, 1, l_down)
    left_copy(1, W_DOWN).start()
    feed_all(0)
    for index in range(len(small_inputs)):
        param_copy(index).wait()
    forward(0, x_in)()
    feed(6)
    big_x[...] = xs[...]
    finish = forward(1, big_x)
    for layer in range(2):
        for matrix in range(4):
            gather_sent(layer, matrix)
    done = backward(1, big_x, -1, finish)
    turn_over(dmid, 0, l_down)
    left_copy(0, W_DOWN).start()
    done = backward(0, x_in, done, lambda: None)

    piece = small_land.shape[1]

    def piece_rows(device):
        return pl.ds(pl.multiple_of(device * piece, piece), piece)

    def small_copy(stage, device, source, target):
        return remote(
            source, target, small_sem.at[stage, 0], small_sem.at[stage, 1], {"dp": device}
        )

    def scatter_small(offset):
        device = lax.rem(me + offset, dp)
        small_copy(0, device, small_mate.at[piece_rows(device), :], small_land.at[me]).start()

    def spread_small(offset):
        device = lax.rem(me + offset, dp)
        small_copy(
            1, device, small_out.at[piece_rows(me), :], small_out.at[piece_rows(me), :]
        ).start()

    to_mate = remote(small_sum.at[1 - sec], small_mate, mate_sem.at[0], mate_sem.at[1], mate)
    to_mate.start()
    add_up(6, done + 1)
    to_mate.wait()
    small_mate[...] += small_sum[sec]
    loop(1, dp, scatter_small)
    add_up(12, done + 1)
    small_land[me] = small_mate[piece_rows(me), :]
    others = small_land.at[pl.ds(0, dp - 1)]
    small_copy(0, sibling, others, others).wait_recv()
    small_out[piece_rows(me), :] = jnp.sum(small_land[...], axis=0)
    loop(1, dp, spread_small)
    add_all(done + 1)

    for unit, (matrix, start, width, _, _, _) in enumerate(UNITS):
        part = pl.ds(start, width)

        @pl.when(sec == 0)
        def _(unit=unit, matrix=matrix, part=part):
            last = held[matrix].at[0, slot_rows(chips), part]
            remote(last, last, last_send.at[matrix], last_recv.at[unit], mate).wait_recv()
            grads[matrix][:, whole_cols(unit, 1)] = held[matrix][0, slot_rows(chips), part].astype(f32)

        @pl.when(sec != 0)
        def _(unit=unit, matrix=matrix, part=part):
            last = held[matrix].at[1, slot_rows(chips), part]
            remote(last, last, last_send.at[matrix], last_recv.at[unit], mate).wait_recv()
            grads[matrix][:, whole_cols(unit, 0)] = held[matrix][1, slot_rows(chips), part].astype(f32)

    small_copy(0, sibling, others, others).wait_send()
    spans = small_out.at[pl.ds(0, (dp - 1) * piece), :]
    small_copy(1, sibling, spans, spans).wait()
    for matrix in range(4):
        own = held[matrix].at[0, pl.ds(0, rows), :]
        remote(own, own, own_send.at[matrix], last_recv.at[0], mate).wait_send()
        remote(own, own, last_send.at[matrix], last_recv.at[0], mate).wait_send()
        for layer in range(2):
            ring_sent(layer, matrix)
            left_copy(layer, matrix).wait_send()
            right_copy(layer, matrix).wait_send()


def closing_kernel(*refs):
    bigs, small, outs, places, sem = refs[:6], refs[6], refs[7:13], refs[13:19], refs[19]
    copies = [
        pltpu.make_async_copy(big, out.at[0], sem.at[i]) for i, (big, out) in enumerate(zip(bigs, outs))
    ]
    for copy in copies:
        copy.start()
    gate, gains, taps, log, bias, out_gain = places
    turned = small[GATE_ROW : GATE_ROW + D // LANES * 2 * HEADS, :].T
    for j in range(D // LANES):
        at = slice(j * LANES, (j + 1) * LANES)
        gate[0, at, :] = turned[:, j * 2 * HEADS : (j + 1) * 2 * HEADS]
        for k in range(2):
            line = GAIN_ROW + k * (D // LANES) + j
            gains[0, k : k + 1, at] = small[line : line + 1, :]
    for j in range(3 * D // LANES):
        at = slice(j * LANES, (j + 1) * LANES)
        for k in range(CONV):
            line = CONV_ROW + k * (3 * D // LANES) + j
            taps[0, k : k + 1, at] = small[line : line + 1, :]
    log[...] = small[LOG_ROW : LOG_ROW + 1, :HEADS]
    bias[...] = small[BIAS_ROW : BIAS_ROW + 1, :HEADS]
    out_gain[...] = small[OUT_ROW : OUT_ROW + 1, :]
    for copy in copies:
        copy.wait()


def padded(row):
    return jnp.pad(row, ((0, 0), (0, LANES - row.shape[1])))


def local(
    dp,
    block_input,
    cotangent,
    marks,
    w_in,
    w_out,
    w_up,
    w_down,
    gate_weights,
    norm_gains,
    conv_weights,
    decay_log,
    decay_bias,
    out_gain,
):
    rows = w_in.shape[1]
    chips = dp // 2
    smalls = jnp.concatenate(
        [padded(decay_log), padded(decay_bias), out_gain, jnp.zeros((5, LANES), f32)], axis=0
    )
    gate_w = gate_weights[0].T
    piece = 8 * -(-SMALL_ROWS // (8 * dp))
    vmem = pl.BlockSpec(memory_space=pltpu.VMEM)
    anywhere = pl.BlockSpec(memory_space=pl.ANY)

    def both(width, kind=f32, lines=BLOCK):
        return pltpu.VMEM((2, lines, width), kind)

    def wide(width, kind=f32, lines=BLOCK):
        return pltpu.VMEM((lines, width), kind)

    dma = pltpu.SemaphoreType.DMA
    scratch = (
        [both(width, bf16, D) for width in HALVES]
        + [both(2 * BLOCK, bf16, D) for _ in HALVES]
        + [both(width, bf16, 2 * BLOCK) for width in HALVES]
        + [both(2 * D), both(3 * HALF), both(3 * HALF), both(FF), both(HALF), both(HALF), both(HALF)]
        + [both(D), wide(D), wide(D), wide(D), wide(D), wide(D, bf16)]
        + [both(LANES)] * 4
        + [wide(LANES), pltpu.VMEM((CONV - 1, BLOCK, LANES), f32)]
        + [wide(LANES)] * 3
        + [both(D, bf16, LANES), both(D, f32, 2), both(3 * D, f32, CONV), both(LANES, f32, 8)]
        + [pltpu.VMEM((3, BLOCK, D), bf16)] * 2
        + [both(LANES, f32, dp * piece), wide(LANES, f32, dp * piece)]
        + [pltpu.VMEM((dp, piece, LANES), f32)]
        + [dma((2, len(UNITS))), dma((4,)), dma((2, len(UNITS), chips - 1))]
        + [dma((2, 4))] * 3
        + [dma((2, 8))] * 2
        + [dma((3,))] * 2
        + [pltpu.SemaphoreType.REGULAR((4,)), dma((2, 2)), dma((4,)), dma((4,))]
        + [dma((len(UNITS),)), dma((4,)), dma((2,))]
    )
    *bigs, small = pl.pallas_call(
        functools.partial(kernel, dp, rows),
        out_shape=[jax.ShapeDtypeStruct((BLOCK, D), f32)] * 2
        + [jax.ShapeDtypeStruct((rows, width), f32) for width in WIDTHS]
        + [jax.ShapeDtypeStruct((dp * piece, LANES), f32)],
        in_specs=[vmem] * 3 + [anywhere] * 4 + [vmem] * 4,
        out_specs=[vmem] * 7,
        scratch_shapes=scratch,
        compiler_params=pltpu.CompilerParams(
            collective_id=0, has_side_effects=True, vmem_limit_bytes=63 * 2**20
        ),
        cost_estimate=pl.CostEstimate(
            flops=6 * BLOCK * D * sum(WIDTHS), bytes_accessed=8 * rows * sum(WIDTHS), transcendentals=0
        ),
    )(
        block_input, cotangent, marks[None, :], w_in[0], w_out[0], w_up[0], w_down[0],
        gate_w, norm_gains[0], conv_weights[0], smalls,
    )
    shapes = [(1, *big.shape) for big in bigs]
    shapes += [(1, D, 2 * HEADS), (1, 2, D), (1, CONV, 3 * D), (1, HEADS), (1, HEADS), (1, LANES)]
    return tuple(
        pl.pallas_call(
            closing_kernel,
            out_shape=[jax.ShapeDtypeStruct(shape, f32) for shape in shapes],
            in_specs=[anywhere] * 6 + [vmem],
            out_specs=[vmem] * 12,
            scratch_shapes=[dma((6,))],
            compiler_params=pltpu.CompilerParams(vmem_limit_bytes=60 * 2**20),
        )(*bigs, small)
    )


def solution(mesh):
    sharded, whole, flat = P("section", "dp", None), P("section", None, None), P("section", None)
    return jax.shard_map(
        functools.partial(local, mesh.shape["dp"]),
        mesh=mesh,
        in_specs=(P("dp", None), P("dp", None), P("dp")) + (sharded,) * 4 + (whole,) * 3 + (flat,) * 3,
        out_specs=(sharded,) * 6 + (whole,) * 3 + (flat,) * 3,
        check_vma=False,
    )
```

```python
import functools

import jax
import jax.numpy as jnp
from jax import lax
from jax.experimental import pallas as pl
from jax.experimental.pallas import tpu as pltpu
from jax.sharding import PartitionSpec as P

D = 1024
FF = 2816
HEADS = 8
HEAD_DIM = 128
CONV = 4
BLOCK = 128
LANES = 128
WIDTHS = (4 * D, D, 2 * FF, FF)
HALVES = tuple(width // 2 for width in WIDTHS)
OWN_HEADS = HEADS // 2
HALF = D // 2
W_IN, W_OUT, W_UP, W_DOWN = range(4)
GATE_ROW, GAIN_ROW, CONV_ROW, LOG_ROW, BIAS_ROW, OUT_ROW, SMALL_ROWS = 0, 128, 144, 240, 241, 242, 243

epsilon = 1e-06
highest = lax.Precision.HIGHEST
MESH = pl.DeviceIdType.MESH
f32, bf16 = jnp.float32, jnp.bfloat16

NN = ((1,), (0,))
NT = ((1,), (1,))
TN = ((0,), (0,))


def unit_table():
    units = []
    for part in range(4):
        units.append((W_IN, part * HALVES[W_OUT], HALVES[W_OUT], part % 2, part * D, D // 2))
    for part in range(2):
        width = HALVES[W_OUT] // 2
        units.append((W_OUT, part * width, width, part, part * width, D // 2))
    low = LANES * -(-FF // (4 * LANES))
    for part in range(2):
        for k, (start, width) in enumerate(((0, low), (low, FF // 2 - low))):
            units.append(
                (W_UP, part * (FF // 2) + start, width, (part + k) % 2, part * FF + start, FF // 2)
            )
    for k, (start, width) in enumerate(((0, low), (low, FF // 2 - low))):
        units.append((W_DOWN, start, width, k, start, FF // 2))
    return units


UNITS = unit_table()


def mm(left, right, dims):
    return lax.dot_general(
        left, right, (dims, ((), ())), precision=highest, preferred_element_type=f32
    )


def dot(left, right, dims=NN):
    return lax.dot_general(left, right, (dims, ((), ())), preferred_element_type=f32)


def sigmoid(x):
    return lax.logistic(x)


def softplus(x):
    return jnp.maximum(x, 0.0) + jnp.log1p(jnp.exp(-jnp.abs(x)))


def cols_at(index, width):
    return pl.ds(pl.multiple_of(index * width, width), width)


def loop(lo, hi, body):
    def step(i, carry):
        body(i)
        return carry

    lax.fori_loop(lo, hi, step, 0)


def kernel(
    dp,
    rows,
    x_in, cot, marks, sh_in, sh_out, sh_up, sh_down, gate_in, gains_in, taps_in, smalls_in,
    layer_out, in_grad, g_in, g_out, g_up, g_down, small_out,
    w_in, w_out, w_up, w_down,
    l_in, l_out, l_up, l_down,
    r_in, r_out, r_up, r_down,
    proj, tot, qkv, upg, delta_o, t_inv, pseudo,
    mids, xs, big_x, dmid, big_a, normed,
    gp, cum, cum_t, beta, mask, same, dcol, drow, dbeta,
    gate_w, gains, taps, smalls,
    swap_out, swap_in, small_sum, small_mate, small_land,
    own_sem, own_send, ring_recv, ring_send, sib_recv, sib_send, pair_recv, pair_send,
    swap_recv, swap_send, ready_sem, small_sem, param_recv, param_send, last_recv, last_send, mate_sem,
):
    chips = dp // 2
    half = chips // 2
    sec, me = lax.axis_index("section"), lax.axis_index("dp")
    chip, core = lax.div(me, 2), lax.rem(me, 2)
    shards = (sh_in, sh_out, sh_up, sh_down)
    held = (w_in, w_out, w_up, w_down)
    left = (l_in, l_out, l_up, l_down)
    right = (r_in, r_out, r_up, r_down)
    grads = (g_in, g_out, g_up, g_down)
    mate = {"section": 1 - sec}

    turn = lax.rem(chip, 2)
    spot = (1 - turn) * lax.div(chip, 2) + turn * (chips - 1 - lax.div(chip, 2))

    def device_at(position):
        back = lax.div(position, half)
        there = (1 - back) * 2 * position + back * (2 * (chips - 1 - position) + 1)
        return 2 * there + core

    towards = (
        device_at(lax.rem(spot + 1, chips)),
        device_at(lax.rem(spot + chips - 1, chips)),
    )
    sibling = 2 * chip + 1 - core

    def rows_of(device):
        return pl.ds(pl.multiple_of(device * rows, rows), rows)

    def remote(source, target, sent, arrival, device):
        return pltpu.make_async_remote_copy(
            src_ref=source,
            dst_ref=target,
            send_sem=sent,
            recv_sem=arrival,
            device_id=device,
            device_id_type=MESH,
        )

    def whole_cols(unit, section):
        _, _, width, _, base, span = UNITS[unit]
        return pl.ds(pl.multiple_of(base + section * span, LANES), width)

    barrier = pltpu.get_barrier_semaphore()

    def greet(offset):
        pl.semaphore_signal(
            barrier, inc=1, device_id={"dp": lax.rem(me + offset, dp)}, device_id_type=MESH
        )

    loop(1, dp, greet)
    pl.semaphore_signal(barrier, inc=1, device_id=mate, device_id_type=MESH)
    pl.semaphore_wait(barrier, dp)

    def own_part(layer, unit):
        matrix, start, width = UNITS[unit][:3]
        return held[matrix].at[layer, rows_of(me), pl.ds(start, width)]

    def place(layer, matrices):
        @pl.when(sec == layer)
        def _():
            for unit, entry in enumerate(UNITS):
                matrix = entry[0]
                if matrix not in matrices:
                    continue
                remote(
                    shards[matrix].at[:, whole_cols(unit, 1 - layer)],
                    own_part(layer, unit),
                    own_send.at[matrix],
                    own_sem.at[layer, unit],
                    mate,
                ).start()
                pltpu.make_async_copy(
                    shards[matrix].at[:, whole_cols(unit, layer)],
                    own_part(layer, unit),
                    own_sem.at[layer, unit],
                ).start()

    MIX, FFN = (W_IN, W_OUT), (W_UP, W_DOWN)
    stages = ((0, MIX), (0, FFN), (1, MIX), (1, FFN))
    place(*stages[0])

    small_inputs = ((gate_in, gate_w), (gains_in, gains), (taps_in, taps), (smalls_in, smalls))

    def param_copy(index):
        source, target = small_inputs[index]
        lines = pl.ds(0, source.shape[0])
        return remote(
            source, target.at[sec, lines], param_send.at[index], param_recv.at[index], mate
        )

    for index, (source, target) in enumerate(small_inputs):
        param_copy(index).start()
        target[sec, 0 : source.shape[0], :] = source[...]
    for layer in range(2):
        gate_w[layer, 2 * HEADS :, :] = jnp.zeros((LANES - 2 * HEADS, D), bf16)

    def ring_copy(layer, unit, source, target, step):
        matrix, way = UNITS[unit][0], UNITS[unit][3]
        return remote(
            source, target, ring_send.at[layer, matrix], ring_recv.at[layer, unit, step], {"dp": towards[way]}
        )

    def to_sibling(layer, matrix, source, target):
        return remote(
            source, target, sib_send.at[layer, matrix], sib_recv.at[layer, matrix], {"dp": sibling}
        )

    def origin(way, step):
        if way == 0:
            return lax.rem(spot + 2 * chips - 1 - step, chips)
        return lax.rem(spot + 1 + step, chips)

    def units_of(matrices):
        return [(unit, *entry[:4]) for unit, entry in enumerate(UNITS) if entry[0] in matrices]

    def send_own(layer, matrices):
        for unit, matrix, start, width, way in units_of(matrices):
            block = own_part(layer, unit)
            pltpu.make_async_copy(block, block, own_sem.at[layer, unit]).wait()
            ring_copy(layer, unit, block, block, 0).start()
            to_sibling(layer, matrix, block, block).start()

    def gather_step(layer, matrices, step, last=False, only=None):
        for unit, matrix, start, width, way in units_of(matrices)[slice(only, None if only is None else only + 1)]:
            device = device_at(origin(way, step))
            block = held[matrix].at[layer, rows_of(device), pl.ds(start, width)]
            ring_copy(layer, unit, block, block, step).wait_recv()
            if not last:
                ring_copy(layer, unit, block, block, step + 1).start()
            to_sibling(layer, matrix, block, block).start()

    def gather_rest(layer, matrices, lo, hi):
        if lo < hi:
            loop(lo, hi, lambda step: gather_step(layer, matrices, step))

    def gather_end(layer, matrices):
        for matrix in matrices:
            every = held[matrix].at[layer, pl.ds(0, chips * rows), :]
            to_sibling(layer, matrix, every, every).wait_recv()

    def gather_sent(layer, matrix):
        every = held[matrix].at[layer, pl.ds(0, chips * rows), :]
        to_sibling(layer, matrix, every, every).wait_send()
        ring_sent(layer, matrix)

    def ring_sent(layer, matrix):
        most = held[matrix].at[layer, pl.ds(0, (chips - 1) * rows), :]
        remote(
            most, most, ring_send.at[layer, matrix], ring_recv.at[layer, 0, 0], {"dp": towards[0]}
        ).wait_send()

    final = chips - 2

    fed = [0, 0, 0]
    ahead = max(final - 3, 0)

    def next_stage(stage):
        if stage + 1 < len(stages):
            send_own(*stages[stage + 1])
        if stage + 2 < len(stages):
            place(*stages[stage + 2])

    def feed(count):
        for _ in range(count):
            stage, step, part = fed
            if stage == len(stages):
                return
            layer, matrices = stages[stage]
            if step == ahead and part == 0:
                next_stage(stage)
            gather_step(layer, matrices, step, step == final, part)
            part += 1
            if part == len(units_of(matrices)):
                step, part = step + 1, 0
            if step > final:
                stage, step = stage + 1, 0
            fed[:] = [stage, step, part]

    def feed_all(stage):
        while fed[0] <= stage and fed[0] < len(stages):
            stop = ahead if fed[1] < ahead else final
            if fed[2] == 0 and fed[1] != ahead and fed[1] < stop:
                gather_rest(*stages[fed[0]], fed[1], stop)
                fed[1] = stop
            else:
                feed(1)

    send_own(*stages[0])
    place(*stages[1])

    row = lax.broadcasted_iota(jnp.int32, (BLOCK, BLOCK), 0)
    col = lax.broadcasted_iota(jnp.int32, (BLOCK, BLOCK), 1)
    starts = jnp.logical_or(marks[...] > 0, col[:1] == 0)
    starts = jnp.where(starts, 1.0, 0.0)
    seg_col = jnp.sum(jnp.where(row >= col, starts, 0.0), axis=1, keepdims=True)
    seg_row = jnp.sum(jnp.where(row == col, seg_col, 0.0), axis=0, keepdims=True)
    within = jnp.where(jnp.logical_and(seg_col == seg_row, row >= col), 1.0, 0.0)
    mask[...] = within
    for m in range(1, CONV):
        near = jnp.sum(jnp.where(row - col == m, within, 0.0), axis=1, keepdims=True)
        same[m - 1] = jnp.broadcast_to(near, (BLOCK, LANES))
    small_sum[...] = jnp.zeros(small_sum.shape, f32)

    dmid[...] = cot[...]
    feed(len(units_of(MIX)))

    swaps = [0]
    OUTPUT_SLOT = 2

    def swap_slot():
        swaps[0] += 1
        return swaps[0] % 2

    def swapping(slot, width):
        part = pl.ds(0, width)
        return remote(
            swap_out.at[slot, :, part], swap_in.at[slot, :, part],
            swap_send.at[slot], swap_recv.at[slot], mate,
        )

    def swap_begin(slot, width):
        swapping(slot, width).start()

    def swap_end(slot, width):
        swapping(slot, width).wait()

    def left_copy(layer, matrix):
        array = left[matrix]
        return remote(
            array.at[layer, :, pl.ds(0, BLOCK)], array.at[layer, :, pl.ds(BLOCK, BLOCK)],
            pair_send.at[layer, matrix], pair_recv.at[layer, matrix], {"dp": sibling},
        )

    def right_copy(layer, matrix):
        array = right[matrix]
        return remote(
            array.at[layer, pl.ds(0, BLOCK), :], array.at[layer, pl.ds(BLOCK, BLOCK), :],
            pair_send.at[layer, 4 + matrix], pair_recv.at[layer, 4 + matrix], {"dp": sibling},
        )

    own_half = pl.ds(pl.multiple_of(sec * HALF, HALF), HALF)
    other_half = pl.ds(pl.multiple_of((1 - sec) * HALF, HALF), HALF)
    mine = pl.ds(0, BLOCK)

    def lane_of(array, lane):
        return jnp.sum(jnp.where(col == lane, array, 0.0), axis=1, keepdims=True)

    def row_of(array, which):
        return jnp.sum(jnp.where(row == which, array, 0.0), axis=0, keepdims=True)

    def part_at(part, i):
        return cols_at(part * OWN_HEADS + i, HEAD_DIM)

    def tap_cols(part, i):
        return cols_at(part * HEADS + sec * OWN_HEADS + i, HEAD_DIM)

    def turn_over(source, layer, turned):
        def part(i):
            at = cols_at(i, 128)
            turned[layer, at, mine] = source[:, at].astype(f32).T.astype(bf16)

        loop(0, D // 128, part)

    def rms(source, layer, gain_row, turned):
        def part(i):
            at = cols_at(i, 32)
            x = source[at, :]
            scale = lax.rsqrt(jnp.mean(x * x, axis=1, keepdims=True) + epsilon)
            normed[at, :] = (x * scale * gains[layer, gain_row : gain_row + 1, :]).astype(bf16)

        loop(0, BLOCK // 32, part)
        turn_over(normed, layer, turned)

    def spread(layer, i):
        h = sec * OWN_HEADS + i
        gap = lane_of(cum[layer], h) - row_of(cum_t[layer], h)
        return jnp.where(mask[...] > 0.0, jnp.exp(jnp.minimum(gap, 0.0)), 0.0)

    apart = jnp.bitwise_xor(row, col)

    def delta_forward(layer, pause):
        span = range(OWN_HEADS)
        weights = [spread(layer, i) for i in span]
        betas = [lane_of(beta[layer], HEADS + sec * OWN_HEADS + i) for i in span]
        keys = [qkv[layer, :, part_at(1, i)] for i in span]
        below = [
            jnp.where(row > col, weights[i], 0.0) * mm(keys[i], keys[i], NT) * betas[i]
            for i in span
        ]
        inverse = [jnp.where(row == col, 1.0, 0.0) - jnp.where(apart == 1, below[i], 0.0) for i in span]
        size = 2
        while size < BLOCK:
            level = jnp.logical_and(apart >= size, apart < 2 * size)
            inner = [mm(jnp.where(level, below[i], 0.0), inverse[i], NN) for i in span]
            inverse = [inverse[i] - mm(inverse[i], inner[i], NN) for i in span]
            if size in (4, 16, 64):
                pause()
            size *= 2
        solved = [mm(inverse[i], betas[i] * qkv[layer, :, part_at(2, i)], NN) for i in span]
        for i in span:
            at = part_at(0, i)
            score = mm(qkv[layer, :, at], keys[i], NT) * weights[i]
            delta_o[layer, :, at] = mm(score, solved[i], NN)
            t_inv[layer, :, at] = inverse[i]
            pseudo[layer, :, at] = solved[i]

    def forward(layer, source):
        stage = 2 * layer + 1
        rms(source, layer, 0, l_in)
        feed_all(stage - 1)
        gather_end(layer, MIX)

        def project(j):
            at = cols_at(j, 512)
            proj[layer, :, at] = dot(normed[...], w_in[layer, :, at])

        loop(0, HALVES[W_IN] // 512, project)
        feed(4)
        pre = dot(normed[...], gate_w[layer], NT)
        gp[layer] = pre
        beta[layer] = sigmoid(pre)
        decay = -jnp.exp(smalls[layer, 0:1, :]) * softplus(pre + smalls[layer, 1:2, :])
        running = mm(jnp.where(row >= col, 1.0, 0.0), decay, NN)
        cum[layer] = running
        cum_t[layer] = running.T
        left_copy(layer, W_IN).start()
        feed(4)

        def head_parts(i):
            for part in range(3):
                at, tap = part_at(part, i), tap_cols(part, i)
                x = proj[layer, :, at]
                total = x * taps[layer, CONV - 1 : CONV, tap]
                for m in range(1, CONV):
                    total += pltpu.roll(x, m, 0) * same[m - 1] * taps[layer, CONV - 1 - m : CONV - m, tap]
                tot[layer, :, at] = total
                value = total * sigmoid(total)
                if part < 2:
                    value = value * lax.rsqrt(jnp.sum(value * value, axis=1, keepdims=True) + epsilon)
                if part == 0:
                    value = value * HEAD_DIM ** (-0.5)
                qkv[layer, :, at] = value

        loop(0, OWN_HEADS // 2, head_parts)
        feed(4)
        loop(OWN_HEADS // 2, OWN_HEADS, head_parts)
        feed(4)
        delta_forward(layer, lambda: feed(4))
        feed(4)
        slot = swap_slot()

        def gate_norm(i):
            at = part_at(0, i)
            out = delta_o[layer, :, at]
            scale = lax.rsqrt(jnp.mean(out * out, axis=1, keepdims=True) + epsilon)
            gate = proj[layer, :, part_at(3, i)]
            mixed = out * scale * smalls[layer, 2:3, :] * (gate * sigmoid(gate))
            swap_out[slot, :, at] = mixed.astype(bf16)

        loop(0, OWN_HEADS, gate_norm)
        swap_begin(slot, HALF)
        normed[:, own_half] = swap_out[slot, :, pl.ds(0, HALF)]
        feed(6)
        swap_end(slot, HALF)
        normed[:, other_half] = swap_in[slot, :, pl.ds(0, HALF)]
        total = dot(normed[...], w_out[layer])
        slot = swap_slot()
        swap_out[slot, :, pl.ds(0, HALF)] = total.astype(bf16)
        swap_begin(slot, HALF)
        mids[layer, :, own_half] = source[:, own_half] + total
        turn_over(normed, layer, l_out)
        left_copy(layer, W_OUT).start()
        feed(6)
        swap_end(slot, HALF)
        mids[layer, :, other_half] = source[:, other_half] + swap_in[slot, :, pl.ds(0, HALF)].astype(f32)
        rms(mids.at[layer], layer, 1, l_up)
        left_copy(layer, W_UP).start()
        feed_all(stage)
        gather_end(layer, FFN)

        def up_part(j):
            at = cols_at(j, 256)
            upg[layer, :, at] = dot(normed[...], w_up[layer, :, at])

        middle = FF // 256 // 2
        loop(0, middle, up_part)
        feed(4)
        loop(middle, FF // 256, up_part)
        feed(4)

        def hidden_part(j):
            at = cols_at(j, LANES)
            first, second = upg[layer, :, at], upg[layer, :, cols_at(j + FF // 2 // LANES, LANES)]
            r_down[layer, mine, at] = (first * sigmoid(first) * second).astype(bf16)

        loop(0, FF // 2 // LANES, hidden_part)
        right_copy(layer, W_DOWN).start()
        feed(4)
        slot = OUTPUT_SLOT

        def down_part(j):
            at = cols_at(j, 256)
            part = dot(r_down[layer, mine, :], w_down[layer, at, :], NT)
            xs[:, at] = mids[layer, :, at] + part
            swap_out[slot, :, at] = part.astype(bf16)

        loop(0, D // 256, down_part)
        swap_begin(slot, D)
        feed(8)

        def finish():
            swap_end(slot, D)
            xs[...] += swap_in[slot].astype(f32)

            @pl.when(sec == layer)
            def _():
                layer_out[...] = xs[...]

        return finish

    def ready(group):
        for device in ({"dp": towards[0]}, {"dp": towards[1]}, mate):
            pl.semaphore_signal(ready_sem.at[group], inc=1, device_id=device, device_id_type=MESH)

    def slot_rows(index):
        return pl.ds(pl.multiple_of(index * rows, rows), rows)

    def sum_step(layer, matrices, step, place, only=None):
        for unit, matrix, start, width, way in units_of(matrices)[slice(only, None if only is None else only + 1)]:
            part = pl.ds(start, width)
            owner = device_at(origin(way, step))
            own = dot(left[matrix][layer, rows_of(owner), :], right[matrix][layer, :, part])
            before = slot_rows(chips - 1 if place == 0 else step - 1)
            here = held[matrix].at[layer, before, part]
            if place > 0:
                ring_copy(layer, unit, here, here, step - 1).wait_recv()
                own = own + held[matrix][layer, before, part].astype(f32)
            if place < 2:
                held[matrix][layer, before, part] = own.astype(bf16)
                ring_copy(
                    layer, unit, here, held[matrix].at[layer, slot_rows(step), part], step
                ).start()
            else:

                @pl.when(sec == layer)
                def _():
                    grads[matrix][:, whole_cols(unit, layer)] = own

                @pl.when(sec != layer)
                def _():
                    held[matrix][layer, slot_rows(chips), part] = own.astype(bf16)
                    last = held[matrix].at[layer, slot_rows(chips), part]
                    remote(last, last, last_send.at[matrix], last_recv.at[unit], mate).start()

    sums = ((1, FFN), (1, MIX), (0, FFN), (0, MIX))

    added = [0, 0, 0]

    def add_begin(group):
        layer, matrices = sums[group]
        for matrix in matrices:
            left_copy(layer, matrix).wait_recv()
            right_copy(layer, matrix).wait_recv()
        pl.semaphore_wait(ready_sem.at[group], 3)

    def add_up(count, upto):
        for _ in range(count):
            group, step, part = added
            if group >= upto:
                return
            layer, matrices = sums[group]
            if step == 0 and part == 0:
                add_begin(group)
            sum_step(layer, matrices, step, 0 if step == 0 else 1 if step < chips - 1 else 2, part)
            part += 1
            if part == len(units_of(matrices)):
                step, part = step + 1, 0
            if step == chips:
                group, step = group + 1, 0
            added[:] = [group, step, part]

    def add_all(upto):
        while added[0] < upto:
            if added[2] == 0 and 0 < added[1] < chips - 1:
                layer, matrices = sums[added[0]]
                loop(added[1], chips - 1, lambda step: sum_step(layer, matrices, step, 1))
                added[1] = chips - 1
            else:
                add_up(1, upto)

    def rms_back(source, layer, gain_row, rest, target, slot):
        gain = gains[layer, gain_row : gain_row + 1, :]

        def part(i, total):
            at = cols_at(i, 32)
            x, dy = source[at, :], big_a[at, :] + swap_in[slot, at, :].astype(f32)
            scale = lax.rsqrt(jnp.mean(x * x, axis=1, keepdims=True) + epsilon)
            unit = x * scale
            dyg = dy * gain
            dx = scale * (dyg - unit * jnp.mean(dyg * unit, axis=1, keepdims=True))
            target[at, :] = dx + rest[at, :]
            return total + jnp.sum(dy * unit, axis=0, keepdims=True)

        total = lax.fori_loop(0, BLOCK // 32, part, jnp.zeros((1, D), f32))

        @pl.when(sec == layer)
        def _():
            for j in range(D // LANES):
                line = GAIN_ROW + gain_row * (D // LANES) + j
                small_sum[layer, line : line + 1, :] = total[:, j * LANES : (j + 1) * LANES]

    strict = row > col

    def backward(layer, source, before, meanwhile):
        group = before + 1
        normed[...] = dmid[...].astype(bf16)
        add_up(4, group)

        def hidden_back(j):
            at = cols_at(j, LANES)
            other = cols_at(j + FF // 2 // LANES, LANES)
            d_hidden = dot(normed[...], w_down[layer, :, at])
            first, second = upg[layer, :, at], upg[layer, :, other]
            gate = sigmoid(first)
            r_up[layer, mine, at] = (
                d_hidden * second * gate * (1.0 + first * (1.0 - gate))
            ).astype(bf16)
            r_up[layer, mine, other] = (d_hidden * (first * gate)).astype(bf16)

        loop(0, FF // 2 // LANES, hidden_back)
        right_copy(layer, W_UP).start()
        add_up(4, group)
        slot = swap_slot()

        def up_back(j):
            at = cols_at(j, 256)
            part = dot(r_up[layer, mine, :], w_up[layer, at, :], NT)
            big_a[:, at] = part
            swap_out[slot, :, at] = part.astype(bf16)

        loop(0, D // 256, up_back)
        swap_begin(slot, D)
        ready(group)
        add_all(group)
        add_up(8, group + 1)
        meanwhile()
        swap_end(slot, D)
        rms_back(mids.at[layer], layer, 1, dmid, dmid, slot)
        r_out[layer, mine, :] = dmid[:, own_half].astype(bf16)
        right_copy(layer, W_OUT).start()
        slot = swap_slot()

        def mixer_back(j):
            at = cols_at(j, 256)
            theirs = pl.ds(pl.multiple_of((1 - sec) * HALF + j * 256, 256), 256)
            swap_out[slot, :, at] = dot(r_out[layer, mine, :], w_out[layer, theirs, :], NT).astype(bf16)

        loop(0, HALF // 256, mixer_back)
        swap_begin(slot, HALF)

        def mixer_own(j):
            at = cols_at(j, 256)
            ours = pl.ds(pl.multiple_of(sec * HALF + j * 256, 256), 256)
            big_a[:, at] = dot(r_out[layer, mine, :], w_out[layer, ours, :], NT)

        loop(0, HALF // 256, mixer_own)
        add_up(6, group + 1)
        swap_end(slot, HALF)

        def gate_norm_back(i):
            at = part_at(0, i)
            out = delta_o[layer, :, at]
            scale = lax.rsqrt(jnp.mean(out * out, axis=1, keepdims=True) + epsilon)
            unit = out * scale
            gate = proj[layer, :, part_at(3, i)]
            passed = sigmoid(gate)
            d_mixed = big_a[:, at] + swap_in[slot, :, at].astype(f32)
            gain = smalls[layer, 2:3, :]
            d_gate = d_mixed * unit * gain * (passed * (1.0 + gate * (1.0 - passed)))
            r_in[layer, mine, part_at(3, i)] = d_gate.astype(bf16)
            d_scaled = d_mixed * (gate * passed)
            small_sum[layer, OUT_ROW : OUT_ROW + 1, :] += jnp.sum(d_scaled * unit, axis=0, keepdims=True)
            d_unit = d_scaled * gain
            delta_o[layer, :, at] = scale * (d_unit - unit * jnp.mean(d_unit * unit, axis=1, keepdims=True))

        loop(0, OWN_HEADS, gate_norm_back)
        add_up(4, group + 1)

        dcol[...] = jnp.zeros(dcol.shape, f32)
        drow[...] = jnp.zeros(drow.shape, f32)
        dbeta[...] = jnp.zeros(dbeta.shape, f32)

        def norm_silu_back(part, i, d_value):
            at = part_at(part, i)
            total = tot[layer, :, at]
            passed = sigmoid(total)
            if part < 2:
                raw = total * passed
                scale = lax.rsqrt(jnp.sum(raw * raw, axis=1, keepdims=True) + epsilon)
                unit = raw * scale
                if part == 0:
                    d_value = d_value * HEAD_DIM ** (-0.5)
                d_value = scale * (d_value - unit * jnp.sum(d_value * unit, axis=1, keepdims=True))
            tot[layer, :, at] = d_value * (passed * (1.0 + total * (1.0 - passed)))

        def delta_backward(i):
            h = sec * OWN_HEADS + i
            at = part_at(0, i)
            weights = spread(layer, i)
            query, key, value = [qkv[layer, :, part_at(part, i)] for part in range(3)]
            write = lane_of(beta[layer], HEADS + h)
            solved, d_out = pseudo[layer, :, at], delta_o[layer, :, at]
            key_key = mm(key, key, NT)
            query_key = mm(query, key, NT)
            d_score = mm(d_out, solved, NT)
            d_pseudo = mm(query_key * weights, d_out, TN)
            d_right = mm(t_inv[layer, :, at], d_pseudo, TN)
            d_left = jnp.where(strict, -mm(d_right, solved, NT), 0.0)
            left_key = d_left * weights
            d_write = jnp.sum(d_right * value, axis=1, keepdims=True) + jnp.sum(
                left_key * key_key, axis=1, keepdims=True
            )
            d_query_key = d_score * weights
            d_key_key = left_key * write
            norm_silu_back(0, i, mm(d_query_key, key, NN))
            norm_silu_back(
                1, i, mm(d_query_key, query, TN) + mm(d_key_key, key, NN) + mm(d_key_key, key, TN)
            )
            norm_silu_back(2, i, write * d_right)
            d_gap = d_query_key * query_key + d_key_key * key_key
            dcol[...] += jnp.where(col == h, jnp.sum(d_gap, axis=1, keepdims=True), 0.0)
            drow[...] += jnp.where(row == h, jnp.sum(d_gap, axis=0, keepdims=True), 0.0)
            dbeta[...] += jnp.where(col == HEADS + h, d_write, 0.0)

        for i in range(OWN_HEADS):
            delta_backward(i)
            add_up(4, group + 1)

        def conv_back(i):
            for part in range(3):
                at, tap = part_at(part, i), tap_cols(part, i)
                d_total, x = tot[layer, :, at], proj[layer, :, at]
                d_proj = d_total * taps[layer, CONV - 1 : CONV, tap]
                line = CONV_ROW + part * HEADS + sec * OWN_HEADS + i
                tiles = 3 * D // LANES
                small_sum[layer, pl.ds(line + (CONV - 1) * tiles, 1), :] = jnp.sum(
                    d_total * x, axis=0, keepdims=True
                )
                for m in range(1, CONV):
                    met = d_total * same[m - 1]
                    weight = taps[layer, CONV - 1 - m : CONV - m, tap]
                    d_proj += pltpu.roll(met * weight, BLOCK - m, 0)
                    small_sum[layer, pl.ds(line + (CONV - 1 - m) * tiles, 1), :] = jnp.sum(
                        met * pltpu.roll(x, m, 0), axis=0, keepdims=True
                    )
                r_in[layer, mine, at] = d_proj.astype(bf16)

        loop(0, OWN_HEADS, conv_back)
        right_copy(layer, W_IN).start()
        add_up(4, group + 1)

        d_running = dcol[...] - drow[...].T
        d_decay = mm(jnp.where(row <= col, 1.0, 0.0), d_running, NN)
        pre = gp[layer] + smalls[layer, 1:2, :]
        rate = -jnp.exp(smalls[layer, 0:1, :])
        is_decay = col < HEADS
        d_pre = jnp.where(is_decay, d_decay * rate * sigmoid(pre), 0.0)
        small_sum[layer, LOG_ROW : LOG_ROW + 1, :] = jnp.sum(
            jnp.where(is_decay, d_decay * rate * softplus(pre), 0.0), axis=0, keepdims=True
        )
        small_sum[layer, BIAS_ROW : BIAS_ROW + 1, :] = jnp.sum(d_pre, axis=0, keepdims=True)
        d_gate_pre = (d_pre + dbeta[...] * beta[layer] * (1.0 - beta[layer])).astype(bf16)
        gate_grad = dot(l_in[layer, :, mine], d_gate_pre).T
        for j in range(D // LANES):
            line = GATE_ROW + j * 2 * HEADS
            small_sum[layer, line : line + 2 * HEADS, :] = gate_grad[
                : 2 * HEADS, j * LANES : (j + 1) * LANES
            ]
        slot = swap_slot()

        def in_back(j):
            at = cols_at(j, 256)
            part = dot(r_in[layer, mine, :], w_in[layer, at, :], NT) + dot(
                d_gate_pre, gate_w[layer, :, at]
            )
            big_a[:, at] = part
            swap_out[slot, :, at] = part.astype(bf16)

        loop(0, D // 256, in_back)
        swap_begin(slot, D)
        ready(group + 1)
        add_all(group + 1)
        add_up(6, group + 2)
        swap_end(slot, D)
        rms_back(source, layer, 0, dmid, dmid, slot)

        @pl.when(sec == layer)
        def _():
            in_grad[...] = dmid[...]

        add_up(4, group + 2)
        return group + 1

    turn_over(dmid, 1, l_down)
    left_copy(1, W_DOWN).start()
    feed_all(0)
    for index in range(len(small_inputs)):
        param_copy(index).wait()
    forward(0, x_in)()
    feed(6)
    big_x[...] = xs[...]
    finish = forward(1, big_x)
    for layer in range(2):
        for matrix in range(4):
            gather_sent(layer, matrix)
    done = backward(1, big_x, -1, finish)
    turn_over(dmid, 0, l_down)
    left_copy(0, W_DOWN).start()
    done = backward(0, x_in, done, lambda: None)

    piece = small_land.shape[1]

    def piece_rows(device):
        return pl.ds(pl.multiple_of(device * piece, piece), piece)

    def small_copy(stage, device, source, target):
        return remote(
            source, target, small_sem.at[stage, 0], small_sem.at[stage, 1], {"dp": device}
        )

    def scatter_small(offset):
        device = lax.rem(me + offset, dp)
        small_copy(0, device, small_mate.at[piece_rows(device), :], small_land.at[me]).start()

    def spread_small(offset):
        device = lax.rem(me + offset, dp)
        small_copy(
            1, device, small_out.at[piece_rows(me), :], small_out.at[piece_rows(me), :]
        ).start()

    to_mate = remote(small_sum.at[1 - sec], small_mate, mate_sem.at[0], mate_sem.at[1], mate)
    to_mate.start()
    add_up(6, done + 1)
    to_mate.wait()
    small_mate[...] += small_sum[sec]
    loop(1, dp, scatter_small)
    add_up(12, done + 1)
    small_land[me] = small_mate[piece_rows(me), :]
    others = small_land.at[pl.ds(0, dp - 1)]
    small_copy(0, sibling, others, others).wait_recv()
    small_out[piece_rows(me), :] = jnp.sum(small_land[...], axis=0)
    loop(1, dp, spread_small)
    add_all(done + 1)

    for unit, (matrix, start, width, _, _, _) in enumerate(UNITS):
        part = pl.ds(start, width)

        @pl.when(sec == 0)
        def _(unit=unit, matrix=matrix, part=part):
            last = held[matrix].at[0, slot_rows(chips), part]
            remote(last, last, last_send.at[matrix], last_recv.at[unit], mate).wait_recv()
            grads[matrix][:, whole_cols(unit, 1)] = held[matrix][0, slot_rows(chips), part].astype(f32)

        @pl.when(sec != 0)
        def _(unit=unit, matrix=matrix, part=part):
            last = held[matrix].at[1, slot_rows(chips), part]
            remote(last, last, last_send.at[matrix], last_recv.at[unit], mate).wait_recv()
            grads[matrix][:, whole_cols(unit, 0)] = held[matrix][1, slot_rows(chips), part].astype(f32)

    small_copy(0, sibling, others, others).wait_send()
    spans = small_out.at[pl.ds(0, (dp - 1) * piece), :]
    small_copy(1, sibling, spans, spans).wait()
    for matrix in range(4):
        own = held[matrix].at[0, pl.ds(0, rows), :]
        remote(own, own, own_send.at[matrix], last_recv.at[0], mate).wait_send()
        remote(own, own, last_send.at[matrix], last_recv.at[0], mate).wait_send()
        for layer in range(2):
            ring_sent(layer, matrix)
            left_copy(layer, matrix).wait_send()
            right_copy(layer, matrix).wait_send()


def closing_kernel(*refs):
    bigs, small, outs, places, sem = refs[:6], refs[6], refs[7:13], refs[13:19], refs[19]
    copies = [
        pltpu.make_async_copy(big, out.at[0], sem.at[i]) for i, (big, out) in enumerate(zip(bigs, outs))
    ]
    for copy in copies:
        copy.start()
    gate, gains, taps, log, bias, out_gain = places
    turned = small[GATE_ROW : GATE_ROW + D // LANES * 2 * HEADS, :].T
    for j in range(D // LANES):
        at = slice(j * LANES, (j + 1) * LANES)
        gate[0, at, :] = turned[:, j * 2 * HEADS : (j + 1) * 2 * HEADS]
        for k in range(2):
            line = GAIN_ROW + k * (D // LANES) + j
            gains[0, k : k + 1, at] = small[line : line + 1, :]
    for j in range(3 * D // LANES):
        at = slice(j * LANES, (j + 1) * LANES)
        for k in range(CONV):
            line = CONV_ROW + k * (3 * D // LANES) + j
            taps[0, k : k + 1, at] = small[line : line + 1, :]
    log[...] = small[LOG_ROW : LOG_ROW + 1, :HEADS]
    bias[...] = small[BIAS_ROW : BIAS_ROW + 1, :HEADS]
    out_gain[...] = small[OUT_ROW : OUT_ROW + 1, :]
    for copy in copies:
        copy.wait()


def padded(row):
    return jnp.pad(row, ((0, 0), (0, LANES - row.shape[1])))


def local(
    dp,
    block_input,
    cotangent,
    marks,
    w_in,
    w_out,
    w_up,
    w_down,
    gate_weights,
    norm_gains,
    conv_weights,
    decay_log,
    decay_bias,
    out_gain,
):
    rows = w_in.shape[1]
    chips = dp // 2
    smalls = jnp.concatenate(
        [padded(decay_log), padded(decay_bias), out_gain, jnp.zeros((5, LANES), f32)], axis=0
    )
    gate_w = gate_weights[0].T
    piece = 8 * -(-SMALL_ROWS // (8 * dp))
    vmem = pl.BlockSpec(memory_space=pltpu.VMEM)
    anywhere = pl.BlockSpec(memory_space=pl.ANY)

    def both(width, kind=f32, lines=BLOCK):
        return pltpu.VMEM((2, lines, width), kind)

    def wide(width, kind=f32, lines=BLOCK):
        return pltpu.VMEM((lines, width), kind)

    dma = pltpu.SemaphoreType.DMA
    scratch = (
        [both(width, bf16, D) for width in HALVES]
        + [both(2 * BLOCK, bf16, D) for _ in HALVES]
        + [both(width, bf16, 2 * BLOCK) for width in HALVES]
        + [both(2 * D), both(3 * HALF), both(3 * HALF), both(FF), both(HALF), both(HALF), both(HALF)]
        + [both(D), wide(D), wide(D), wide(D), wide(D), wide(D, bf16)]
        + [both(LANES)] * 4
        + [wide(LANES), pltpu.VMEM((CONV - 1, BLOCK, LANES), f32)]
        + [wide(LANES)] * 3
        + [both(D, bf16, LANES), both(D, f32, 2), both(3 * D, f32, CONV), both(LANES, f32, 8)]
        + [pltpu.VMEM((3, BLOCK, D), bf16)] * 2
        + [both(LANES, f32, dp * piece), wide(LANES, f32, dp * piece)]
        + [pltpu.VMEM((dp, piece, LANES), f32)]
        + [dma((2, len(UNITS))), dma((4,)), dma((2, len(UNITS), chips - 1))]
        + [dma((2, 4))] * 3
        + [dma((2, 8))] * 2
        + [dma((3,))] * 2
        + [pltpu.SemaphoreType.REGULAR((4,)), dma((2, 2)), dma((4,)), dma((4,))]
        + [dma((len(UNITS),)), dma((4,)), dma((2,))]
    )
    *bigs, small = pl.pallas_call(
        functools.partial(kernel, dp, rows),
        out_shape=[jax.ShapeDtypeStruct((BLOCK, D), f32)] * 2
        + [jax.ShapeDtypeStruct((rows, width), f32) for width in WIDTHS]
        + [jax.ShapeDtypeStruct((dp * piece, LANES), f32)],
        in_specs=[vmem] * 3 + [anywhere] * 4 + [vmem] * 4,
        out_specs=[vmem] * 7,
        scratch_shapes=scratch,
        compiler_params=pltpu.CompilerParams(
            collective_id=0, has_side_effects=True, vmem_limit_bytes=63 * 2**20
        ),
        cost_estimate=pl.CostEstimate(
            flops=6 * BLOCK * D * sum(WIDTHS), bytes_accessed=8 * rows * sum(WIDTHS), transcendentals=0
        ),
    )(
        block_input, cotangent, marks[None, :], w_in[0], w_out[0], w_up[0], w_down[0],
        gate_w, norm_gains[0], conv_weights[0], smalls,
    )
    shapes = [(1, *big.shape) for big in bigs]
    shapes += [(1, D, 2 * HEADS), (1, 2, D), (1, CONV, 3 * D), (1, HEADS), (1, HEADS), (1, LANES)]
    return tuple(
        pl.pallas_call(
            closing_kernel,
            out_shape=[jax.ShapeDtypeStruct(shape, f32) for shape in shapes],
            in_specs=[anywhere] * 6 + [vmem],
            out_specs=[vmem] * 12,
            scratch_shapes=[dma((6,))],
            compiler_params=pltpu.CompilerParams(vmem_limit_bytes=60 * 2**20),
        )(*bigs, small)
    )


def solution(mesh):
    sharded, whole, flat = P("section", "dp", None), P("section", None, None), P("section", None)
    return jax.shard_map(
        functools.partial(local, mesh.shape["dp"]),
        mesh=mesh,
        in_specs=(P("dp", None), P("dp", None), P("dp")) + (sharded,) * 4 + (whole,) * 3 + (flat,) * 3,
        out_specs=(sharded,) * 6 + (whole,) * 3 + (flat,) * 3,
        check_vma=False,
    )
```
